32 devices in a mesh: lamella: 2 (over x), lat: 16 (over z, y, core).
Axes of the slice: x: 2, y: 2, z: 4, core: 2. Of those that a mesh axis runs over, the one named last changes fastest.
Arguments:
- potential: bfloat16 [6, 2048, 4096], P(None, ('lamella', 'lat')), parts along dimension 1, may hold values from -6 to 6
- tilt_index: int32 [4], P('lamella'), parts along dimension 0, may hold values from 0 to 40
- slice_order: int32 [6], P('lamella'), parts along dimension 0, may hold values from 0 to 5
- tilt_table: float32 [41, 2], replicated, may hold values from -8 to 8
- fresnel_taps: float32 [2, 63], replicated, may hold values from -0.5 to 0.5
- ctf_taps: float32 [2, 127], replicated, may hold values from -0.375 to 0.375
- mtf_taps: float32 [15], replicated, may hold values from 0.02 to 0.12
- owner: int32 [32], P('lamella'), parts along dimension 0, may hold values from 0 to 15, each once
Outputs:
- exit_wave: float32 [2, 2, 2048, 4096], P(None, None, ('lamella', 'lat')), parts along dimension 2
- detector: float32 [32, 256, 1024], P(('lamella', 'lat')), parts along dimension 0
The draws below stay inside these ranges and needn't reach their ends.
There are 2 independent parts, one for each index of `lamella`. The reference program is written for one: setup_inputs(seed, part) draws one part's arguments, and reference() takes and returns one part's arrays. A program takes and returns all parts, laid end to end along the dimension named above; an argument that names none is the same for every part. Nothing has to cross between parts.
Inputs may be any that keep to these rules, and one draw needn't show every extreme that they name: owner names every tile position once.
All inputs are finite; a program needn't handle non-finite values.
Results may differ from the reference program's by a relative error of at most 0.012.
Values may be sent and summed in bfloat16 or wider, within the bound.
No kernel may reach another device: no remote copies, remote signals or barrier semaphores. Data moves between devices by JAX's collectives and lax.ppermute only.
A program may use at most 64 MiB of HBM per device.

```python
import math
import jax
import jax.numpy as jnp
from jax import lax

NY = 4096
WAVES = 2
STEPS = 3
NSLICE = 6
NTILT = 41
FRESNEL_TAPS = 63
CTF_TAPS = 127
MTF_TAPS = 15
NX = 1024
TILES = 16
TILE_W = 256
N_LAT = 16


def shard_levels(rng, extent, cuts, smallest, top_value):
    def one(axis_at, parts):
        steps = jax.random.uniform(jax.random.fold_in(jax.random.fold_in(rng, 6), axis_at), (parts,), jnp.float32, smallest / len(cuts), top_value / len(cuts))
        return jnp.repeat(jnp.exp(steps), extent[axis_at] // parts).reshape((-1,) + (1,) * (len(extent) - axis_at - 1))

    gain = one(*cuts[0])
    for cut in cuts[1:]:
        gain = gain * one(*cut)
    return gain


def bell_draw(stream_key, extent, scale, bound, cuts=(), kind=jnp.bfloat16):
    result = jax.random.normal(stream_key, extent, jnp.float32) * scale
    if len(cuts) > 0:
        result = shard_levels(stream_key, extent, cuts, -0.22, 0.18) * result
    return jnp.clip(result, min=-bound, max=bound).astype(kind)


def setup_inputs(seed: int = 0, part: int = 0) -> dict:
    streams_of = jax.random.split(jax.random.key(seed), 9)
    part_splits = jax.random.split(jax.random.fold_in(streams_of[8], part), 9)
    return {
        "potential": bell_draw(part_splits[0], (NSLICE, NX, NY), 1.0, 6.0, ((1, 16),)),
        "tilt_index": jax.random.randint(part_splits[1], (WAVES,), 0, NTILT).astype(jnp.int32),
        "slice_order": jax.random.randint(part_splits[2], (STEPS,), 0, NSLICE).astype(jnp.int32),
        "tilt_table": jnp.clip(jax.random.uniform(streams_of[3], (NTILT, 2), jnp.float32, -8.0, 8.0), -8.0, 8.0),
        "fresnel_taps": bell_draw(streams_of[4], (2, FRESNEL_TAPS), (2 * FRESNEL_TAPS) ** -0.5, 0.5, (), jnp.float32),
        "ctf_taps": bell_draw(streams_of[5], (2, CTF_TAPS), (2 * CTF_TAPS) ** -0.5, 0.375, (), jnp.float32),
        "mtf_taps": jnp.clip(jax.random.uniform(streams_of[6], (MTF_TAPS,), jnp.float32, 0.02, 0.12), 0.02, 0.12),
        "owner": jax.random.permutation(part_splits[7], N_LAT).astype(jnp.int32),
    }


highest = lax.Precision.HIGHEST


def conv_complex(field_in, tap_pair, along_cols):
    reach = (tap_pair.shape[1] - 1) // 2
    short_taps = tap_pair.astype(jnp.bfloat16)
    real_taps = short_taps[0]
    imag_taps = short_taps[1]
    kernel = jnp.stack([jnp.stack([real_taps, -imag_taps]), jnp.stack([imag_taps, real_taps])])
    if along_cols:
        kernel = kernel[:, :, None, :]
        padding = ((0, 0), (reach, reach))
    else:
        kernel = kernel[:, :, :, None]
        padding = ((reach, reach), (0, 0))
    return lax.conv_general_dilated(field_in, kernel, (1, 1), padding, dimension_numbers=("NCHW", "OIHW", "NCHW"), preferred_element_type=jnp.float32)


def conv_real(field_in, tap_list, along_cols):
    reach = (tap_list.shape[0] - 1) // 2
    if along_cols:
        kernel = tap_list[None, None, None, :]
        padding = ((0, 0), (reach, reach))
    else:
        kernel = tap_list[None, None, :, None]
        padding = ((reach, reach), (0, 0))
    return lax.conv_general_dilated(field_in, kernel, (1, 1), padding, dimension_numbers=("NCHW", "OIHW", "NCHW"), precision=highest)


def reference(potential, tilt_index, slice_order, tilt_table, fresnel_taps, ctf_taps, mtf_taps, owner):
    row_pos = jnp.arange(NX, dtype=jnp.float32) / NX
    col_pos = jnp.arange(NY, dtype=jnp.float32) / NY
    tilts = tilt_table[tilt_index]
    theta = 2.0 * math.pi * (tilts[:, 0, None, None] * row_pos[None, :, None] + tilts[:, 1, None, None] * col_pos[None, None, :])
    wave_field = jnp.stack([jnp.cos(theta), jnp.sin(theta)], axis=1)
    for step_index in range(STEPS):
        phase_field = lax.dynamic_index_in_dim(potential, slice_order[step_index], 0, keepdims=False).astype(jnp.float32)
        cosine = jnp.cos(phase_field)
        sine_part = jnp.sin(phase_field)
        real_part = wave_field[:, 0] * cosine - wave_field[:, 1] * sine_part
        imag_part = wave_field[:, 0] * sine_part + wave_field[:, 1] * cosine
        transmitted = jnp.stack([real_part, imag_part], axis=1).astype(jnp.bfloat16)
        spread = conv_complex(transmitted, fresnel_taps, True).astype(jnp.bfloat16)
        wave_field = conv_complex(spread, fresnel_taps, False)
    exit_wave = wave_field
    focused = conv_complex(exit_wave.astype(jnp.bfloat16), ctf_taps, True).astype(jnp.bfloat16)
    image_wave = conv_complex(focused, ctf_taps, False)
    intensity = jnp.sum(image_wave * image_wave, axis=(0, 1)) / WAVES
    tile_stack = intensity.reshape(NX, TILES, TILE_W).transpose(1, 0, 2)[:, None]
    tile_stack = conv_real(conv_real(tile_stack, mtf_taps, False), mtf_taps, True)[:, 0]
    detector = jnp.zeros((TILES, TILE_W, NX), jnp.float32).at[owner].set(tile_stack.transpose(0, 2, 1))
    return exit_wave, detector
```

```python
import functools
import math

import jax
import jax.numpy as jnp
from jax import lax
from jax.experimental import pallas as pl
from jax.experimental.pallas import tpu as pltpu
from jax.sharding import PartitionSpec as P

highest = lax.Precision.HIGHEST
SIN_TURN = (
    6.2831854820251465,
    -41.34170150756836,
    81.60513305664062,
    -76.70301818847656,
    42.02592849731445,
    -14.899847030639648,
    3.2381374835968018,
)
COS_TURN = (
    1.0,
    -19.73920440673828,
    64.93911743164062,
    -85.45014190673828,
    60.16762924194336,
    -25.967599868774414,
    6.528658390045166,
)
HALO = 32
STEP = 256


def spread_taps(tap_list, tap_index):
    count = tap_list.shape[-1]
    which = jnp.arange(count, dtype=jnp.int32)
    onehot = (tap_index[..., None] == which).astype(jnp.float32)
    return jnp.einsum("...k,iok->...io", tap_list, onehot, precision=highest)


def short(tap_pair):
    return tap_pair.astype(jnp.bfloat16).astype(jnp.float32)


def column_band(tap_pair):
    reach = (tap_pair.shape[1] - 1) // 2
    inputs = jnp.arange(256, dtype=jnp.int32)[:, None]
    outputs = jnp.arange(128, dtype=jnp.int32)[None, :]
    real, imag = spread_taps(short(tap_pair), inputs - outputs - 64 + reach)
    joined = jnp.stack(
        [jnp.stack([real, imag], axis=1), jnp.stack([-imag, real], axis=1)], axis=0
    )
    joined = joined.reshape(2, 2, 128, 2, 128).transpose(1, 0, 2, 3, 4)
    return joined.reshape(512, 256).astype(jnp.bfloat16)


def row_band(tap_pair, rows_out, rows_in, offset):
    outputs = jnp.arange(rows_out, dtype=jnp.int32)[:, None]
    inputs = jnp.arange(rows_in, dtype=jnp.int32)[None, :]
    return spread_taps(short(tap_pair), inputs - outputs - offset)


def horner(coefs, z):
    total = coefs[-1] * z + coefs[-2]
    for coef in coefs[-3::-1]:
        total = total * z + coef
    return total


def cos_sin(phase):
    turns = phase * (1.0 / (2.0 * math.pi))
    rest = turns - jnp.round(turns)
    z = rest * rest
    return horner(COS_TURN, z), horner(SIN_TURN, z) * rest


def dot(a, b):
    return jnp.dot(a, b, preferred_element_type=jnp.float32)


def split_parts(product, rows):
    out = []
    for k in range(product.shape[1] // 256):
        top = product[:rows, 256 * k : 256 * (k + 1)]
        low = product[rows:, 256 * k : 256 * (k + 1)]
        out.append((top[:, :128] - low[:, 128:], top[:, 128:] + low[:, :128]))
    return out


def lanes_inside(block, shift, col_count):
    cols = block * 128 - shift + lax.broadcasted_iota(jnp.int32, (1, 128), 1)
    return ((cols >= 0) & (cols < col_count)).astype(jnp.float32)


def first_kernel(waves, order, *refs):
    pieces, (ex, ey, band, out, ring) = refs[:5], refs[5:]

    @pl.when(pl.program_id(0) == 0)
    def _():
        ring[:, :, :256] = jnp.zeros((waves, ring.shape[1], 256), jnp.bfloat16)

    for blk in range(2):
        lanes = pl.ds(128 * blk, 128)
        row = 0
        for piece in pieces:
            rows = piece.shape[-2]
            for start in range(0, rows, 32):
                if len(piece.shape) == 3:
                    phase = piece[0, pl.ds(start, 32), lanes]
                else:
                    phase = piece[pl.ds(start, 32), lanes]
                cosine, sine = cos_sin(phase.astype(jnp.float32))
                for w in range(waves):
                    yr, yi = ey[2 * w : 2 * w + 1, lanes], ey[2 * w + 1 : 2 * w + 2, lanes]
                    ur, ui = cosine * yr - sine * yi, cosine * yi + sine * yr
                    xr = ex[pl.ds(row, 32), 2 * w : 2 * w + 1]
                    xi = ex[pl.ds(row, 32), 2 * w + 1 : 2 * w + 2]
                    to = 256 * (blk + 1)
                    ring[w, pl.ds(row, 32), to : to + 128] = (ur * xr - ui * xi).astype(jnp.bfloat16)
                    ring[w, pl.ds(row, 32), to + 128 : to + 256] = (ur * xi + ui * xr).astype(
                        jnp.bfloat16
                    )
                row += 32
    for w in range(waves):
        for blk in range(2):
            lanes = pl.ds(256 * blk, 256)
            out[w, :, lanes] = dot(ring[w, :, 256 * blk : 256 * blk + 512], band[...]).astype(
                jnp.bfloat16
            )
        ring[w, :, :256] = ring[w, :, 512:768]


def gather_rows(pieces, lanes):
    found = []
    for piece in pieces:
        if len(piece.shape) == 3:
            found.append(piece[0, :, lanes])
        else:
            found.append(piece[:, lanes])
    return jnp.concatenate(found, axis=0).astype(jnp.float32)


def transmit(ring, product, phases, masks, waves, rows):
    factors = []
    for phase, mask in zip(phases, masks):
        cosine, sine = cos_sin(phase)
        factors.append((cosine * mask, sine * mask))
    for w in range(waves):
        for blk, (real, imag) in enumerate(split_parts(product[w], rows)):
            cosine, sine = factors[blk]
            to = 256 * (blk + 1)
            ring[w, :, to : to + 128] = (real * cosine - imag * sine).astype(jnp.bfloat16)
            ring[w, :, to + 128 : to + 256] = (real * sine + imag * cosine).astype(jnp.bfloat16)


def second_kernel(waves, col_count, order, *refs):
    pieces, (spread, rows_band, band, out, ring, last) = refs[:3], refs[3:]
    g = pl.program_id(0)

    @pl.when(g == 0)
    def _():
        ring[:, :, :256] = jnp.zeros((waves, ring.shape[1], 256), jnp.bfloat16)
        last[...] = jnp.zeros_like(last)

    rows = ring.shape[1]
    low = lax.broadcasted_iota(jnp.int32, (rows, 128), 1) < 64
    turned = [last[...]]
    for blk in range(2):
        turned.append(pltpu.roll(gather_rows(pieces, pl.ds(128 * blk, 128)), 64, 1))
    last[...] = turned[2]
    phases = [jnp.where(low, turned[0], turned[1]), jnp.where(low, turned[1], turned[2])]
    masks = [lanes_inside(2 * g, 64, col_count), lanes_inside(2 * g + 1, 64, col_count)]
    product = [dot(rows_band[...], spread[w]) for w in range(waves)]
    transmit(ring, product, phases, masks, waves, rows)
    for w in range(waves):
        for blk in range(2):
            out[w, :, 256 * blk : 256 * (blk + 1)] = dot(
                ring[w, :, 256 * blk : 256 * blk + 512], band[...]
            ).astype(jnp.bfloat16)
        ring[w, :, :256] = ring[w, :, 512:768]


def third_kernel(waves, col_count, order, owner, *refs):
    pieces = refs[:3]
    spread, rows_band, band, last_band, wide_band, exit_wave, focused, ring, last, waved, turned = refs[3:]
    g = pl.program_id(0)

    @pl.when(g == 0)
    def _():
        ring[:, :, :256] = jnp.zeros((waves, ring.shape[1], 256), jnp.bfloat16)
        waved[:, :, :256] = jnp.zeros((waves, waved.shape[1], 256), jnp.bfloat16)
        turned[...] = jnp.zeros_like(turned)
        last[...] = jnp.zeros_like(last)

    rows, kept = ring.shape[1], waved.shape[1]
    phases = [last[...], gather_rows(pieces, pl.ds(0, 128))]
    last[...] = gather_rows(pieces, pl.ds(128, 128))
    masks = [lanes_inside(2 * g - 1, 0, col_count), lanes_inside(2 * g, 0, col_count)]
    product = [dot(rows_band[...], spread[w]) for w in range(waves)]
    transmit(ring, product, phases, masks, waves, rows)
    low = lax.broadcasted_iota(jnp.int32, (kept, 128), 1) < 64
    masks = [lanes_inside(2 * g - 1, 64, col_count), lanes_inside(2 * g, 64, col_count)]
    for w in range(waves):
        for blk in range(2):
            made = dot(ring[w, :, 256 * blk : 256 * blk + 512], band[...]).astype(jnp.bfloat16)
            ((real, imag),) = split_parts(dot(last_band[...], made), kept)
            to = 256 * (blk + 1)
            for part, value in enumerate((real, imag)):
                waved[w, :, to + 128 * part : to + 128 * part + 128] = (value * masks[blk]).astype(
                    jnp.bfloat16
                )
                rolled = pltpu.roll(value, 64, 1)
                exit_wave[w, part, :, 128 * blk : 128 * blk + 128] = jnp.where(
                    low, turned[w, part], rolled
                )
                turned[w, part] = rolled
            made = dot(waved[w, :, 256 * blk : 256 * blk + 512], wide_band[...]).astype(jnp.bfloat16)
            for part in range(2):
                block = made[:, 128 * part : 128 * part + 128]
                if len(focused.shape) == 5:
                    focused[0, w, part, :, 128 * blk : 128 * blk + 128] = block
                else:
                    focused[w, part, :, 128 * blk : 128 * blk + 128] = block
        ring[w, :, :256] = ring[w, :, 512:768]
        waved[w, :, :256] = waved[w, :, 512:768]


def detector_kernel(waves, tile_wave, taps_band, row_taps, col_taps, out, padded):
    sources, rows, width = tile_wave.shape[0], tile_wave.shape[3], tile_wave.shape[4]
    total = sources * rows
    edge = jnp.zeros((64, width), jnp.float32)
    padded[:64] = edge
    padded[64 + total :] = edge
    for b in range(total // 128):
        image = None
        for w in range(waves):
            parts = []
            for part in range(2):
                window = []
                for k in range(2 * b - 1, 2 * b + 3):
                    if 0 <= k < total // 64:
                        window.append(tile_wave[k, w, part])
                    else:
                        window.append(jnp.zeros((64, width), jnp.bfloat16))
                parts.append(jnp.concatenate(window, axis=0))
            real, imag = dot(taps_band[...], parts[0]), dot(taps_band[...], parts[1])
            re = real[:128] - imag[128:]
            im = imag[:128] + real[128:]
            term = re * re + im * im
            image = term if image is None else image + term
        padded[64 + 128 * b : 192 + 128 * b] = image / waves
    for b in range(total // 128):
        rows_done = jnp.dot(
            row_taps[...],
            padded[128 * b : 128 * b + 256],
            precision=highest,
            preferred_element_type=jnp.float32,
        )
        out[:, 128 * b : 128 * b + 128] = lax.dot_general(
            col_taps[...],
            rows_done,
            (((1,), (1,)), ((), ())),
            precision=highest,
            preferred_element_type=jnp.float32,
        )


def block_windows(values):
    length = values.shape[-1]
    padded = jnp.pad(values, [(0, 0)] * (values.ndim - 1) + [(64, 64)])
    blocks = padded.reshape(values.shape[:-1] + (length // 128 + 1, 128))
    return jnp.concatenate([blocks[..., :-1, :], blocks[..., 1:, :]], axis=-1)


def narrow_tiles(focused, owner, wide_rows, row_taps, col_taps, lane_count):
    waves, _, rows, col_count = focused.shape
    width = col_count // lane_count
    slots = jnp.arange(lane_count, dtype=jnp.int32)
    placing = (owner[None, :] == slots[:, None]).astype(jnp.bfloat16)
    focused = focused.reshape(waves, 2, rows, lane_count, width)
    focused = jnp.einsum("jl,acrlk->jackr", placing, focused, preferred_element_type=jnp.float32)
    sent = focused.astype(jnp.bfloat16)
    tile_wave = lax.all_to_all(sent, "lat", split_axis=0, concat_axis=4, tiled=True)[0]
    windows = block_windows(tile_wave)
    taps_band = wide_rows.reshape(2, 128, 256)
    made = jnp.einsum("acwbi,doi->acdwbo", windows, taps_band, preferred_element_type=jnp.float32)
    real = made[:, 0, 0] - made[:, 1, 1]
    imag = made[:, 1, 0] + made[:, 0, 1]
    image = jnp.sum(real * real + imag * imag, axis=0) / waves
    image = image.reshape(width, lane_count * rows)
    blurred = jnp.einsum("wbi,oi->wbo", block_windows(image), row_taps, precision=highest)
    return jnp.dot(col_taps, blurred.reshape(width, lane_count * rows), precision=highest)


def local(potential, tilt_index, slice_order, tilt_table, fresnel_taps, ctf_taps, mtf_taps, owner):
    row_count, col_count = potential.shape[1:]
    lane_count = lax.axis_size("lat")
    total_rows = row_count * lane_count
    tile_cols = col_count // lane_count
    waves = tilt_index.shape[0]
    first_row = lax.axis_index("lat") * row_count
    steps = col_count // STEP

    def neighbour(value, offset):
        pairs = [(i, i + offset) for i in range(lane_count) if 0 <= i + offset < lane_count]
        return lax.ppermute(value, "lat", pairs)

    def chosen(step, start, rows):
        return lax.dynamic_slice(
            potential, (slice_order[step], start, 0), (1, rows, col_count)
        )[0]

    whole = chosen(0, 0, row_count)
    up1, down1 = neighbour(whole, 1), neighbour(whole, -1)
    up2 = neighbour(chosen(0, row_count - HALO, HALO), 2)
    down2 = neighbour(chosen(0, 0, HALO), -2)
    whole = chosen(1, 0, row_count)
    second_up, second_down = neighbour(whole, 1), neighbour(whole, -1)
    third_up = neighbour(chosen(2, row_count - HALO, HALO), 1)
    third_down = neighbour(chosen(2, 0, HALO), -1)

    rows1, rows2, rows3 = (row_count + 2 * HALO * k for k in (3, 2, 1))

    def inside(halo_rows, count):
        at = first_row - halo_rows + jnp.arange(count, dtype=jnp.int32)
        return ((at >= 0) & (at < total_rows)).astype(jnp.float32), at

    tilts = jnp.take(tilt_table, tilt_index, axis=0)
    keep, at = inside(3 * HALO, rows1)
    angle = 2.0 * math.pi * tilts[:, 0, None] * (at.astype(jnp.float32) / total_rows)
    ex = jnp.stack([jnp.cos(angle), jnp.sin(angle)], axis=1).reshape(2 * waves, rows1) * keep
    ex = jnp.pad(ex.T, ((0, 0), (0, 128 - 2 * waves)))
    across = jnp.arange(col_count, dtype=jnp.float32) / col_count
    angle = 2.0 * math.pi * tilts[:, 1, None] * across
    ey = jnp.stack([jnp.cos(angle), jnp.sin(angle)], axis=1).reshape(2 * waves, col_count)
    ey = jnp.pad(ey, ((0, 8 - 2 * waves), (0, STEP)))

    band = column_band(fresnel_taps)
    wide_band = column_band(ctf_taps)
    full_rows = row_band(fresnel_taps, rows2, rows1, 1)

    def stacked(count, count_in, halo_rows):
        keep = inside(halo_rows, count)[0]
        cut = full_rows[:, :count, :count_in] * keep[None, :, None]
        return cut.reshape(2 * count, count_in).astype(jnp.bfloat16)

    band2 = stacked(rows2, rows1, 2 * HALO)
    band3 = stacked(rows3, rows2, HALO)
    band4 = stacked(row_count, rows3, 0)
    wide_rows = row_band(ctf_taps, 128, 256, 1).reshape(256, 256).astype(jnp.bfloat16)
    mtf_reach = (mtf_taps.shape[0] - 1) // 2
    at = jnp.arange(256, dtype=jnp.int32)
    row_taps = spread_taps(mtf_taps, at[None, :] - at[:128, None] - 64 + mtf_reach)
    at = jnp.arange(tile_cols, dtype=jnp.int32)
    col_taps = spread_taps(mtf_taps, at[None, :] - at[:, None] + mtf_reach)

    def clamp(g):
        return jnp.minimum(g, steps - 1)

    def piece(rows):
        return pl.BlockSpec((rows, STEP), lambda g, *_: (0, clamp(g)))

    def mine(step, start, rows):
        return pl.BlockSpec(
            (1, rows, STEP), lambda g, order, *_: (order[step], start // rows, clamp(g))
        )

    def fixed(*shape):
        return pl.BlockSpec(shape, lambda g, *_: (0,) * len(shape))

    def blocks(rows):
        return pl.BlockSpec((waves, rows, 512), lambda g, *_: (0, 0, g))

    params = pltpu.CompilerParams(
        dimension_semantics=("arbitrary",), vmem_limit_bytes=48 * 1024 * 1024
    )

    def cost(flops, count):
        return pl.CostEstimate(flops=flops, bytes_accessed=count, transcendentals=0)

    spread_cols = (steps + 1) * 512
    spread = pl.pallas_call(
        functools.partial(first_kernel, waves),
        name="first_step",
        out_shape=jax.ShapeDtypeStruct((waves, rows1, spread_cols), jnp.bfloat16),
        grid_spec=pltpu.PrefetchScalarGridSpec(
            num_scalar_prefetch=1,
            grid=(steps + 1,),
            in_specs=[
                piece(HALO),
                piece(row_count),
                mine(0, 0, row_count),
                piece(row_count),
                piece(HALO),
                fixed(rows1, 128),
                pl.BlockSpec((8, STEP), lambda g, *_: (0, g)),
                fixed(512, 256),
            ],
            out_specs=blocks(rows1),
            scratch_shapes=[pltpu.VMEM((waves, rows1, 768), jnp.bfloat16)],
        ),
        compiler_params=params,
        cost_estimate=cost(waves * rows1 * spread_cols * 1024, 12 << 20),
    )(slice_order, up2, up1, potential, down1, down2, ex, ey, band)

    spread = pl.pallas_call(
        functools.partial(second_kernel, waves, col_count),
        name="second_step",
        out_shape=jax.ShapeDtypeStruct((waves, rows2, spread_cols), jnp.bfloat16),
        grid_spec=pltpu.PrefetchScalarGridSpec(
            num_scalar_prefetch=1,
            grid=(steps + 1,),
            in_specs=[
                piece(row_count),
                mine(1, 0, row_count),
                piece(row_count),
                blocks(rows1),
                fixed(2 * rows2, rows1),
                fixed(512, 256),
            ],
            out_specs=blocks(rows2),
            scratch_shapes=[
                pltpu.VMEM((waves, rows2, 768), jnp.bfloat16),
                pltpu.VMEM((rows2, 128), jnp.float32),
            ],
        ),
        compiler_params=params,
        cost_estimate=cost(waves * rows2 * spread_cols * 2048, 16 << 20),
    )(slice_order, second_up, potential, second_down, spread, band2, band)

    def done(g):
        return jnp.maximum(g - 1, 0)

    placed = tile_cols == STEP
    if placed:
        focused_shape = (lane_count, waves, 2, row_count, tile_cols)
        focused_spec = pl.BlockSpec(
            (1, waves, 2, row_count, tile_cols),
            lambda g, order, owner: (owner[done(g)], 0, 0, 0, 0),
        )
    else:
        focused_shape = (waves, 2, row_count, col_count)
        focused_spec = pl.BlockSpec(
            (waves, 2, row_count, STEP), lambda g, *_: (0, 0, 0, done(g))
        )
    exit_wave, focused = pl.pallas_call(
        functools.partial(third_kernel, waves, col_count),
        name="third_step",
        out_shape=(
            jax.ShapeDtypeStruct((waves, 2, row_count, col_count), jnp.float32),
            jax.ShapeDtypeStruct(focused_shape, jnp.bfloat16),
        ),
        grid_spec=pltpu.PrefetchScalarGridSpec(
            num_scalar_prefetch=2,
            grid=(steps + 1,),
            in_specs=[
                piece(HALO),
                mine(2, 0, row_count),
                piece(HALO),
                blocks(rows2),
                fixed(2 * rows3, rows2),
                fixed(512, 256),
                fixed(2 * row_count, rows3),
                fixed(512, 256),
            ],
            out_specs=(
                pl.BlockSpec((waves, 2, row_count, STEP), lambda g, *_: (0, 0, 0, done(g))),
                focused_spec,
            ),
            scratch_shapes=[
                pltpu.VMEM((waves, rows3, 768), jnp.bfloat16),
                pltpu.VMEM((rows3, 128), jnp.float32),
                pltpu.VMEM((waves, row_count, 768), jnp.bfloat16),
                pltpu.VMEM((waves, 2, row_count, 128), jnp.float32),
            ],
        ),
        compiler_params=params,
        cost_estimate=cost(waves * rows3 * spread_cols * 3072, 16 << 20),
    )(slice_order, owner, third_up, potential, third_down, spread, band3, band, band4, wide_band)

    if not placed:
        detector = narrow_tiles(focused, owner, wide_rows, row_taps, col_taps, lane_count)
        return exit_wave, detector[None]

    tile_wave = lax.all_to_all(focused, "lat", split_axis=0, concat_axis=0, tiled=True)
    detector = pl.pallas_call(
        functools.partial(detector_kernel, waves),
        name="detector",
        out_shape=jax.ShapeDtypeStruct((tile_cols, total_rows), jnp.float32),
        in_specs=[pl.BlockSpec(memory_space=pltpu.VMEM)] * 4,
        out_specs=pl.BlockSpec(memory_space=pltpu.VMEM),
        scratch_shapes=[pltpu.VMEM((total_rows + 128, tile_cols), jnp.float32)],
        compiler_params=pltpu.CompilerParams(vmem_limit_bytes=48 * 1024 * 1024),
        cost_estimate=cost(1 << 33, 4 << 20),
    )(tile_wave, wide_rows, row_taps, col_taps)
    return exit_wave, detector[None]


def solution(mesh):
    placed = (
        P(None, ("lamella", "lat"), None),
        P("lamella"),
        P("lamella"),
        P(),
        P(),
        P(),
        P(),
        P("lamella"),
    )
    return jax.shard_map(
        local,
        mesh=mesh,
        in_specs=placed,
        out_specs=(P(None, None, ("lamella", "lat"), None), P(("lamella", "lat"), None, None)),
        check_vma=False,
    )
```

```python
import functools
import math

import jax
import jax.numpy as jnp
from jax import lax
from jax.experimental import pallas as pl
from jax.experimental.pallas import tpu as pltpu
from jax.sharding import PartitionSpec as P

highest = lax.Precision.HIGHEST
SIN_TURN = (
    6.2831854820251465,
    -41.34170150756836,
    81.60513305664062,
    -76.70301818847656,
    42.02592849731445,
    -14.899847030639648,
    3.2381374835968018,
)
COS_TURN = (
    1.0,
    -19.73920440673828,
    64.93911743164062,
    -85.45014190673828,
    60.16762924194336,
    -25.967599868774414,
    6.528658390045166,
)
SIN_QUARTER = (
    0.4204482138156891,
    -0.004379667341709137,
    1.3686111742572393e-05,
    -2.0339173900651986e-08,
    1.679661791598175e-11,
)
COS_QUARTER = (
    1.6817927360534668,
    -0.052555955946445465,
    0.00027371387113817036,
    -5.690624220733298e-07,
    5.977824346636851e-10,
)
HALO = 32
STEP = 256


def horner(coefs, z):
    total = coefs[-1] * z + coefs[-2]
    for coef in coefs[-3::-1]:
        total = total * z + coef
    return total


def cos_sin_turns(turns):
    rest = turns - jnp.round(turns)
    z = rest * rest
    return horner(COS_TURN, z), horner(SIN_TURN, z) * rest


def cos_sin(phase):
    z = phase * phase
    quarter_sin = horner(SIN_QUARTER, z) * phase
    half_sin = quarter_sin * horner(COS_QUARTER, z)
    half_cos = math.sqrt(2.0) - quarter_sin * quarter_sin
    return 1.0 - half_sin * half_sin, half_sin * half_cos


def dot(a, b):
    return jnp.dot(a, b, preferred_element_type=jnp.float32)


def split_parts(product, rows):
    out = []
    for k in range(product.shape[1] // 256):
        top = product[:rows, 256 * k : 256 * (k + 1)]
        low = product[rows:, 256 * k : 256 * (k + 1)]
        out.append((top[:, :128] - low[:, 128:], top[:, 128:] + low[:, :128]))
    return out


def lanes_inside(block, shift, col_count):
    cols = block * 128 - shift + lax.broadcasted_iota(jnp.int32, (1, 128), 1)
    return ((cols >= 0) & (cols < col_count)).astype(jnp.float32)


def pick_kernel(halo, order, potential, *refs):
    outs, sems = refs[:-1], refs[-1]
    rows = potential.shape[1]
    whole, low, high = pl.ds(0, rows), pl.ds(0, halo), pl.ds(rows - halo, halo)
    picks = ((0, whole), (0, high), (0, low), (1, whole), (2, high), (2, low))
    copies = []
    for i, (step, part) in enumerate(picks):
        copy = pltpu.make_async_copy(potential.at[order[step], part], outs[i], sems.at[i])
        copy.start()
        copies.append(copy)
    for copy in copies:
        copy.wait()


def toeplitz(row, count, shift):
    wide = jnp.broadcast_to(row, (count, 256))
    return pltpu.roll(wide, shift % 256, 1, stride=1, stride_axis=0)


def inside_rows(first, count, total):
    at = first + lax.broadcasted_iota(jnp.int32, (count, 1), 0)
    return ((at >= 0) & (at < total)).astype(jnp.float32)


def prepare_kernel(
    waves, rows, total_rows, col_count, tilt_index, first_row, tilt_table, fresnel, ctf, mtf,
    band, wide_band, band2, band3, band4, wide_rows, row_taps, col_taps, ex, ey, line,
):
    line[...] = jnp.zeros_like(line)
    line[0:2, : fresnel.shape[1]] = fresnel[...].astype(jnp.bfloat16).astype(jnp.float32)
    line[2:4, : ctf.shape[1]] = ctf[...].astype(jnp.bfloat16).astype(jnp.float32)
    line[4:5, : mtf.shape[1]] = mtf[...]
    first = first_row[0]

    def columns(target, at, shift):
        for part in range(2):
            made = toeplitz(line[at + part : at + part + 1], 128, shift)
            for k in range(2):
                turned = jnp.transpose(made[:, 128 * k : 128 * k + 128])
                up, down = 256 * k, 256 * k + 128
                if part == 0:
                    target[up:down, :128] = turned.astype(jnp.bfloat16)
                    target[down : down + 128, 128:] = turned.astype(jnp.bfloat16)
                else:
                    target[up:down, 128:] = turned.astype(jnp.bfloat16)
                    target[down : down + 128, :128] = (-turned).astype(jnp.bfloat16)

    columns(band, 0, 65 - (fresnel.shape[1] + 1) // 2)
    columns(wide_band, 2, 65 - (ctf.shape[1] + 1) // 2)
    for target, halo in ((band2, 2 * HALO), (band3, HALO), (band4, 0)):
        count, count_in = target.shape[0] // 2, target.shape[1]
        keep = inside_rows(first - halo, count, total_rows)
        for part in range(2):
            made = toeplitz(line[part : part + 1], count, HALO - (fresnel.shape[1] - 1) // 2) * keep
            target[count * part : count * part + count] = made[:, :count_in].astype(jnp.bfloat16)
    for part in range(2):
        made = toeplitz(line[2 + part : 3 + part], 128, 65 - (ctf.shape[1] + 1) // 2)
        wide_rows[128 * part : 128 * part + 128] = made.astype(jnp.bfloat16)
    reach = (mtf.shape[1] - 1) // 2
    row_taps[...] = toeplitz(line[4:5], 128, 64 - reach)
    width = col_taps.shape[0]
    off = lax.broadcasted_iota(jnp.int32, (width, 256), 1) - lax.broadcasted_iota(
        jnp.int32, (width, 256), 0
    )
    made = jnp.where(jnp.abs(off) <= reach, toeplitz(line[4:5], width, -reach), 0.0)
    col_taps[...] = made[:, :width]
    count = ex.shape[1]
    at = first - 3 * HALO + lax.broadcasted_iota(jnp.int32, (count, 128), 0)
    keep = ((at >= 0) & (at < total_rows)).astype(jnp.float32)
    at = at.astype(jnp.float32) * (1.0 / total_rows)
    across = lax.broadcasted_iota(jnp.int32, (1, ey.shape[1]), 1)
    keep_cols = (across < col_count).astype(jnp.float32)
    across = across.astype(jnp.float32) * (1.0 / col_count)
    for w in range(waves):
        cosine, sine = cos_sin_turns(at * tilt_table[tilt_index[w], 0])
        ex[2 * w] = cosine * keep
        ex[2 * w + 1] = sine * keep
        cosine, sine = cos_sin_turns(across * tilt_table[tilt_index[w], 1])
        ey[2 * w : 2 * w + 1] = cosine * keep_cols
        ey[2 * w + 1 : 2 * w + 2] = sine * keep_cols


def first_kernel(waves, order, *refs):
    pieces, (ex, ey, band, out, ring) = refs[:5], refs[5:]

    @pl.when(pl.program_id(0) == 0)
    def _():
        ring[:, :, :256] = jnp.zeros((waves, ring.shape[1], 256), jnp.bfloat16)

    for blk in range(2):
        lanes = pl.ds(128 * blk, 128)
        row = 0
        for piece in pieces:
            rows = piece.shape[-2]
            for start in range(0, rows, 32):
                if len(piece.shape) == 3:
                    phase = piece[0, pl.ds(start, 32), lanes]
                else:
                    phase = piece[pl.ds(start, 32), lanes]
                cosine, sine = cos_sin(phase.astype(jnp.float32))
                for w in range(waves):
                    yr, yi = ey[2 * w : 2 * w + 1, lanes], ey[2 * w + 1 : 2 * w + 2, lanes]
                    ur, ui = cosine * yr - sine * yi, cosine * yi + sine * yr
                    xr = ex[2 * w, pl.ds(row, 32)]
                    xi = ex[2 * w + 1, pl.ds(row, 32)]
                    to = 256 * (blk + 1)
                    ring[w, pl.ds(row, 32), to : to + 128] = (ur * xr - ui * xi).astype(jnp.bfloat16)
                    ring[w, pl.ds(row, 32), to + 128 : to + 256] = (ur * xi + ui * xr).astype(
                        jnp.bfloat16
                    )
                row += 32
    for w in range(waves):
        for blk in range(2):
            lanes = pl.ds(256 * blk, 256)
            out[w, :, lanes] = dot(ring[w, :, 256 * blk : 256 * blk + 512], band[...]).astype(
                jnp.bfloat16
            )
        ring[w, :, :256] = ring[w, :, 512:768]


def gather_rows(pieces, lanes):
    found = []
    for piece in pieces:
        if len(piece.shape) == 3:
            found.append(piece[0, :, lanes])
        else:
            found.append(piece[:, lanes])
    return jnp.concatenate(found, axis=0).astype(jnp.float32)


def transmit(ring, product, phases, masks, waves, rows):
    factors = []
    for phase, mask in zip(phases, masks):
        cosine, sine = cos_sin(phase)
        factors.append((cosine * mask, sine * mask))
    for w in range(waves):
        for blk, (real, imag) in enumerate(split_parts(product[w], rows)):
            cosine, sine = factors[blk]
            to = 256 * (blk + 1)
            ring[w, :, to : to + 128] = (real * cosine - imag * sine).astype(jnp.bfloat16)
            ring[w, :, to + 128 : to + 256] = (real * sine + imag * cosine).astype(jnp.bfloat16)


def second_kernel(waves, col_count, order, *refs):
    pieces, (spread, rows_band, band, out, ring, last) = refs[:3], refs[3:]
    g = pl.program_id(0)

    @pl.when(g == 0)
    def _():
        ring[:, :, :256] = jnp.zeros((waves, ring.shape[1], 256), jnp.bfloat16)
        last[...] = jnp.zeros_like(last)

    rows = ring.shape[1]
    low = lax.broadcasted_iota(jnp.int32, (rows, 128), 1) < 64
    turned = [last[...]]
    for blk in range(2):
        turned.append(pltpu.roll(gather_rows(pieces, pl.ds(128 * blk, 128)), 64, 1))
    last[...] = turned[2]
    phases = [jnp.where(low, turned[0], turned[1]), jnp.where(low, turned[1], turned[2])]
    masks = [lanes_inside(2 * g, 64, col_count), lanes_inside(2 * g + 1, 64, col_count)]
    product = [dot(rows_band[...], spread[w]) for w in range(waves)]
    transmit(ring, product, phases, masks, waves, rows)
    for w in range(waves):
        for blk in range(2):
            out[w, :, 256 * blk : 256 * (blk + 1)] = dot(
                ring[w, :, 256 * blk : 256 * blk + 512], band[...]
            ).astype(jnp.bfloat16)
        ring[w, :, :256] = ring[w, :, 512:768]


def third_kernel(waves, col_count, order, owner, *refs):
    pieces = refs[:3]
    spread, rows_band, band, last_band, wide_band, exit_wave, focused, ring, last, waved, turned = refs[3:]
    g = pl.program_id(0)

    @pl.when(g == 0)
    def _():
        ring[:, :, :256] = jnp.zeros((waves, ring.shape[1], 256), jnp.bfloat16)
        waved[:, :, :256] = jnp.zeros((waves, waved.shape[1], 256), jnp.bfloat16)
        turned[...] = jnp.zeros_like(turned)
        last[...] = jnp.zeros_like(last)

    rows, kept = ring.shape[1], waved.shape[1]
    phases = [last[...], gather_rows(pieces, pl.ds(0, 128))]
    last[...] = gather_rows(pieces, pl.ds(128, 128))
    masks = [lanes_inside(2 * g - 1, 0, col_count), lanes_inside(2 * g, 0, col_count)]
    product = [dot(rows_band[...], spread[w]) for w in range(waves)]
    transmit(ring, product, phases, masks, waves, rows)
    low = lax.broadcasted_iota(jnp.int32, (kept, 128), 1) < 64
    masks = [lanes_inside(2 * g - 1, 64, col_count), lanes_inside(2 * g, 64, col_count)]
    for w in range(waves):
        for blk in range(2):
            made = dot(ring[w, :, 256 * blk : 256 * blk + 512], band[...]).astype(jnp.bfloat16)
            ((real, imag),) = split_parts(dot(last_band[...], made), kept)
            to = 256 * (blk + 1)
            for part, value in enumerate((real, imag)):
                waved[w, :, to + 128 * part : to + 128 * part + 128] = (value * masks[blk]).astype(
                    jnp.bfloat16
                )
                rolled = pltpu.roll(value, 64, 1)
                exit_wave[w, part, :, 128 * blk : 128 * blk + 128] = jnp.where(
                    low, turned[w, part], rolled
                )
                turned[w, part] = rolled
            made = dot(waved[w, :, 256 * blk : 256 * blk + 512], wide_band[...]).astype(jnp.bfloat16)
            for part in range(2):
                block = made[:, 128 * part : 128 * part + 128]
                if len(focused.shape) == 5:
                    focused[0, w, part, :, 128 * blk : 128 * blk + 128] = block
                else:
                    focused[w, part, :, 128 * blk : 128 * blk + 128] = block
        ring[w, :, :256] = ring[w, :, 512:768]
        waved[w, :, :256] = waved[w, :, 512:768]


def detector_kernel(waves, tile_wave, taps_band, row_taps, col_taps, out, padded):
    sources, rows, width = tile_wave.shape[0], tile_wave.shape[3], tile_wave.shape[4]
    total = sources * rows
    edge = jnp.zeros((64, width), jnp.float32)
    padded[:64] = edge
    padded[64 + total :] = edge
    for b in range(total // 128):
        image = None
        for w in range(waves):
            parts = []
            for part in range(2):
                window = []
                for k in range(2 * b - 1, 2 * b + 3):
                    if 0 <= k < total // 64:
                        window.append(tile_wave[k, w, part])
                    else:
                        window.append(jnp.zeros((64, width), jnp.bfloat16))
                parts.append(jnp.concatenate(window, axis=0))
            real, imag = dot(taps_band[...], parts[0]), dot(taps_band[...], parts[1])
            re = real[:128] - imag[128:]
            im = imag[:128] + real[128:]
            term = re * re + im * im
            image = term if image is None else image + term
        padded[64 + 128 * b : 192 + 128 * b] = image / waves
    for b in range(total // 128):
        rows_done = jnp.dot(
            row_taps[...],
            padded[128 * b : 128 * b + 256],
            precision=highest,
            preferred_element_type=jnp.float32,
        )
        out[:, 128 * b : 128 * b + 128] = lax.dot_general(
            col_taps[...],
            rows_done,
            (((1,), (1,)), ((), ())),
            precision=highest,
            preferred_element_type=jnp.float32,
        )


def block_windows(values):
    length = values.shape[-1]
    padded = jnp.pad(values, [(0, 0)] * (values.ndim - 1) + [(64, 64)])
    blocks = padded.reshape(values.shape[:-1] + (length // 128 + 1, 128))
    return jnp.concatenate([blocks[..., :-1, :], blocks[..., 1:, :]], axis=-1)


def narrow_tiles(focused, owner, wide_rows, row_taps, col_taps, lane_count):
    waves, _, rows, col_count = focused.shape
    width = col_count // lane_count
    slots = jnp.arange(lane_count, dtype=jnp.int32)
    placing = (owner[None, :] == slots[:, None]).astype(jnp.bfloat16)
    focused = focused.reshape(waves, 2, rows, lane_count, width)
    focused = jnp.einsum("jl,acrlk->jackr", placing, focused, preferred_element_type=jnp.float32)
    sent = focused.astype(jnp.bfloat16)
    tile_wave = lax.all_to_all(sent, "lat", split_axis=0, concat_axis=4, tiled=True)[0]
    windows = block_windows(tile_wave)
    taps_band = wide_rows.reshape(2, 128, 256)
    made = jnp.einsum("acwbi,doi->acdwbo", windows, taps_band, preferred_element_type=jnp.float32)
    real = made[:, 0, 0] - made[:, 1, 1]
    imag = made[:, 1, 0] + made[:, 0, 1]
    image = jnp.sum(real * real + imag * imag, axis=0) / waves
    image = image.reshape(width, lane_count * rows)
    blurred = jnp.einsum("wbi,oi->wbo", block_windows(image), row_taps, precision=highest)
    return jnp.dot(col_taps, blurred.reshape(width, lane_count * rows), precision=highest)


def local(potential, tilt_index, slice_order, tilt_table, fresnel_taps, ctf_taps, mtf_taps, owner):
    row_count, col_count = potential.shape[1:]
    lane_count = lax.axis_size("lat")
    total_rows = row_count * lane_count
    tile_cols = col_count // lane_count
    waves = tilt_index.shape[0]
    first_row = lax.axis_index("lat") * row_count
    steps = col_count // STEP

    def neighbour(value, offset):
        pairs = [(i, i + offset) for i in range(lane_count) if 0 <= i + offset < lane_count]
        return lax.ppermute(value, "lat", pairs)

    rows1, rows2, rows3 = (row_count + 2 * HALO * k for k in (3, 2, 1))
    anywhere = pl.BlockSpec(memory_space=pl.ANY)
    in_vmem = pl.BlockSpec(memory_space=pltpu.VMEM)
    in_smem = pl.BlockSpec(memory_space=pltpu.SMEM)
    picked = pl.pallas_call(
        functools.partial(pick_kernel, HALO),
        name="pick_rows",
        out_shape=[
            jax.ShapeDtypeStruct((rows, col_count), potential.dtype)
            for rows in (row_count, HALO, HALO, row_count, HALO, HALO)
        ],
        in_specs=[in_smem, anywhere],
        out_specs=[anywhere] * 6,
        scratch_shapes=[pltpu.SemaphoreType.DMA((6,))],
        cost_estimate=pl.CostEstimate(flops=0, bytes_accessed=4 << 20, transcendentals=0),
    )(slice_order, potential)
    whole, high, low, second, third_high, third_low = picked
    up1, down1 = neighbour(whole, 1), neighbour(whole, -1)
    up2, down2 = neighbour(high, 2), neighbour(low, -2)
    second_up, second_down = neighbour(second, 1), neighbour(second, -1)
    third_up, third_down = neighbour(third_high, 1), neighbour(third_low, -1)

    def made(shape, dtype):
        return jax.ShapeDtypeStruct(shape, dtype)

    band, wide_band, band2, band3, band4, wide_rows, row_taps, col_taps, ex, ey = pl.pallas_call(
        functools.partial(prepare_kernel, waves, row_count, total_rows, col_count),
        name="prepare",
        out_shape=[
            made((512, 256), jnp.bfloat16),
            made((512, 256), jnp.bfloat16),
            made((2 * rows2, rows1), jnp.bfloat16),
            made((2 * rows3, rows2), jnp.bfloat16),
            made((2 * row_count, rows3), jnp.bfloat16),
            made((256, 256), jnp.bfloat16),
            made((128, 256), jnp.float32),
            made((tile_cols, tile_cols), jnp.float32),
            made((2 * waves, rows1, 128), jnp.float32),
            made((2 * waves, col_count + STEP), jnp.float32),
        ],
        in_specs=[in_smem] * 3 + [in_vmem] * 3,
        out_specs=[in_vmem] * 10,
        scratch_shapes=[pltpu.VMEM((8, 256), jnp.float32)],
        cost_estimate=pl.CostEstimate(flops=1 << 31, bytes_accessed=2 << 20, transcendentals=0),
    )(tilt_index, first_row[None], tilt_table, fresnel_taps, ctf_taps, mtf_taps[None])

    def clamp(g):
        return jnp.minimum(g, steps - 1)

    def piece(rows):
        return pl.BlockSpec((rows, STEP), lambda g, *_: (0, clamp(g)))

    def mine(step, start, rows):
        return pl.BlockSpec(
            (1, rows, STEP), lambda g, order, *_: (order[step], start // rows, clamp(g))
        )

    def fixed(*shape):
        return pl.BlockSpec(shape, lambda g, *_: (0,) * len(shape))

    def blocks(rows):
        return pl.BlockSpec((waves, rows, 512), lambda g, *_: (0, 0, g))

    params = pltpu.CompilerParams(
        dimension_semantics=("arbitrary",), vmem_limit_bytes=48 * 1024 * 1024
    )

    def cost(flops, count):
        return pl.CostEstimate(flops=flops, bytes_accessed=count, transcendentals=0)

    spread_cols = (steps + 1) * 512
    spread = pl.pallas_call(
        functools.partial(first_kernel, waves),
        name="first_step",
        out_shape=jax.ShapeDtypeStruct((waves, rows1, spread_cols), jnp.bfloat16),
        grid_spec=pltpu.PrefetchScalarGridSpec(
            num_scalar_prefetch=1,
            grid=(steps + 1,),
            in_specs=[
                piece(HALO),
                piece(row_count),
                mine(0, 0, row_count),
                piece(row_count),
                piece(HALO),
                fixed(2 * waves, rows1, 128),
                pl.BlockSpec((2 * waves, STEP), lambda g, *_: (0, g)),
                fixed(512, 256),
            ],
            out_specs=blocks(rows1),
            scratch_shapes=[pltpu.VMEM((waves, rows1, 768), jnp.bfloat16)],
        ),
        compiler_params=params,
        cost_estimate=cost(waves * rows1 * spread_cols * 1024, 12 << 20),
    )(slice_order, up2, up1, potential, down1, down2, ex, ey, band)

    spread = pl.pallas_call(
        functools.partial(second_kernel, waves, col_count),
        name="second_step",
        out_shape=jax.ShapeDtypeStruct((waves, rows2, spread_cols), jnp.bfloat16),
        grid_spec=pltpu.PrefetchScalarGridSpec(
            num_scalar_prefetch=1,
            grid=(steps + 1,),
            in_specs=[
                piece(row_count),
                mine(1, 0, row_count),
                piece(row_count),
                blocks(rows1),
                fixed(2 * rows2, rows1),
                fixed(512, 256),
            ],
            out_specs=blocks(rows2),
            scratch_shapes=[
                pltpu.VMEM((waves, rows2, 768), jnp.bfloat16),
                pltpu.VMEM((rows2, 128), jnp.float32),
            ],
        ),
        compiler_params=params,
        cost_estimate=cost(waves * rows2 * spread_cols * 2048, 16 << 20),
    )(slice_order, second_up, potential, second_down, spread, band2, band)

    def done(g):
        return jnp.maximum(g - 1, 0)

    placed = tile_cols == STEP
    if placed:
        focused_shape = (lane_count, waves, 2, row_count, tile_cols)
        focused_spec = pl.BlockSpec(
            (1, waves, 2, row_count, tile_cols),
            lambda g, order, owner: (owner[done(g)], 0, 0, 0, 0),
        )
    else:
        focused_shape = (waves, 2, row_count, col_count)
        focused_spec = pl.BlockSpec(
            (waves, 2, row_count, STEP), lambda g, *_: (0, 0, 0, done(g))
        )
    exit_wave, focused = pl.pallas_call(
        functools.partial(third_kernel, waves, col_count),
        name="third_step",
        out_shape=(
            jax.ShapeDtypeStruct((waves, 2, row_count, col_count), jnp.float32),
            jax.ShapeDtypeStruct(focused_shape, jnp.bfloat16),
        ),
        grid_spec=pltpu.PrefetchScalarGridSpec(
            num_scalar_prefetch=2,
            grid=(steps + 1,),
            in_specs=[
                piece(HALO),
                mine(2, 0, row_count),
                piece(HALO),
                blocks(rows2),
                fixed(2 * rows3, rows2),
                fixed(512, 256),
                fixed(2 * row_count, rows3),
                fixed(512, 256),
            ],
            out_specs=(
                pl.BlockSpec((waves, 2, row_count, STEP), lambda g, *_: (0, 0, 0, done(g))),
                focused_spec,
            ),
            scratch_shapes=[
                pltpu.VMEM((waves, rows3, 768), jnp.bfloat16),
                pltpu.VMEM((rows3, 128), jnp.float32),
                pltpu.VMEM((waves, row_count, 768), jnp.bfloat16),
                pltpu.VMEM((waves, 2, row_count, 128), jnp.float32),
            ],
        ),
        compiler_params=params,
        cost_estimate=cost(waves * rows3 * spread_cols * 3072, 16 << 20),
    )(slice_order, owner, third_up, potential, third_down, spread, band3, band, band4, wide_band)

    if not placed:
        detector = narrow_tiles(focused, owner, wide_rows, row_taps, col_taps, lane_count)
        return exit_wave, detector[None]

    tile_wave = lax.all_to_all(focused, "lat", split_axis=0, concat_axis=0, tiled=True)
    detector = pl.pallas_call(
        functools.partial(detector_kernel, waves),
        name="detector",
        out_shape=jax.ShapeDtypeStruct((tile_cols, total_rows), jnp.float32),
        in_specs=[pl.BlockSpec(memory_space=pltpu.VMEM)] * 4,
        out_specs=pl.BlockSpec(memory_space=pltpu.VMEM),
        scratch_shapes=[pltpu.VMEM((total_rows + 128, tile_cols), jnp.float32)],
        compiler_params=pltpu.CompilerParams(vmem_limit_bytes=48 * 1024 * 1024),
        cost_estimate=cost(1 << 33, 4 << 20),
    )(tile_wave, wide_rows, row_taps, col_taps)
    return exit_wave, detector[None]


def solution(mesh):
    placed = (
        P(None, ("lamella", "lat"), None),
        P("lamella"),
        P("lamella"),
        P(),
        P(),
        P(),
        P(),
        P("lamella"),
    )
    return jax.shard_map(
        local,
        mesh=mesh,
        in_specs=placed,
        out_specs=(P(None, None, ("lamella", "lat"), None), P(("lamella", "lat"), None, None)),
        check_vma=False,
    )
```

```python
import functools
import math

import jax
import jax.numpy as jnp
from jax import lax
from jax.experimental import pallas as pl
from jax.experimental.pallas import tpu as pltpu
from jax.sharding import PartitionSpec as P

highest = lax.Precision.HIGHEST
SIN_TURN = (
    6.2831854820251465,
    -41.34170150756836,
    81.60513305664062,
    -76.70301818847656,
    42.02592849731445,
    -14.899847030639648,
    3.2381374835968018,
)
COS_TURN = (
    1.0,
    -19.73920440673828,
    64.93911743164062,
    -85.45014190673828,
    60.16762924194336,
    -25.967599868774414,
    6.528658390045166,
)
SIN_QUARTER = (
    0.4204482138156891,
    -0.004379667341709137,
    1.3686111742572393e-05,
    -2.0339173900651986e-08,
    1.679661791598175e-11,
)
COS_QUARTER = (
    1.6817927360534668,
    -0.052555955946445465,
    0.00027371387113817036,
    -5.690624220733298e-07,
    5.977824346636851e-10,
)
HALO = 32
STEP = 256


def horner(coefs, z):
    total = coefs[-1] * z + coefs[-2]
    for coef in coefs[-3::-1]:
        total = total * z + coef
    return total


def cos_sin_turns(turns):
    rest = turns - jnp.round(turns)
    z = rest * rest
    return horner(COS_TURN, z), horner(SIN_TURN, z) * rest


def cos_sin(phase):
    z = phase * phase
    quarter_sin = horner(SIN_QUARTER, z) * phase
    half_sin = quarter_sin * horner(COS_QUARTER, z)
    half_cos = math.sqrt(2.0) - quarter_sin * quarter_sin
    return 1.0 - half_sin * half_sin, half_sin * half_cos


def dot(a, b):
    return jnp.dot(a, b, preferred_element_type=jnp.float32)


def split_parts(product, rows):
    out = []
    for k in range(product.shape[1] // 256):
        top = product[:rows, 256 * k : 256 * (k + 1)]
        low = product[rows:, 256 * k : 256 * (k + 1)]
        out.append((top[:, :128] - low[:, 128:], top[:, 128:] + low[:, :128]))
    return out


def lanes_inside(block, shift, col_count):
    cols = block * 128 - shift + lax.broadcasted_iota(jnp.int32, (1, 128), 1)
    return ((cols >= 0) & (cols < col_count)).astype(jnp.float32)


def toeplitz(row, count, shift):
    wide = jnp.broadcast_to(row, (count, 256))
    return pltpu.roll(wide, shift % 256, 1, stride=1, stride_axis=0)


def inside_rows(first, count, total):
    at = first + lax.broadcasted_iota(jnp.int32, (count, 1), 0)
    return ((at >= 0) & (at < total)).astype(jnp.float32)


def prepare_kernel(
    waves, rows, total_rows, col_count, tilt_index, first_row, tilt_table, fresnel, ctf, mtf,
    band, wide_band, band2, band3, band4, wide_rows, row_taps, col_taps, ex, ey, line,
):
    line[...] = jnp.zeros_like(line)
    line[0:2, : fresnel.shape[1]] = fresnel[...].astype(jnp.bfloat16).astype(jnp.float32)
    line[2:4, : ctf.shape[1]] = ctf[...].astype(jnp.bfloat16).astype(jnp.float32)
    line[4:5, : mtf.shape[1]] = mtf[...]
    first = first_row[0]

    def columns(target, at, shift):
        for part in range(2):
            made = toeplitz(line[at + part : at + part + 1], 128, shift)
            for k in range(2):
                turned = jnp.transpose(made[:, 128 * k : 128 * k + 128])
                up, down = 256 * k, 256 * k + 128
                if part == 0:
                    target[up:down, :128] = turned.astype(jnp.bfloat16)
                    target[down : down + 128, 128:] = turned.astype(jnp.bfloat16)
                else:
                    target[up:down, 128:] = turned.astype(jnp.bfloat16)
                    target[down : down + 128, :128] = (-turned).astype(jnp.bfloat16)

    columns(band, 0, 65 - (fresnel.shape[1] + 1) // 2)
    columns(wide_band, 2, 65 - (ctf.shape[1] + 1) // 2)
    for target, halo in ((band2, 2 * HALO), (band3, HALO), (band4, 0)):
        count, count_in = target.shape[0] // 2, target.shape[1]
        keep = inside_rows(first - halo, count, total_rows)
        for part in range(2):
            made = toeplitz(line[part : part + 1], count, HALO - (fresnel.shape[1] - 1) // 2) * keep
            target[count * part : count * part + count] = made[:, :count_in].astype(jnp.bfloat16)
    for part in range(2):
        made = toeplitz(line[2 + part : 3 + part], 128, 65 - (ctf.shape[1] + 1) // 2)
        wide_rows[128 * part : 128 * part + 128] = made.astype(jnp.bfloat16)
    reach = (mtf.shape[1] - 1) // 2
    row_taps[...] = toeplitz(line[4:5], 128, 64 - reach)
    width = col_taps.shape[0]
    off = lax.broadcasted_iota(jnp.int32, (width, 256), 1) - lax.broadcasted_iota(
        jnp.int32, (width, 256), 0
    )
    made = jnp.where(jnp.abs(off) <= reach, toeplitz(line[4:5], width, -reach), 0.0)
    col_taps[...] = made[:, :width]
    count = ex.shape[1]
    at = first - 3 * HALO + lax.broadcasted_iota(jnp.int32, (count, 128), 0)
    keep = ((at >= 0) & (at < total_rows)).astype(jnp.float32)
    at = at.astype(jnp.float32) * (1.0 / total_rows)
    across = lax.broadcasted_iota(jnp.int32, (1, ey.shape[1]), 1)
    keep_cols = (across < col_count).astype(jnp.float32)
    across = across.astype(jnp.float32) * (1.0 / col_count)
    for w in range(waves):
        cosine, sine = cos_sin_turns(at * tilt_table[tilt_index[w], 0])
        ex[2 * w] = cosine * keep
        ex[2 * w + 1] = sine * keep
        cosine, sine = cos_sin_turns(across * tilt_table[tilt_index[w], 1])
        ey[2 * w : 2 * w + 1] = cosine * keep_cols
        ey[2 * w + 1 : 2 * w + 2] = sine * keep_cols


def rows_of(piece, start, count, lanes):
    if len(piece.shape) == 3:
        found = piece[0, pl.ds(start, count), lanes]
    else:
        found = piece[pl.ds(start, count), lanes]
    return found.astype(jnp.float32)


def chunks(pieces, size):
    row = 0
    for piece in pieces:
        for start in range(0, piece.shape[-2], size):
            yield piece, start, row
            row += size


def columns_pass(ring, band):
    waves, rows = ring.shape[:2]
    pairs = [(w, blk) for w in range(waves) for blk in range(2)]
    windows = [ring[w, :, 256 * blk : 256 * blk + 512] for w, blk in pairs]
    result = dot(jnp.concatenate(windows, axis=0), band[...])
    for w in range(waves):
        ring[w, :, :256] = ring[w, :, 512:768]
    return {pair: result[rows * i : rows * i + rows] for i, pair in enumerate(pairs)}


def store_spread(spread, result):
    for (w, blk), value in result.items():
        spread[w, :, 256 * blk : 256 * blk + 256] = value.astype(jnp.bfloat16)


def start_wave(pieces, ex, ey, ring, waves):
    for piece, start, row in chunks(pieces, 32):
        for blk in range(2):
            lanes = pl.ds(128 * blk, 128)
            cosine, sine = cos_sin(rows_of(piece, start, 32, lanes))
            to = 256 * (blk + 1)
            for w in range(waves):
                yr, yi = ey[2 * w : 2 * w + 1, lanes], ey[2 * w + 1 : 2 * w + 2, lanes]
                ur, ui = cosine * yr - sine * yi, cosine * yi + sine * yr
                xr, xi = ex[2 * w, pl.ds(row, 32)], ex[2 * w + 1, pl.ds(row, 32)]
                ring[w, pl.ds(row, 32), to : to + 128] = (ur * xr - ui * xi).astype(jnp.bfloat16)
                ring[w, pl.ds(row, 32), to + 128 : to + 256] = (ur * xi + ui * xr).astype(
                    jnp.bfloat16
                )


def transmit(pieces, product, ring, last, masks, turn):
    waves, rows = ring.shape[:2]
    low = lax.broadcasted_iota(jnp.int32, (32, 128), 1) < 64
    for piece, start, row in chunks(pieces, 32):
        here = pl.ds(row, 32)
        found = [rows_of(piece, start, 32, pl.ds(128 * blk, 128)) for blk in range(2)]
        if turn:
            found = [pltpu.roll(value, 64, 1) for value in found]
            phases = [jnp.where(low, last[here], found[0]), jnp.where(low, found[0], found[1])]
        else:
            phases = [last[here], found[0]]
        last[here] = found[1]
        for blk in range(2):
            cosine, sine = cos_sin(phases[blk])
            cosine, sine = cosine * masks[blk], sine * masks[blk]
            to = 256 * (blk + 1)
            for w in range(waves):
                top = product[w, here, 256 * blk : 256 * blk + 256]
                under = product[w, pl.ds(rows + row, 32), 256 * blk : 256 * blk + 256]
                real, imag = top[:, :128] - under[:, 128:], top[:, 128:] + under[:, :128]
                ring[w, here, to : to + 128] = (real * cosine - imag * sine).astype(jnp.bfloat16)
                ring[w, here, to + 128 : to + 256] = (real * sine + imag * cosine).astype(
                    jnp.bfloat16
                )


def steps_kernel(
    waves, col_count, lag, order, owner, *refs
):
    first, second, third = refs[:5], refs[5:8], refs[8:11]
    ex, ey, band, band2, band3, band4, wide_band, exit_wave, focused = refs[11:20]
    ring1, ring2, ring3, spread1, spread2, product2, product3, waved, last2, last3, turned = refs[20:]
    g = pl.program_id(0)

    def clear(ring):
        ring[:, :, :256] = jnp.zeros((waves, ring.shape[1], 256), jnp.bfloat16)

    @pl.when(g == 0)
    def _():
        clear(ring1)

    @pl.when(g == lag)
    def _():
        clear(ring2)
        last2[...] = jnp.zeros_like(last2)

    @pl.when(g == 2 * lag)
    def _():
        clear(ring3)
        clear(waved)
        last3[...] = jnp.zeros_like(last3)
        turned[...] = jnp.zeros_like(turned)

    def stage1():
        start_wave(first, ex, ey, ring1, waves)
        store_spread(spread1, columns_pass(ring1, band))

    def stage2():
        at = g - lag
        masks = [lanes_inside(2 * at, 64, col_count), lanes_inside(2 * at + 1, 64, col_count)]
        for w in range(waves):
            product2[w] = dot(band2[...], spread1[w])
        transmit(second, product2, ring2, last2, masks, True)
        store_spread(spread2, columns_pass(ring2, band))

    def stage3():
        at = g - 2 * lag
        masks = [lanes_inside(2 * at - 1, 0, col_count), lanes_inside(2 * at, 0, col_count)]
        for w in range(waves):
            product3[w] = dot(band3[...], spread2[w])
        transmit(third, product3, ring3, last3, masks, False)
        result = columns_pass(ring3, band)
        kept = waved.shape[1]
        low = lax.broadcasted_iota(jnp.int32, (kept, 128), 1) < 64
        masks = [lanes_inside(2 * at - 1, 64, col_count), lanes_inside(2 * at, 64, col_count)]
        for w in range(waves):
            made = jnp.concatenate([result[w, 0], result[w, 1]], axis=1).astype(jnp.bfloat16)
            for blk, parts in enumerate(split_parts(dot(band4[...], made), kept)):
                to = 256 * (blk + 1)
                for part, value in enumerate(parts):
                    at_lane = to + 128 * part
                    waved[w, :, at_lane : at_lane + 128] = (value * masks[blk]).astype(jnp.bfloat16)
                    rolled = pltpu.roll(value, 64, 1)
                    exit_wave[w, part, :, 128 * blk : 128 * blk + 128] = jnp.where(
                        low, turned[w, part], rolled
                    )
                    turned[w, part] = rolled
        for (w, blk), value in columns_pass(waved, wide_band).items():
            for part in range(2):
                block = value[:, 128 * part : 128 * part + 128].astype(jnp.bfloat16)
                if len(focused.shape) == 5:
                    focused[0, w, part, :, 128 * blk : 128 * blk + 128] = block
                else:
                    focused[w, part, :, 128 * blk : 128 * blk + 128] = block

    for stage in (stage1, stage2, stage3) if lag == 0 else (stage3, stage2, stage1):
        stage()


def pick_kernel(halo, order, potential, *refs):
    outs, held, load_sems, sems = refs[:-3], refs[-3], refs[-2], refs[-1]
    rows = potential.shape[1]
    whole, low, high = pl.ds(0, rows), pl.ds(0, halo), pl.ds(rows - halo, halo)
    both1, up2, down2, up_rest, down_rest = outs
    after, beside = pl.ds(rows, halo), pl.ds(0, rows)
    picks = (
        (0, whole, both1, None), (0, high, up2, None), (0, low, down2, None),
        (1, whole, up_rest, beside), (1, whole, down_rest, beside),
        (2, high, up_rest, after), (2, low, down_rest, after),
    )
    loads = []
    for step in range(3):
        load = pltpu.make_async_copy(potential.at[order[step]], held.at[step], load_sems.at[step])
        load.start()
        loads.append(load)
    copies = []
    for i, (step, part, target, where) in enumerate(picks):
        if loads[step] is not None:
            loads[step].wait()
            loads[step] = None
        target = target if where is None else target.at[where]
        copy = pltpu.make_async_copy(held.at[step, part], target, sems.at[i])
        copy.start()
        copies.append(copy)
    for copy in copies:
        copy.wait()


def detector_kernel(waves, tile_wave, taps_band, row_taps, col_taps, out, padded):
    sources, rows, width = tile_wave.shape[0], tile_wave.shape[3], tile_wave.shape[4]
    total = sources * rows
    edge = jnp.zeros((64, width), jnp.float32)
    padded[:64] = edge
    padded[64 + total :] = edge
    for b in range(total // 128):
        image = None
        for w in range(waves):
            parts = []
            for part in range(2):
                window = []
                for k in range(2 * b - 1, 2 * b + 3):
                    if 0 <= k < total // 64:
                        window.append(tile_wave[k, w, part])
                    else:
                        window.append(jnp.zeros((64, width), jnp.bfloat16))
                parts.append(jnp.concatenate(window, axis=0))
            real, imag = dot(taps_band[...], parts[0]), dot(taps_band[...], parts[1])
            re = real[:128] - imag[128:]
            im = imag[:128] + real[128:]
            term = re * re + im * im
            image = term if image is None else image + term
        padded[64 + 128 * b : 192 + 128 * b] = image / waves
    for b in range(total // 128):
        rows_done = jnp.dot(
            row_taps[...],
            padded[128 * b : 128 * b + 256],
            precision=highest,
            preferred_element_type=jnp.float32,
        )
        out[:, 128 * b : 128 * b + 128] = lax.dot_general(
            col_taps[...],
            rows_done,
            (((1,), (1,)), ((), ())),
            precision=highest,
            preferred_element_type=jnp.float32,
        )


def block_windows(values):
    length = values.shape[-1]
    padded = jnp.pad(values, [(0, 0)] * (values.ndim - 1) + [(64, 64)])
    blocks = padded.reshape(values.shape[:-1] + (length // 128 + 1, 128))
    return jnp.concatenate([blocks[..., :-1, :], blocks[..., 1:, :]], axis=-1)


def narrow_tiles(focused, owner, wide_rows, row_taps, col_taps, lane_count):
    waves, _, rows, col_count = focused.shape
    width = col_count // lane_count
    slots = jnp.arange(lane_count, dtype=jnp.int32)
    placing = (owner[None, :] == slots[:, None]).astype(jnp.bfloat16)
    focused = focused.reshape(waves, 2, rows, lane_count, width)
    focused = jnp.einsum("jl,acrlk->jackr", placing, focused, preferred_element_type=jnp.float32)
    sent = focused.astype(jnp.bfloat16)
    tile_wave = lax.all_to_all(sent, "lat", split_axis=0, concat_axis=4, tiled=True)[0]
    windows = block_windows(tile_wave)
    taps_band = wide_rows.reshape(2, 128, 256)
    made = jnp.einsum("acwbi,doi->acdwbo", windows, taps_band, preferred_element_type=jnp.float32)
    real = made[:, 0, 0] - made[:, 1, 1]
    imag = made[:, 1, 0] + made[:, 0, 1]
    image = jnp.sum(real * real + imag * imag, axis=0) / waves
    image = image.reshape(width, lane_count * rows)
    blurred = jnp.einsum("wbi,oi->wbo", block_windows(image), row_taps, precision=highest)
    return jnp.dot(col_taps, blurred.reshape(width, lane_count * rows), precision=highest)


def local(potential, tilt_index, slice_order, tilt_table, fresnel_taps, ctf_taps, mtf_taps, owner):
    row_count, col_count = potential.shape[1:]
    lane_count = lax.axis_size("lat")
    total_rows = row_count * lane_count
    tile_cols = col_count // lane_count
    waves = tilt_index.shape[0]
    first_row = lax.axis_index("lat") * row_count
    steps = col_count // STEP

    def neighbour(value, offset):
        pairs = [(i, i + offset) for i in range(lane_count) if 0 <= i + offset < lane_count]
        return lax.ppermute(value, "lat", pairs)

    rows1, rows2, rows3 = (row_count + 2 * HALO * k for k in (3, 2, 1))
    anywhere = pl.BlockSpec(memory_space=pl.ANY)
    in_vmem = pl.BlockSpec(memory_space=pltpu.VMEM)
    in_smem = pl.BlockSpec(memory_space=pltpu.SMEM)
    picked = pl.pallas_call(
        functools.partial(pick_kernel, HALO),
        name="pick_rows",
        out_shape=[
            jax.ShapeDtypeStruct((rows, col_count), potential.dtype)
            for rows in (row_count, HALO, HALO, row_count + HALO, row_count + HALO)
        ],
        in_specs=[in_smem, anywhere],
        out_specs=[anywhere] * 5,
        scratch_shapes=[
            pltpu.VMEM((3, row_count, col_count), potential.dtype),
            pltpu.SemaphoreType.DMA((3,)),
            pltpu.SemaphoreType.DMA((7,)),
        ],
        cost_estimate=pl.CostEstimate(flops=0, bytes_accessed=4 << 20, transcendentals=0),
    )(slice_order, potential)
    whole, high, low, rest_high, rest_low = picked
    up1, down1 = neighbour(whole, 1), neighbour(whole, -1)
    up2, down2 = neighbour(high, 2), neighbour(low, -2)
    up_rest, down_rest = neighbour(rest_high, 1), neighbour(rest_low, -1)

    def made(shape, dtype):
        return jax.ShapeDtypeStruct(shape, dtype)

    band, wide_band, band2, band3, band4, wide_rows, row_taps, col_taps, ex, ey = pl.pallas_call(
        functools.partial(prepare_kernel, waves, row_count, total_rows, col_count),
        name="prepare",
        out_shape=[
            made((512, 256), jnp.bfloat16),
            made((512, 256), jnp.bfloat16),
            made((2 * rows2, rows1), jnp.bfloat16),
            made((2 * rows3, rows2), jnp.bfloat16),
            made((2 * row_count, rows3), jnp.bfloat16),
            made((256, 256), jnp.bfloat16),
            made((128, 256), jnp.float32),
            made((tile_cols, tile_cols), jnp.float32),
            made((2 * waves, rows1, 128), jnp.float32),
            made((2 * waves, col_count + STEP), jnp.float32),
        ],
        in_specs=[in_smem] * 3 + [in_vmem] * 3,
        out_specs=[in_vmem] * 10,
        scratch_shapes=[pltpu.VMEM((8, 256), jnp.float32)],
        cost_estimate=pl.CostEstimate(flops=1 << 31, bytes_accessed=2 << 20, transcendentals=0),
    )(tilt_index, first_row[None], tilt_table, fresnel_taps, ctf_taps, mtf_taps[None])

    lag = 1

    def clamp(g):
        return jnp.clip(g, 0, steps - 1)

    def piece(step, start, rows):
        return pl.BlockSpec((rows, STEP), lambda g, *_: (start // rows, clamp(g - step * lag)))

    def mine(step):
        return pl.BlockSpec(
            (1, row_count, STEP), lambda g, order, *_: (order[step], 0, clamp(g - step * lag))
        )

    def fixed(*shape):
        return pl.BlockSpec(shape, lambda g, *_: (0,) * len(shape))

    def done(g):
        return clamp(g - 1 - 2 * lag)

    placed = tile_cols == STEP
    if placed:
        focused_shape = (lane_count, waves, 2, row_count, tile_cols)
        focused_spec = pl.BlockSpec(
            (1, waves, 2, row_count, tile_cols),
            lambda g, order, owner: (owner[done(g)], 0, 0, 0, 0),
        )
    else:
        focused_shape = (waves, 2, row_count, col_count)
        focused_spec = pl.BlockSpec((waves, 2, row_count, STEP), lambda g, *_: (0, 0, 0, done(g)))

    def rings(rows, lanes, dtype=jnp.bfloat16):
        return pltpu.VMEM((waves, rows, lanes), dtype)

    exit_wave, focused = pl.pallas_call(
        functools.partial(steps_kernel, waves, col_count, lag),
        name="steps",
        out_shape=(
            made((waves, 2, row_count, col_count), jnp.float32),
            made(focused_shape, jnp.bfloat16),
        ),
        grid_spec=pltpu.PrefetchScalarGridSpec(
            num_scalar_prefetch=2,
            grid=(steps + 1 + 2 * lag,),
            in_specs=[
                piece(0, 0, HALO),
                piece(0, 0, row_count),
                mine(0),
                piece(0, 0, row_count),
                piece(0, 0, HALO),
                piece(1, 0, row_count),
                mine(1),
                piece(1, 0, row_count),
                piece(2, row_count, HALO),
                mine(2),
                piece(2, row_count, HALO),
                fixed(2 * waves, rows1, 128),
                pl.BlockSpec((2 * waves, STEP), lambda g, *_: (0, jnp.minimum(g, steps))),
                fixed(512, 256),
                fixed(2 * rows2, rows1),
                fixed(2 * rows3, rows2),
                fixed(2 * row_count, rows3),
                fixed(512, 256),
            ],
            out_specs=(
                pl.BlockSpec((waves, 2, row_count, STEP), lambda g, *_: (0, 0, 0, done(g))),
                focused_spec,
            ),
            scratch_shapes=[
                rings(rows1, 768),
                rings(rows2, 768),
                rings(rows3, 768),
                rings(rows1, 512),
                rings(rows2, 512),
                rings(2 * rows2, 512, jnp.float32),
                rings(2 * rows3, 512, jnp.float32),
                rings(row_count, 768),
                pltpu.VMEM((rows2, 128), jnp.float32),
                pltpu.VMEM((rows3, 128), jnp.float32),
                pltpu.VMEM((waves, 2, row_count, 128), jnp.float32),
            ],
        ),
        compiler_params=pltpu.CompilerParams(
            dimension_semantics=("arbitrary",), vmem_limit_bytes=40 * 1024 * 1024
        ),
        cost_estimate=pl.CostEstimate(
            flops=1 << 34, bytes_accessed=12 << 20, transcendentals=0
        ),
    )(
        slice_order, owner,
        up2, up1, potential, down1, down2,
        up_rest, potential, down_rest,
        up_rest, potential, down_rest,
        ex, ey, band, band2, band3, band4, wide_band,
    )

    if not placed:
        detector = narrow_tiles(focused, owner, wide_rows, row_taps, col_taps, lane_count)
        return exit_wave, detector[None]

    tile_wave = lax.all_to_all(focused, "lat", split_axis=0, concat_axis=0, tiled=True)
    detector = pl.pallas_call(
        functools.partial(detector_kernel, waves),
        name="detector",
        out_shape=jax.ShapeDtypeStruct((tile_cols, total_rows), jnp.float32),
        in_specs=[pl.BlockSpec(memory_space=pltpu.VMEM)] * 4,
        out_specs=pl.BlockSpec(memory_space=pltpu.VMEM),
        scratch_shapes=[pltpu.VMEM((total_rows + 128, tile_cols), jnp.float32)],
        compiler_params=pltpu.CompilerParams(vmem_limit_bytes=48 * 1024 * 1024),
        cost_estimate=pl.CostEstimate(
            flops=1 << 33, bytes_accessed=4 << 20, transcendentals=0
        ),
    )(tile_wave, wide_rows, row_taps, col_taps)
    return exit_wave, detector[None]


def solution(mesh):
    placed = (
        P(None, ("lamella", "lat"), None),
        P("lamella"),
        P("lamella"),
        P(),
        P(),
        P(),
        P(),
        P("lamella"),
    )
    return jax.shard_map(
        local,
        mesh=mesh,
        in_specs=placed,
        out_specs=(P(None, None, ("lamella", "lat"), None), P(("lamella", "lat"), None, None)),
        check_vma=False,
    )
```

```python
import functools
import math

import jax
import jax.numpy as jnp
from jax import lax
from jax.experimental import pallas as pl
from jax.experimental.pallas import tpu as pltpu
from jax.sharding import PartitionSpec as P

highest = lax.Precision.HIGHEST
SIN_TURN = (
    6.2831854820251465,
    -41.34170150756836,
    81.60513305664062,
    -76.70301818847656,
    42.02592849731445,
    -14.899847030639648,
    3.2381374835968018,
)
COS_TURN = (
    1.0,
    -19.73920440673828,
    64.93911743164062,
    -85.45014190673828,
    60.16762924194336,
    -25.967599868774414,
    6.528658390045166,
)
SIN_QUARTER = (
    0.4204482138156891,
    -0.004379667341709137,
    1.3686111742572393e-05,
    -2.0339173900651986e-08,
    1.679661791598175e-11,
)
COS_QUARTER = (
    1.6817927360534668,
    -0.052555955946445465,
    0.00027371387113817036,
    -5.690624220733298e-07,
    5.977824346636851e-10,
)
HALO = 32
STEP = 256


def horner(coefs, z):
    total = coefs[-1] * z + coefs[-2]
    for coef in coefs[-3::-1]:
        total = total * z + coef
    return total


def cos_sin_turns(turns):
    rest = turns - jnp.round(turns)
    z = rest * rest
    return horner(COS_TURN, z), horner(SIN_TURN, z) * rest


def cos_sin(phase):
    z = phase * phase
    quarter_sin = horner(SIN_QUARTER, z) * phase
    half_sin = quarter_sin * horner(COS_QUARTER, z)
    half_cos = math.sqrt(2.0) - quarter_sin * quarter_sin
    return 1.0 - half_sin * half_sin, half_sin * half_cos


def dot(a, b):
    return jnp.dot(a, b, preferred_element_type=jnp.float32)


def lanes_inside(block, shift, col_count):
    cols = block * 128 - shift + lax.broadcasted_iota(jnp.int32, (1, 128), 1)
    return ((cols >= 0) & (cols < col_count)).astype(jnp.float32)


def rows_of(ref, lead, start, count, lanes):
    if lead is None:
        found = ref[pl.ds(start, count), lanes]
    else:
        found = ref[lead, pl.ds(start, count), lanes]
    return found.astype(jnp.float32)


def chunks(pieces, size):
    row = 0
    for ref, lead, first, rows in pieces:
        for start in range(0, rows, size):
            yield ref, lead, first + start, row
            row += size


def columns_tasks(ring, band, store):
    waves = ring.shape[0]

    def task(w, blk):
        store(w, blk, dot(ring[w, :, 256 * blk : 256 * blk + 512], band[...]))
        if blk == 1:
            ring[w, :, :256] = ring[w, :, 512:768]

    return [functools.partial(task, w, blk) for w in range(waves) for blk in range(2)]


def spread_store(spread):
    rows = spread.shape[1] // 2

    def store(w, blk, value):
        lanes = pl.ds(128 * blk, 128)
        spread[w, :rows, lanes] = value[:, :128].astype(jnp.bfloat16)
        spread[w, rows:, lanes] = value[:, 128:].astype(jnp.bfloat16)

    return store


def rows_tasks(product, rows_band, spread):
    def task(w):
        product[w] = dot(rows_band[...], spread[w])

    return [functools.partial(task, w) for w in range(spread.shape[0])]


def run(*lists):
    for tasks in lists:
        for task in tasks:
            task()


def start_tasks(pieces, ex, ey, first_lane, ring):
    waves = ring.shape[0]

    def task(ref, lead, start, row):
        for blk in range(2):
            lanes = pl.ds(128 * blk, 128)
            cosine, sine = cos_sin(rows_of(ref, lead, start, 32, lanes))
            to = 256 * (blk + 1)
            for w in range(waves):
                at = pl.ds(first_lane + 128 * blk, 128)
                yr, yi = ey[2 * w : 2 * w + 1, at], ey[2 * w + 1 : 2 * w + 2, at]
                ur, ui = cosine * yr - sine * yi, cosine * yi + sine * yr
                xr, xi = ex[2 * w, pl.ds(row, 32)], ex[2 * w + 1, pl.ds(row, 32)]
                ring[w, pl.ds(row, 32), to : to + 128] = (ur * xr - ui * xi).astype(jnp.bfloat16)
                ring[w, pl.ds(row, 32), to + 128 : to + 256] = (ur * xi + ui * xr).astype(
                    jnp.bfloat16
                )

    return [functools.partial(task, *chunk) for chunk in chunks(pieces, 32)]


def transmit_tasks(pieces, product, ring, last, masks, turn):
    waves, rows = ring.shape[:2]

    def task(ref, lead, start, row):
        here = pl.ds(row, 32)
        found = [rows_of(ref, lead, start, 32, pl.ds(128 * blk, 128)) for blk in range(2)]
        if turn:
            low = lax.broadcasted_iota(jnp.int32, (32, 128), 1) < 64
            found = [pltpu.roll(value, 64, 1) for value in found]
            phases = [jnp.where(low, last[here], found[0]), jnp.where(low, found[0], found[1])]
        else:
            phases = [last[here], found[0]]
        last[here] = found[1]
        for blk in range(2):
            cosine, sine = cos_sin(phases[blk])
            cosine, sine = cosine * masks[blk], sine * masks[blk]
            to = 256 * (blk + 1)
            for w in range(waves):
                real = product[w, here, 128 * blk : 128 * blk + 128]
                imag = product[w, pl.ds(rows + row, 32), 128 * blk : 128 * blk + 128]
                ring[w, here, to : to + 128] = (real * cosine - imag * sine).astype(jnp.bfloat16)
                ring[w, here, to + 128 : to + 256] = (real * sine + imag * cosine).astype(
                    jnp.bfloat16
                )

    return [functools.partial(task, *chunk) for chunk in chunks(pieces, 32)]


def steps_kernel(waves, rows, col_count, begin, count, resumed, handed, order, owner, *refs):
    up2, up, own, down, down2, ex, ey, mats = refs[:8]
    refs = refs[8:]
    given, refs = (refs[:7], refs[9:]) if resumed else (None, refs)
    exit_wave, focused = refs[:2]
    given_on, refs = (refs[2:9], refs[9:]) if handed else (None, refs[2:])
    ring1, ring2, ring3, waved, last2, last3, turned = carried = refs[:7]
    spread1, spread2, spread3, product2, product3 = refs[7:]
    g = pl.program_id(0) + begin
    rings = carried[:4]

    @pl.when(g == begin)
    def _():
        for i, ref in enumerate(carried):
            if given is None:
                if i < 4:
                    ref[:, :, :256] = jnp.zeros((waves, ref.shape[1], 256), jnp.bfloat16)
                else:
                    ref[...] = jnp.zeros_like(ref)
            elif i < 4:
                ref[:, :, :256] = given[i][...]
            else:
                ref[...] = given[i][...]

    sizes = [ring.shape[1] for ring in rings]
    band2 = mats.at[pl.ds(0, 2 * sizes[1]), pl.ds(0, 2 * sizes[0])]
    at = 2 * sizes[1]
    band3 = mats.at[pl.ds(at, 2 * sizes[2]), pl.ds(0, 2 * sizes[1])]
    at += 2 * sizes[2]
    band4 = mats.at[pl.ds(at, 2 * sizes[3]), pl.ds(0, 2 * sizes[2])]
    at += 2 * sizes[3]
    band = mats.at[pl.ds(at, 512), pl.ds(0, 256)]
    wide_band = mats.at[pl.ds(at, 512), pl.ds(256, 256)]
    first = (
        (up2, None, 0, HALO), (up, None, 0, rows), (own, order[0], 0, rows),
        (down, None, 0, rows), (down2, None, 0, HALO),
    )
    second = ((up, None, rows, rows), (own, order[1], 0, rows), (down, None, rows, rows))
    third = (
        (up, None, 2 * rows, HALO), (own, order[2], 0, rows), (down, None, 2 * rows, HALO)
    )
    masks2 = [lanes_inside(2 * g + blk, 64, col_count) for blk in range(2)]
    masks3 = [lanes_inside(2 * g - 1 + blk, 0, col_count) for blk in range(2)]
    masks4 = [lanes_inside(2 * g - 1 + blk, 64, col_count) for blk in range(2)]
    kept = waved.shape[1]
    low = lax.broadcasted_iota(jnp.int32, (kept, 128), 1) < 64

    def exit_task(w):
        product = dot(band4[...], spread3[w])
        for blk in range(2):
            for part in range(2):
                value = product[kept * part : kept * part + kept, 128 * blk : 128 * blk + 128]
                lane = 256 * (blk + 1) + 128 * part
                waved[w, :, lane : lane + 128] = (value * masks4[blk]).astype(jnp.bfloat16)
                rolled = pltpu.roll(value, 64, 1)
                exit_wave[w, part, :, 128 * blk : 128 * blk + 128] = jnp.where(
                    low, turned[w, part], rolled
                )
                turned[w, part] = rolled

    def focused_store(w, blk, value):
        for part in range(2):
            block = value[:, 128 * part : 128 * part + 128].astype(jnp.bfloat16)
            if len(focused.shape) == 5:
                focused[0, w, part, :, 128 * blk : 128 * blk + 128] = block
            else:
                focused[w, part, :, 128 * blk : 128 * blk + 128] = block

    first_lane = pl.multiple_of(g * STEP, STEP)
    start = start_tasks(first, ex, ey, first_lane, ring1)
    run(start, columns_tasks(ring1, band, spread_store(spread1)))
    run(rows_tasks(product2, band2, spread1))
    run(transmit_tasks(second, product2, ring2, last2, masks2, True))
    run(columns_tasks(ring2, band, spread_store(spread2)))
    run(rows_tasks(product3, band3, spread2))
    run(transmit_tasks(third, product3, ring3, last3, masks3, False))
    run(columns_tasks(ring3, band, spread_store(spread3)))
    run([functools.partial(exit_task, w) for w in range(waves)])
    run(columns_tasks(waved, wide_band, focused_store))

    if handed:

        @pl.when(g == begin + count - 1)
        def _():
            for i, ref in enumerate(carried):
                given_on[i][...] = ref[:, :, :256] if i < 4 else ref[...]


def pick_kernel(halo, edges, order, potential, *refs):
    outs, held, load_sems, sems = refs[:-3], refs[-3], refs[-2], refs[-1]
    rows = potential.shape[1]
    loads = []
    for step in range(3):
        load = pltpu.make_async_copy(potential.at[order[step]], held.at[step], load_sems.at[step])
        load.start()
        loads.append(load)
    for load in loads:
        load.wait()
    copies = []
    for i, (left, right) in enumerate(zip(edges[:-1], edges[1:])):
        lanes = pl.ds(left, right - left)
        up, down, up2, down2 = outs[4 * i : 4 * i + 4]
        high, low = pl.ds(rows - halo, halo), pl.ds(0, halo)
        after = pl.ds(2 * rows, halo)
        pairs = []
        for target, part in ((up, high), (down, low)):
            for step in range(2):
                pairs.append((held.at[step, :, lanes], target.at[pl.ds(rows * step, rows)]))
            pairs.append((held.at[2, part, lanes], target.at[after]))
        pairs += [(held.at[0, high, lanes], up2), (held.at[0, low, lanes], down2)]
        for source, target in pairs:
            copy = pltpu.make_async_copy(source, target, sems.at[len(copies)])
            copy.start()
            copies.append(copy)
    for copy in copies:
        copy.wait()


def toeplitz(row, count, shift):
    wide = jnp.broadcast_to(row, (count, 256))
    return pltpu.roll(wide, shift % 256, 1, stride=1, stride_axis=0)


def inside_rows(first, count, total):
    at = first + lax.broadcasted_iota(jnp.int32, (count, 1), 0)
    return ((at >= 0) & (at < total)).astype(jnp.float32)


def prepare_kernel(
    waves, rows, total_rows, col_count, tilt_index, first_row, tilt_table, fresnel, ctf, mtf,
    mats, wide_rows, row_taps, col_taps, ex, ey, line,
):
    rows3, rows2, rows1 = (rows + 2 * HALO * k for k in (1, 2, 3))
    mats[...] = jnp.zeros_like(mats)
    at = 2 * rows2 + 2 * rows3 + 2 * rows
    band, wide_band = (mats.at[pl.ds(at, 512), pl.ds(256 * i, 256)] for i in range(2))
    band2 = mats.at[pl.ds(0, 2 * rows2), pl.ds(0, 2 * rows1)]
    band3 = mats.at[pl.ds(2 * rows2, 2 * rows3), pl.ds(0, 2 * rows2)]
    band4 = mats.at[pl.ds(2 * rows2 + 2 * rows3, 2 * rows), pl.ds(0, 2 * rows3)]
    line[...] = jnp.zeros_like(line)
    line[0:2, : fresnel.shape[1]] = fresnel[...].astype(jnp.bfloat16).astype(jnp.float32)
    line[2:4, : ctf.shape[1]] = ctf[...].astype(jnp.bfloat16).astype(jnp.float32)
    line[4:5, : mtf.shape[1]] = mtf[...]
    first = first_row[0]

    def columns(target, at, shift):
        for part in range(2):
            made = toeplitz(line[at + part : at + part + 1], 128, shift)
            for k in range(2):
                turned = jnp.transpose(made[:, 128 * k : 128 * k + 128])
                up, down = 256 * k, 256 * k + 128
                if part == 0:
                    target[up:down, :128] = turned.astype(jnp.bfloat16)
                    target[down : down + 128, 128:] = turned.astype(jnp.bfloat16)
                else:
                    target[up:down, 128:] = turned.astype(jnp.bfloat16)
                    target[down : down + 128, :128] = (-turned).astype(jnp.bfloat16)

    columns(band, 0, 65 - (fresnel.shape[1] + 1) // 2)
    columns(wide_band, 2, 65 - (ctf.shape[1] + 1) // 2)
    for target, halo in ((band2, 2 * HALO), (band3, HALO), (band4, 0)):
        count, count_in = target.shape[0] // 2, target.shape[1] // 2
        keep = inside_rows(first - halo, count, total_rows)
        for part in range(2):
            made = toeplitz(line[part : part + 1], count, HALO - (fresnel.shape[1] - 1) // 2) * keep
            made = made[:, :count_in].astype(jnp.bfloat16)
            if part == 0:
                target[:count, :count_in] = made
                target[count:, count_in:] = made
            else:
                target[:count, count_in:] = -made
                target[count:, :count_in] = made
    for part in range(2):
        made = toeplitz(line[2 + part : 3 + part], 128, 65 - (ctf.shape[1] + 1) // 2)
        wide_rows[128 * part : 128 * part + 128] = made.astype(jnp.bfloat16)
    reach = (mtf.shape[1] - 1) // 2
    row_taps[...] = toeplitz(line[4:5], 128, 64 - reach)
    width = col_taps.shape[0]
    off = lax.broadcasted_iota(jnp.int32, (width, 256), 1) - lax.broadcasted_iota(
        jnp.int32, (width, 256), 0
    )
    made = jnp.where(jnp.abs(off) <= reach, toeplitz(line[4:5], width, -reach), 0.0)
    col_taps[...] = made[:, :width]
    count = ex.shape[1]
    at = first - 3 * HALO + lax.broadcasted_iota(jnp.int32, (count, 128), 0)
    keep = ((at >= 0) & (at < total_rows)).astype(jnp.float32)
    at = at.astype(jnp.float32) * (1.0 / total_rows)
    across = lax.broadcasted_iota(jnp.int32, (1, ey.shape[1]), 1)
    keep_cols = (across < col_count).astype(jnp.float32)
    across = across.astype(jnp.float32) * (1.0 / col_count)
    for w in range(waves):
        cosine, sine = cos_sin_turns(at * tilt_table[tilt_index[w], 0])
        ex[2 * w] = cosine * keep
        ex[2 * w + 1] = sine * keep
        cosine, sine = cos_sin_turns(across * tilt_table[tilt_index[w], 1])
        ey[2 * w : 2 * w + 1] = cosine * keep_cols
        ey[2 * w + 1 : 2 * w + 2] = sine * keep_cols


def detector_kernel(waves, tile_wave, taps_band, row_taps, col_taps, out, padded):
    sources, rows, width = tile_wave.shape[0], tile_wave.shape[3], tile_wave.shape[4]
    total = sources * rows
    edge = jnp.zeros((64, width), jnp.float32)
    padded[:64] = edge
    padded[64 + total :] = edge
    for b in range(total // 128):
        image = None
        for w in range(waves):
            parts = []
            for part in range(2):
                window = []
                for k in range(2 * b - 1, 2 * b + 3):
                    if 0 <= k < total // 64:
                        window.append(tile_wave[k, w, part])
                    else:
                        window.append(jnp.zeros((64, width), jnp.bfloat16))
                parts.append(jnp.concatenate(window, axis=0))
            real, imag = dot(taps_band[...], parts[0]), dot(taps_band[...], parts[1])
            re = real[:128] - imag[128:]
            im = imag[:128] + real[128:]
            term = re * re + im * im
            image = term if image is None else image + term
        padded[64 + 128 * b : 192 + 128 * b] = image / waves
    for b in range(total // 128):
        rows_done = jnp.dot(
            row_taps[...],
            padded[128 * b : 128 * b + 256],
            precision=highest,
            preferred_element_type=jnp.float32,
        )
        out[:, 128 * b : 128 * b + 128] = lax.dot_general(
            col_taps[...],
            rows_done,
            (((1,), (1,)), ((), ())),
            precision=highest,
            preferred_element_type=jnp.float32,
        )


def block_windows(values):
    length = values.shape[-1]
    padded = jnp.pad(values, [(0, 0)] * (values.ndim - 1) + [(64, 64)])
    blocks = padded.reshape(values.shape[:-1] + (length // 128 + 1, 128))
    return jnp.concatenate([blocks[..., :-1, :], blocks[..., 1:, :]], axis=-1)


def narrow_tiles(focused, owner, wide_rows, row_taps, col_taps, lane_count):
    waves, _, rows, col_count = focused.shape
    width = col_count // lane_count
    slots = jnp.arange(lane_count, dtype=jnp.int32)
    placing = (owner[None, :] == slots[:, None]).astype(jnp.bfloat16)
    focused = focused.reshape(waves, 2, rows, lane_count, width)
    focused = jnp.einsum("jl,acrlk->jackr", placing, focused, preferred_element_type=jnp.float32)
    sent = focused.astype(jnp.bfloat16)
    tile_wave = lax.all_to_all(sent, "lat", split_axis=0, concat_axis=4, tiled=True)[0]
    windows = block_windows(tile_wave)
    taps_band = wide_rows.reshape(2, 128, 256)
    made = jnp.einsum("acwbi,doi->acdwbo", windows, taps_band, preferred_element_type=jnp.float32)
    real = made[:, 0, 0] - made[:, 1, 1]
    imag = made[:, 1, 0] + made[:, 0, 1]
    image = jnp.sum(real * real + imag * imag, axis=0) / waves
    image = image.reshape(width, lane_count * rows)
    blurred = jnp.einsum("wbi,oi->wbo", block_windows(image), row_taps, precision=highest)
    return jnp.dot(col_taps, blurred.reshape(width, lane_count * rows), precision=highest)


def local(potential, tilt_index, slice_order, tilt_table, fresnel_taps, ctf_taps, mtf_taps, owner):
    row_count, col_count = potential.shape[1:]
    lane_count = lax.axis_size("lat")
    total_rows = row_count * lane_count
    tile_cols = col_count // lane_count
    waves = tilt_index.shape[0]
    first_row = lax.axis_index("lat") * row_count
    steps = col_count // STEP

    def neighbour(value, offset):
        pairs = [(i, i + offset) for i in range(lane_count) if 0 <= i + offset < lane_count]
        return lax.ppermute(value, "lat", pairs)

    rows1, rows2, rows3 = (row_count + 2 * HALO * k for k in (3, 2, 1))
    anywhere = pl.BlockSpec(memory_space=pl.ANY)
    in_vmem = pl.BlockSpec(memory_space=pltpu.VMEM)
    in_smem = pl.BlockSpec(memory_space=pltpu.SMEM)
    widths = [steps // 2, steps - steps // 2]
    edges = [STEP * sum(widths[:i]) for i in range(len(widths) + 1)]
    sent_rows = (2 * row_count + HALO, 2 * row_count + HALO, HALO, HALO)
    picked = pl.pallas_call(
        functools.partial(pick_kernel, HALO, edges),
        name="pick_rows",
        out_shape=[
            jax.ShapeDtypeStruct((rows, STEP * width), potential.dtype)
            for width in widths
            for rows in sent_rows
        ],
        in_specs=[in_smem, anywhere],
        out_specs=[anywhere] * (4 * len(widths)),
        scratch_shapes=[
            pltpu.VMEM((3, row_count, col_count), potential.dtype),
            pltpu.SemaphoreType.DMA((3,)),
            pltpu.SemaphoreType.DMA((8 * len(widths),)),
        ],
        cost_estimate=pl.CostEstimate(flops=0, bytes_accessed=4 << 20, transcendentals=0),
    )(slice_order, potential)
    halos = [
        [neighbour(value, offset) for value, offset in zip(picked[4 * i : 4 * i + 4], (1, -1, 2, -2))]
        for i in range(len(widths))
    ]

    mats_shape = (2 * rows2 + 2 * rows3 + 2 * row_count + 512, 2 * rows1)

    def made(shape, dtype):
        return jax.ShapeDtypeStruct(shape, dtype)

    mats, wide_rows, row_taps, col_taps, ex, ey = pl.pallas_call(
        functools.partial(prepare_kernel, waves, row_count, total_rows, col_count),
        name="prepare",
        out_shape=[
            made(mats_shape, jnp.bfloat16),
            made((256, 256), jnp.bfloat16),
            made((128, 256), jnp.float32),
            made((tile_cols, tile_cols), jnp.float32),
            made((2 * waves, rows1, 128), jnp.float32),
            made((2 * waves, col_count + STEP), jnp.float32),
        ],
        in_specs=[in_smem] * 3 + [in_vmem] * 3,
        out_specs=[in_vmem] * 6,
        scratch_shapes=[pltpu.VMEM((8, 256), jnp.float32)],
        cost_estimate=pl.CostEstimate(flops=1 << 31, bytes_accessed=2 << 20, transcendentals=0),
    )(tilt_index, first_row[None], tilt_table, fresnel_taps, ctf_taps, mtf_taps[None])

    def clamp(g):
        return jnp.clip(g, 0, steps - 1)

    def fixed(*shape):
        return pl.BlockSpec(shape, lambda g, *_: (0,) * len(shape))

    placed = tile_cols == STEP
    if placed:
        focused_shape = (lane_count, waves, 2, row_count, tile_cols)
    else:
        focused_shape = (waves, 2, row_count, col_count)
    carried = [((waves, rows, 256), jnp.bfloat16) for rows in (rows1, rows2, rows3, row_count)]
    carried += [
        ((rows2, 128), jnp.float32),
        ((rows3, 128), jnp.float32),
        ((waves, 2, row_count, 128), jnp.float32),
    ]

    def ring(rows, lanes, dtype=jnp.bfloat16):
        return pltpu.VMEM((waves, rows, lanes), dtype)

    outputs = [
        made((waves, 2, row_count, col_count), jnp.float32),
        made(focused_shape, jnp.bfloat16),
    ]
    given = None
    for i, width in enumerate(widths):
        begin, last_call = edges[i] // STEP, i + 1 == len(widths)
        count = width + 1 if last_call else width

        def piece(rows, width=width):
            return pl.BlockSpec((rows, STEP), lambda g, *_: (0, jnp.minimum(g, width - 1)))

        def done(g, begin=begin):
            return clamp(g + begin - 1)

        if placed:
            focused_spec = pl.BlockSpec(
                (1, waves, 2, row_count, tile_cols),
                lambda g, order, owner, done=done: (owner[done(g)], 0, 0, 0, 0),
            )
        else:
            focused_spec = pl.BlockSpec(
                (waves, 2, row_count, STEP), lambda g, *_, done=done: (0, 0, 0, done(g))
            )
        up, down, up2, down2 = halos[i]
        args = [slice_order, owner, up2, up, potential, down, down2, ex, ey, mats]
        in_specs = [
            piece(HALO),
            piece(2 * row_count + HALO),
            pl.BlockSpec(
                (potential.shape[0], row_count, STEP),
                lambda g, *_, begin=begin: (0, 0, clamp(g + begin)),
            ),
            piece(2 * row_count + HALO),
            piece(HALO),
            fixed(*ex.shape),
            fixed(*ey.shape),
            fixed(*mats.shape),
        ]
        aliases = {}
        if given is not None:
            args += given
            in_specs += [fixed(*shape) for shape, _ in carried] + [anywhere, anywhere]
            aliases = {len(args) - 2: 0, len(args) - 1: 1}
        out_shape = list(outputs)
        out_specs = [
            pl.BlockSpec((waves, 2, row_count, STEP), lambda g, *_, done=done: (0, 0, 0, done(g))),
            focused_spec,
        ]
        if not last_call:
            out_shape += [made(shape, dtype) for shape, dtype in carried]
            out_specs += [fixed(*shape) for shape, _ in carried]
        results = pl.pallas_call(
            functools.partial(
                steps_kernel, waves, row_count, col_count, begin, count, given is not None, not last_call
            ),
            name="steps",
            out_shape=out_shape,
            grid_spec=pltpu.PrefetchScalarGridSpec(
                num_scalar_prefetch=2,
                grid=(count,),
                in_specs=in_specs,
                out_specs=out_specs,
                scratch_shapes=[ring(rows, 768) for rows in (rows1, rows2, rows3, row_count)]
                + [pltpu.VMEM(shape, dtype) for shape, dtype in carried[4:]]
                + [ring(2 * rows, 256) for rows in (rows1, rows2, rows3)]
                + [ring(2 * rows, 256, jnp.float32) for rows in (rows2, rows3)],
            ),
            input_output_aliases=aliases,
            compiler_params=pltpu.CompilerParams(
                dimension_semantics=("arbitrary",), vmem_limit_bytes=24 * 1024 * 1024
            ),
            cost_estimate=pl.CostEstimate(
                flops=count * (1 << 30), bytes_accessed=count << 19, transcendentals=0
            ),
        )(*args)
        given = list(results[2:]) + list(results[:2])
    exit_wave, focused = results[:2]

    if not placed:
        detector = narrow_tiles(focused, owner, wide_rows, row_taps, col_taps, lane_count)
        return exit_wave, detector[None]

    tile_wave = lax.all_to_all(focused, "lat", split_axis=0, concat_axis=0, tiled=True)
    detector = pl.pallas_call(
        functools.partial(detector_kernel, waves),
        name="detector",
        out_shape=jax.ShapeDtypeStruct((tile_cols, total_rows), jnp.float32),
        in_specs=[pl.BlockSpec(memory_space=pltpu.VMEM)] * 4,
        out_specs=pl.BlockSpec(memory_space=pltpu.VMEM),
        scratch_shapes=[pltpu.VMEM((total_rows + 128, tile_cols), jnp.float32)],
        compiler_params=pltpu.CompilerParams(vmem_limit_bytes=48 * 1024 * 1024),
        cost_estimate=pl.CostEstimate(
            flops=1 << 33, bytes_accessed=4 << 20, transcendentals=0
        ),
    )(tile_wave, wide_rows, row_taps, col_taps)
    return exit_wave, detector[None]


def solution(mesh):
    placed = (
        P(None, ("lamella", "lat"), None),
        P("lamella"),
        P("lamella"),
        P(),
        P(),
        P(),
        P(),
        P("lamella"),
    )
    return jax.shard_map(
        local,
        mesh=mesh,
        in_specs=placed,
        out_specs=(P(None, None, ("lamella", "lat"), None), P(("lamella", "lat"), None, None)),
        check_vma=False,
    )
```

```python
import functools
import math

import jax
import jax.numpy as jnp
from jax import lax
from jax.experimental import pallas as pl
from jax.experimental.pallas import tpu as pltpu
from jax.sharding import PartitionSpec as P

highest = lax.Precision.HIGHEST
SIN_TURN = (
    6.2831854820251465,
    -41.34170150756836,
    81.60513305664062,
    -76.70301818847656,
    42.02592849731445,
    -14.899847030639648,
    3.2381374835968018,
)
COS_TURN = (
    1.0,
    -19.73920440673828,
    64.93911743164062,
    -85.45014190673828,
    60.16762924194336,
    -25.967599868774414,
    6.528658390045166,
)
SIN_QUARTER = (
    0.4204482138156891,
    -0.004379667341709137,
    1.3686111742572393e-05,
    -2.0339173900651986e-08,
    1.679661791598175e-11,
)
COS_QUARTER = (
    1.6817927360534668,
    -0.052555955946445465,
    0.00027371387113817036,
    -5.690624220733298e-07,
    5.977824346636851e-10,
)
HALO = 32
STEP = 256


def horner(coefs, z):
    total = coefs[-1] * z + coefs[-2]
    for coef in coefs[-3::-1]:
        total = total * z + coef
    return total


def cos_sin_turns(turns):
    rest = turns - jnp.round(turns)
    z = rest * rest
    return horner(COS_TURN, z), horner(SIN_TURN, z) * rest


def cos_sin(phase):
    z = phase * phase
    quarter_sin = horner(SIN_QUARTER, z) * phase
    half_sin = quarter_sin * horner(COS_QUARTER, z)
    half_cos = math.sqrt(2.0) - quarter_sin * quarter_sin
    return 1.0 - half_sin * half_sin, half_sin * half_cos


def dot(a, b):
    return jnp.dot(a, b, preferred_element_type=jnp.float32)


def lanes_inside(block, shift, col_count):
    cols = block * 128 - shift + lax.broadcasted_iota(jnp.int32, (1, 128), 1)
    return ((cols >= 0) & (cols < col_count)).astype(jnp.float32)


def rows_of(ref, lead, start, count, lanes):
    if lead is None:
        found = ref[pl.ds(start, count), lanes]
    else:
        found = ref[lead, pl.ds(start, count), lanes]
    return found.astype(jnp.float32)


def chunks(pieces, size):
    row = 0
    for ref, lead, first, rows in pieces:
        for start in range(0, rows, size):
            yield ref, lead, first + start, row
            row += size


def columns_tasks(ring, band, store):
    waves = ring.shape[0]

    def task(w, blk):
        store(w, blk, dot(ring[w, :, 256 * blk : 256 * blk + 512], band[...]))
        if blk == 1:
            ring[w, :, :256] = ring[w, :, 512:768]

    return [functools.partial(task, w, blk) for w in range(waves) for blk in range(2)]


def spread_store(spread):
    rows = spread.shape[1] // 2

    def store(w, blk, value):
        lanes = pl.ds(128 * blk, 128)
        spread[w, :rows, lanes] = value[:, :128].astype(jnp.bfloat16)
        spread[w, rows:, lanes] = value[:, 128:].astype(jnp.bfloat16)

    return store


def rows_tasks(product, rows_band, spread):
    def task(w):
        product[w] = dot(rows_band[...], spread[w])

    return [functools.partial(task, w) for w in range(spread.shape[0])]


def run(*lists):
    for tasks in lists:
        for task in tasks:
            task()


def start_tasks(pieces, ex, ey, first_lane, first_wave, ring):
    waves = ring.shape[0]

    def task(ref, lead, start, row):
        for blk in range(2):
            lanes = pl.ds(128 * blk, 128)
            cosine, sine = cos_sin(rows_of(ref, lead, start, 32, lanes))
            to = 256 * (blk + 1)
            for w in range(waves):
                at = pl.ds(first_lane + 128 * blk, 128)
                v = 2 * (w + first_wave)
                yr, yi = ey[v : v + 1, at], ey[v + 1 : v + 2, at]
                ur, ui = cosine * yr - sine * yi, cosine * yi + sine * yr
                xr, xi = ex[v, pl.ds(row, 32)], ex[v + 1, pl.ds(row, 32)]
                ring[w, pl.ds(row, 32), to : to + 128] = (ur * xr - ui * xi).astype(jnp.bfloat16)
                ring[w, pl.ds(row, 32), to + 128 : to + 256] = (ur * xi + ui * xr).astype(
                    jnp.bfloat16
                )

    return [functools.partial(task, *chunk) for chunk in chunks(pieces, 32)]


def transmit_tasks(pieces, product, ring, last, masks, turn):
    waves, rows = ring.shape[:2]

    def task(ref, lead, start, row):
        here = pl.ds(row, 32)
        found = [rows_of(ref, lead, start, 32, pl.ds(128 * blk, 128)) for blk in range(2)]
        if turn:
            low = lax.broadcasted_iota(jnp.int32, (32, 128), 1) < 64
            found = [pltpu.roll(value, 64, 1) for value in found]
            phases = [jnp.where(low, last[here], found[0]), jnp.where(low, found[0], found[1])]
        else:
            phases = [last[here], found[0]]
        last[here] = found[1]
        for blk in range(2):
            cosine, sine = cos_sin(phases[blk])
            cosine, sine = cosine * masks[blk], sine * masks[blk]
            to = 256 * (blk + 1)
            for w in range(waves):
                real = product[w, here, 128 * blk : 128 * blk + 128]
                imag = product[w, pl.ds(rows + row, 32), 128 * blk : 128 * blk + 128]
                ring[w, here, to : to + 128] = (real * cosine - imag * sine).astype(jnp.bfloat16)
                ring[w, here, to + 128 : to + 256] = (real * sine + imag * cosine).astype(
                    jnp.bfloat16
                )

    return [functools.partial(task, *chunk) for chunk in chunks(pieces, 32)]


def steps_kernel(
    waves, first_wave, rows, col_count, begin, count, kept_outputs, resumed, handed, order, owner, *refs
):
    up2, up, own, down, down2, ex, ey, mats = refs[:8]
    refs = refs[8:]
    given, refs = (refs[:7], refs[7:]) if resumed else (None, refs)
    refs = refs[kept_outputs:]
    exit_wave, focused = refs[:2]
    given_on, refs = (refs[2:9], refs[9:]) if handed else (None, refs[2:])
    ring1, ring2, ring3, waved, last2, last3, turned = carried = refs[:7]
    spread1, spread2, spread3, product2, product3 = refs[7:]
    g = pl.program_id(0) + begin
    rings = carried[:4]

    @pl.when(g == begin)
    def _():
        for i, ref in enumerate(carried):
            if given is None:
                if i < 4:
                    ref[:, :, :256] = jnp.zeros((waves, ref.shape[1], 256), jnp.bfloat16)
                else:
                    ref[...] = jnp.zeros_like(ref)
            elif i < 4:
                ref[:, :, :256] = given[i][...]
            else:
                ref[...] = given[i][...]

    sizes = [ring.shape[1] for ring in rings]
    band2 = mats.at[pl.ds(0, 2 * sizes[1]), pl.ds(0, 2 * sizes[0])]
    at = 2 * sizes[1]
    band3 = mats.at[pl.ds(at, 2 * sizes[2]), pl.ds(0, 2 * sizes[1])]
    at += 2 * sizes[2]
    band4 = mats.at[pl.ds(at, 2 * sizes[3]), pl.ds(0, 2 * sizes[2])]
    at += 2 * sizes[3]
    band = mats.at[pl.ds(at, 512), pl.ds(0, 256)]
    wide_band = mats.at[pl.ds(at, 512), pl.ds(256, 256)]
    first = (
        (up2, None, 0, HALO), (up, None, 0, rows), (own, order[0], 0, rows),
        (down, None, 0, rows), (down2, None, 0, HALO),
    )
    second = ((up, None, rows, rows), (own, order[1], 0, rows), (down, None, rows, rows))
    third = (
        (up, None, 2 * rows, HALO), (own, order[2], 0, rows), (down, None, 2 * rows, HALO)
    )
    masks2 = [lanes_inside(2 * g + blk, 64, col_count) for blk in range(2)]
    masks3 = [lanes_inside(2 * g - 1 + blk, 0, col_count) for blk in range(2)]
    masks4 = [lanes_inside(2 * g - 1 + blk, 64, col_count) for blk in range(2)]
    kept = waved.shape[1]
    low = lax.broadcasted_iota(jnp.int32, (kept, 128), 1) < 64

    def exit_task(w):
        product = dot(band4[...], spread3[w])
        for blk in range(2):
            for part in range(2):
                value = product[kept * part : kept * part + kept, 128 * blk : 128 * blk + 128]
                lane = 256 * (blk + 1) + 128 * part
                waved[w, :, lane : lane + 128] = (value * masks4[blk]).astype(jnp.bfloat16)
                rolled = pltpu.roll(value, 64, 1)
                exit_wave[w, part, :, 128 * blk : 128 * blk + 128] = jnp.where(
                    low, turned[w, part], rolled
                )
                turned[w, part] = rolled

    def focused_store(w, blk, value):
        for part in range(2):
            block = value[:, 128 * part : 128 * part + 128].astype(jnp.bfloat16)
            if len(focused.shape) == 5:
                focused[0, w, part, :, 128 * blk : 128 * blk + 128] = block
            else:
                focused[w, part, :, 128 * blk : 128 * blk + 128] = block

    first_lane = pl.multiple_of(g * STEP, STEP)
    start = start_tasks(first, ex, ey, first_lane, first_wave, ring1)
    run(start, columns_tasks(ring1, band, spread_store(spread1)))
    run(rows_tasks(product2, band2, spread1))
    run(transmit_tasks(second, product2, ring2, last2, masks2, True))
    run(columns_tasks(ring2, band, spread_store(spread2)))
    run(rows_tasks(product3, band3, spread2))
    run(transmit_tasks(third, product3, ring3, last3, masks3, False))
    run(columns_tasks(ring3, band, spread_store(spread3)))
    run([functools.partial(exit_task, w) for w in range(waves)])
    run(columns_tasks(waved, wide_band, focused_store))

    if handed:

        @pl.when(g == begin + count - 1)
        def _():
            for i, ref in enumerate(carried):
                given_on[i][...] = ref[:, :, :256] if i < 4 else ref[...]


def pick_kernel(halo, edges, order, potential, *refs):
    outs, held, load_sems, sems = refs[:-3], refs[-3], refs[-2], refs[-1]
    rows = potential.shape[1]
    loads = []
    for step in range(3):
        load = pltpu.make_async_copy(potential.at[order[step]], held.at[step], load_sems.at[step])
        load.start()
        loads.append(load)
    for load in loads:
        load.wait()
    high, low = pl.ds(rows - halo, halo), pl.ds(0, halo)
    pairs = [(held.at[0, high], outs[0]), (held.at[0, low], outs[1])]
    for i, (left, right) in enumerate(zip(edges[:-1], edges[1:])):
        lanes = pl.ds(left, right - left)
        for target, part in ((outs[2 + 2 * i], high), (outs[3 + 2 * i], low)):
            for step in range(2):
                pairs.append((held.at[step, :, lanes], target.at[pl.ds(rows * step, rows)]))
            pairs.append((held.at[2, part, lanes], target.at[pl.ds(2 * rows, halo)]))
    copies = []
    for source, target in pairs:
        copy = pltpu.make_async_copy(source, target, sems.at[len(copies)])
        copy.start()
        copies.append(copy)
    for copy in copies:
        copy.wait()


def toeplitz(row, count, shift):
    wide = jnp.broadcast_to(row, (count, 256))
    return pltpu.roll(wide, shift % 256, 1, stride=1, stride_axis=0)


def inside_rows(first, count, total):
    at = first + lax.broadcasted_iota(jnp.int32, (count, 1), 0)
    return ((at >= 0) & (at < total)).astype(jnp.float32)


def prepare_kernel(
    waves, rows, total_rows, col_count, tilt_index, first_row, tilt_table, fresnel, ctf, mtf,
    mats, wide_rows, row_taps, col_taps, ex, ey, line,
):
    rows3, rows2, rows1 = (rows + 2 * HALO * k for k in (1, 2, 3))
    mats[...] = jnp.zeros_like(mats)
    at = 2 * rows2 + 2 * rows3 + 2 * rows
    band, wide_band = (mats.at[pl.ds(at, 512), pl.ds(256 * i, 256)] for i in range(2))
    band2 = mats.at[pl.ds(0, 2 * rows2), pl.ds(0, 2 * rows1)]
    band3 = mats.at[pl.ds(2 * rows2, 2 * rows3), pl.ds(0, 2 * rows2)]
    band4 = mats.at[pl.ds(2 * rows2 + 2 * rows3, 2 * rows), pl.ds(0, 2 * rows3)]
    line[...] = jnp.zeros_like(line)
    line[0:2, : fresnel.shape[1]] = fresnel[...].astype(jnp.bfloat16).astype(jnp.float32)
    line[2:4, : ctf.shape[1]] = ctf[...].astype(jnp.bfloat16).astype(jnp.float32)
    line[4:5, : mtf.shape[1]] = mtf[...]
    first = first_row[0]

    def columns(target, at, shift):
        for part in range(2):
            made = toeplitz(line[at + part : at + part + 1], 128, shift)
            for k in range(2):
                turned = jnp.transpose(made[:, 128 * k : 128 * k + 128])
                up, down = 256 * k, 256 * k + 128
                if part == 0:
                    target[up:down, :128] = turned.astype(jnp.bfloat16)
                    target[down : down + 128, 128:] = turned.astype(jnp.bfloat16)
                else:
                    target[up:down, 128:] = turned.astype(jnp.bfloat16)
                    target[down : down + 128, :128] = (-turned).astype(jnp.bfloat16)

    columns(band, 0, 65 - (fresnel.shape[1] + 1) // 2)
    columns(wide_band, 2, 65 - (ctf.shape[1] + 1) // 2)
    for target, halo in ((band2, 2 * HALO), (band3, HALO), (band4, 0)):
        count, count_in = target.shape[0] // 2, target.shape[1] // 2
        keep = inside_rows(first - halo, count, total_rows)
        for part in range(2):
            made = toeplitz(line[part : part + 1], count, HALO - (fresnel.shape[1] - 1) // 2) * keep
            made = made[:, :count_in].astype(jnp.bfloat16)
            if part == 0:
                target[:count, :count_in] = made
                target[count:, count_in:] = made
            else:
                target[:count, count_in:] = -made
                target[count:, :count_in] = made
    for part in range(2):
        made = toeplitz(line[2 + part : 3 + part], 128, 65 - (ctf.shape[1] + 1) // 2)
        wide_rows[128 * part : 128 * part + 128] = made.astype(jnp.bfloat16)
    reach = (mtf.shape[1] - 1) // 2
    row_taps[...] = toeplitz(line[4:5], 128, 64 - reach)
    width = col_taps.shape[0]
    off = lax.broadcasted_iota(jnp.int32, (width, 256), 1) - lax.broadcasted_iota(
        jnp.int32, (width, 256), 0
    )
    made = jnp.where(jnp.abs(off) <= reach, toeplitz(line[4:5], width, -reach), 0.0)
    col_taps[...] = made[:, :width]
    count = ex.shape[1]
    at = first - 3 * HALO + lax.broadcasted_iota(jnp.int32, (count, 128), 0)
    keep = ((at >= 0) & (at < total_rows)).astype(jnp.float32)
    at = at.astype(jnp.float32) * (1.0 / total_rows)
    across = lax.broadcasted_iota(jnp.int32, (1, ey.shape[1]), 1)
    keep_cols = (across < col_count).astype(jnp.float32)
    across = across.astype(jnp.float32) * (1.0 / col_count)
    for w in range(waves):
        cosine, sine = cos_sin_turns(at * tilt_table[tilt_index[w], 0])
        ex[2 * w] = cosine * keep
        ex[2 * w + 1] = sine * keep
        cosine, sine = cos_sin_turns(across * tilt_table[tilt_index[w], 1])
        ey[2 * w : 2 * w + 1] = cosine * keep_cols
        ey[2 * w + 1 : 2 * w + 2] = sine * keep_cols


def add_intensity(tile_wave, taps_band, store):
    total = tile_wave.shape[0] * tile_wave.shape[3]
    for b in range(total // 128):
        parts = []
        for part in range(2):
            window = []
            for k in range(2 * b - 1, 2 * b + 3):
                if 0 <= k < total // 64:
                    window.append(tile_wave[k, 0, part])
                else:
                    window.append(jnp.zeros((64, tile_wave.shape[4]), jnp.bfloat16))
            parts.append(jnp.concatenate(window, axis=0))
        real, imag = dot(taps_band[...], parts[0]), dot(taps_band[...], parts[1])
        re = real[:128] - imag[128:]
        im = imag[:128] + real[128:]
        store(b, re * re + im * im)


def intensity_kernel(tile_wave, before, taps_band, out):
    def store(b, value):
        at = pl.ds(128 * b, 128)
        out[at] = value if before is None else before[at] + value

    add_intensity(tile_wave, taps_band, store)


def detector_kernel(waves, tile_wave, before, taps_band, row_taps, col_taps, out, padded):
    total, width = before.shape
    edge = jnp.zeros((64, width), jnp.float32)
    padded[:64] = edge
    padded[64 + total :] = edge

    def store(b, value):
        at = pl.ds(128 * b, 128)
        padded[64 + 128 * b : 192 + 128 * b] = (before[at] + value) / waves

    add_intensity(tile_wave, taps_band, store)
    for b in range(total // 128):
        rows_done = jnp.dot(
            row_taps[...],
            padded[128 * b : 128 * b + 256],
            precision=highest,
            preferred_element_type=jnp.float32,
        )
        out[:, 128 * b : 128 * b + 128] = lax.dot_general(
            col_taps[...],
            rows_done,
            (((1,), (1,)), ((), ())),
            precision=highest,
            preferred_element_type=jnp.float32,
        )


def block_windows(values):
    length = values.shape[-1]
    padded = jnp.pad(values, [(0, 0)] * (values.ndim - 1) + [(64, 64)])
    blocks = padded.reshape(values.shape[:-1] + (length // 128 + 1, 128))
    return jnp.concatenate([blocks[..., :-1, :], blocks[..., 1:, :]], axis=-1)


def narrow_tiles(focused, owner, wide_rows, row_taps, col_taps, lane_count):
    waves, _, rows, col_count = focused.shape
    width = col_count // lane_count
    slots = jnp.arange(lane_count, dtype=jnp.int32)
    placing = (owner[None, :] == slots[:, None]).astype(jnp.bfloat16)
    focused = focused.reshape(waves, 2, rows, lane_count, width)
    focused = jnp.einsum("jl,acrlk->jackr", placing, focused, preferred_element_type=jnp.float32)
    sent = focused.astype(jnp.bfloat16)
    tile_wave = lax.all_to_all(sent, "lat", split_axis=0, concat_axis=4, tiled=True)[0]
    windows = block_windows(tile_wave)
    taps_band = wide_rows.reshape(2, 128, 256)
    made = jnp.einsum("acwbi,doi->acdwbo", windows, taps_band, preferred_element_type=jnp.float32)
    real = made[:, 0, 0] - made[:, 1, 1]
    imag = made[:, 1, 0] + made[:, 0, 1]
    image = jnp.sum(real * real + imag * imag, axis=0) / waves
    image = image.reshape(width, lane_count * rows)
    blurred = jnp.einsum("wbi,oi->wbo", block_windows(image), row_taps, precision=highest)
    return jnp.dot(col_taps, blurred.reshape(width, lane_count * rows), precision=highest)


def local(potential, tilt_index, slice_order, tilt_table, fresnel_taps, ctf_taps, mtf_taps, owner):
    row_count, col_count = potential.shape[1:]
    lane_count = lax.axis_size("lat")
    total_rows = row_count * lane_count
    tile_cols = col_count // lane_count
    waves = tilt_index.shape[0]
    first_row = lax.axis_index("lat") * row_count
    steps = col_count // STEP

    def neighbour(value, offset):
        pairs = [(i, i + offset) for i in range(lane_count) if 0 <= i + offset < lane_count]
        return lax.ppermute(value, "lat", pairs)

    rows1, rows2, rows3 = (row_count + 2 * HALO * k for k in (3, 2, 1))
    anywhere = pl.BlockSpec(memory_space=pl.ANY)
    in_vmem = pl.BlockSpec(memory_space=pltpu.VMEM)
    in_smem = pl.BlockSpec(memory_space=pltpu.SMEM)
    widths = [steps // 2, steps - steps // 2]
    edges = [STEP * sum(widths[:i]) for i in range(len(widths) + 1)]
    sent_rows = 2 * row_count + HALO
    picked = pl.pallas_call(
        functools.partial(pick_kernel, HALO, edges),
        name="pick_rows",
        out_shape=[jax.ShapeDtypeStruct((HALO, col_count), potential.dtype)] * 2
        + [
            jax.ShapeDtypeStruct((sent_rows, STEP * width), potential.dtype)
            for width in widths
            for _ in range(2)
        ],
        in_specs=[in_smem, anywhere],
        out_specs=[anywhere] * (2 + 2 * len(widths)),
        scratch_shapes=[
            pltpu.VMEM((3, row_count, col_count), potential.dtype),
            pltpu.SemaphoreType.DMA((3,)),
            pltpu.SemaphoreType.DMA((2 + 6 * len(widths),)),
        ],
        cost_estimate=pl.CostEstimate(flops=0, bytes_accessed=4 << 20, transcendentals=0),
    )(slice_order, potential)
    up2, down2 = neighbour(picked[0], 2), neighbour(picked[1], -2)
    halos = [
        (neighbour(picked[2 + 2 * i], 1), neighbour(picked[3 + 2 * i], -1))
        for i in range(len(widths))
    ]

    mats_shape = (2 * rows2 + 2 * rows3 + 2 * row_count + 512, 2 * rows1)

    def made(shape, dtype):
        return jax.ShapeDtypeStruct(shape, dtype)

    mats, wide_rows, row_taps, col_taps, ex, ey = pl.pallas_call(
        functools.partial(prepare_kernel, waves, row_count, total_rows, col_count),
        name="prepare",
        out_shape=[
            made(mats_shape, jnp.bfloat16),
            made((256, 256), jnp.bfloat16),
            made((128, 256), jnp.float32),
            made((tile_cols, tile_cols), jnp.float32),
            made((2 * waves, rows1, 128), jnp.float32),
            made((2 * waves, col_count + STEP), jnp.float32),
        ],
        in_specs=[in_smem] * 3 + [in_vmem] * 3,
        out_specs=[in_vmem] * 6,
        scratch_shapes=[pltpu.VMEM((8, 256), jnp.float32)],
        cost_estimate=pl.CostEstimate(flops=1 << 31, bytes_accessed=2 << 20, transcendentals=0),
    )(tilt_index, first_row[None], tilt_table, fresnel_taps, ctf_taps, mtf_taps[None])

    def clamp(g):
        return jnp.clip(g, 0, steps - 1)

    def fixed(*shape):
        return pl.BlockSpec(shape, lambda g, *_: (0,) * len(shape))

    placed = tile_cols == STEP
    if placed:
        focused_shape = (lane_count, 1, 2, row_count, tile_cols)
    else:
        focused_shape = (1, 2, row_count, col_count)
    carried = [((1, rows, 256), jnp.bfloat16) for rows in (rows1, rows2, rows3, row_count)]
    carried += [
        ((rows2, 128), jnp.float32),
        ((rows3, 128), jnp.float32),
        ((1, 2, row_count, 128), jnp.float32),
    ]

    def ring(rows, lanes, dtype=jnp.bfloat16):
        return pltpu.VMEM((1, rows, lanes), dtype)

    outputs = [
        made((waves, 2, row_count, col_count), jnp.float32),
        made(focused_shape, jnp.bfloat16),
    ]
    exit_wave, focused = None, [None] * waves
    for first_wave in range(waves):
        given = []
        for i, width in enumerate(widths):
            begin, last_call = edges[i] // STEP, i + 1 == len(widths)
            count = width + 1 if last_call else width

            def piece(width=width):
                return pl.BlockSpec((sent_rows, STEP), lambda g, *_: (0, jnp.minimum(g, width - 1)))

            def far(begin=begin):
                return pl.BlockSpec((HALO, STEP), lambda g, *_: (0, clamp(g + begin)))

            def done(g, begin=begin):
                return clamp(g + begin - 1)

            up, down = halos[i]
            args = [slice_order, owner, up2, up, potential, down, down2, ex, ey, mats]
            in_specs = [
                far(),
                piece(),
                pl.BlockSpec(
                    (potential.shape[0], row_count, STEP),
                    lambda g, *_, begin=begin: (0, 0, clamp(g + begin)),
                ),
                piece(),
                far(),
                fixed(*ex.shape),
                fixed(*ey.shape),
                fixed(*mats.shape),
            ]
            args += given
            in_specs += [fixed(*shape) for shape, _ in carried[: len(given)]]
            aliases = {}
            for at, kept in enumerate((exit_wave, focused[first_wave])):
                if kept is not None:
                    aliases[len(args)] = at
                    args.append(kept)
                    in_specs.append(anywhere)
            if placed:
                focused_spec = pl.BlockSpec(
                    (1, 1, 2, row_count, tile_cols),
                    lambda g, order, owner, done=done: (owner[done(g)], 0, 0, 0, 0),
                )
            else:
                focused_spec = pl.BlockSpec(
                    (1, 2, row_count, STEP), lambda g, *_, done=done: (0, 0, 0, done(g))
                )
            out_shape = list(outputs)
            out_specs = [
                pl.BlockSpec(
                    (1, 2, row_count, STEP),
                    lambda g, *_, done=done, first_wave=first_wave: (first_wave, 0, 0, done(g)),
                ),
                focused_spec,
            ]
            if not last_call:
                out_shape += [made(shape, dtype) for shape, dtype in carried]
                out_specs += [fixed(*shape) for shape, _ in carried]
            exit_wave, focused[first_wave], *given = pl.pallas_call(
                functools.partial(
                    steps_kernel, 1, first_wave, row_count, col_count, begin, count,
                    len(aliases), i > 0, not last_call,
                ),
                name="steps",
                out_shape=out_shape,
                grid_spec=pltpu.PrefetchScalarGridSpec(
                    num_scalar_prefetch=2,
                    grid=(count,),
                    in_specs=in_specs,
                    out_specs=out_specs,
                    scratch_shapes=[ring(rows, 768) for rows in (rows1, rows2, rows3, row_count)]
                    + [pltpu.VMEM(shape, dtype) for shape, dtype in carried[4:]]
                    + [ring(2 * rows, 256) for rows in (rows1, rows2, rows3)]
                    + [ring(2 * rows, 256, jnp.float32) for rows in (rows2, rows3)],
                ),
                input_output_aliases=aliases,
                compiler_params=pltpu.CompilerParams(
                    dimension_semantics=("arbitrary",), vmem_limit_bytes=20 * 1024 * 1024
                ),
                cost_estimate=pl.CostEstimate(
                    flops=count * (1 << 29), bytes_accessed=count << 19, transcendentals=0
                ),
            )(*args)

    if not placed:
        joined = jnp.concatenate(focused, axis=0)
        detector = narrow_tiles(joined, owner, wide_rows, row_taps, col_taps, lane_count)
        return exit_wave, detector[None]

    tile_waves = [
        lax.all_to_all(value, "lat", split_axis=0, concat_axis=0, tiled=True) for value in focused
    ]
    image = jnp.zeros((total_rows, tile_cols), jnp.float32) if waves == 1 else None
    for tile_wave in tile_waves[:-1]:
        before = [] if image is None else [image]

        def kernel(*refs, alone=image is None):
            tile_ref, band_ref, out_ref = refs[0], refs[-2], refs[-1]
            intensity_kernel(tile_ref, None if alone else refs[1], band_ref, out_ref)

        image = pl.pallas_call(
            kernel,
            name="intensity",
            out_shape=made((total_rows, tile_cols), jnp.float32),
            in_specs=[in_vmem] * (2 + len(before)),
            out_specs=in_vmem,
            compiler_params=pltpu.CompilerParams(vmem_limit_bytes=20 * 1024 * 1024),
            cost_estimate=pl.CostEstimate(
                flops=1 << 31, bytes_accessed=2 << 20, transcendentals=0
            ),
        )(tile_wave, *before, wide_rows)
    detector = pl.pallas_call(
        functools.partial(detector_kernel, waves),
        name="detector",
        out_shape=made((tile_cols, total_rows), jnp.float32),
        in_specs=[in_vmem] * 5,
        out_specs=in_vmem,
        scratch_shapes=[pltpu.VMEM((total_rows + 128, tile_cols), jnp.float32)],
        compiler_params=pltpu.CompilerParams(vmem_limit_bytes=20 * 1024 * 1024),
        cost_estimate=pl.CostEstimate(flops=1 << 33, bytes_accessed=4 << 20, transcendentals=0),
    )(tile_waves[-1], image, wide_rows, row_taps, col_taps)
    return exit_wave, detector[None]


def solution(mesh):
    placed = (
        P(None, ("lamella", "lat"), None),
        P("lamella"),
        P("lamella"),
        P(),
        P(),
        P(),
        P(),
        P("lamella"),
    )
    return jax.shard_map(
        local,
        mesh=mesh,
        in_specs=placed,
        out_specs=(P(None, None, ("lamella", "lat"), None), P(("lamella", "lat"), None, None)),
        check_vma=False,
    )
```

```python
import functools
import math

import jax
import jax.numpy as jnp
from jax import lax
from jax.experimental import pallas as pl
from jax.experimental.pallas import tpu as pltpu
from jax.sharding import PartitionSpec as P

highest = lax.Precision.HIGHEST
SIN_TURN = (
    6.2831854820251465,
    -41.34170150756836,
    81.60513305664062,
    -76.70301818847656,
    42.02592849731445,
    -14.899847030639648,
    3.2381374835968018,
)
COS_TURN = (
    1.0,
    -19.73920440673828,
    64.93911743164062,
    -85.45014190673828,
    60.16762924194336,
    -25.967599868774414,
    6.528658390045166,
)
SIN_QUARTER = (
    0.4204482138156891,
    -0.004379667341709137,
    1.3686111742572393e-05,
    -2.0339173900651986e-08,
    1.679661791598175e-11,
)
COS_QUARTER = (
    1.6817927360534668,
    -0.052555955946445465,
    0.00027371387113817036,
    -5.690624220733298e-07,
    5.977824346636851e-10,
)
HALO = 32
STEP = 512
TILE = 256


def horner(coefs, z):
    total = coefs[-1] * z + coefs[-2]
    for coef in coefs[-3::-1]:
        total = total * z + coef
    return total


def cos_sin_turns(turns):
    rest = turns - jnp.round(turns)
    z = rest * rest
    return horner(COS_TURN, z), horner(SIN_TURN, z) * rest


def cos_sin(phase):
    z = phase * phase
    quarter_sin = horner(SIN_QUARTER, z) * phase
    half_sin = quarter_sin * horner(COS_QUARTER, z)
    half_cos = math.sqrt(2.0) - quarter_sin * quarter_sin
    return 1.0 - half_sin * half_sin, half_sin * half_cos


def dot(a, b):
    return jnp.dot(a, b, preferred_element_type=jnp.float32)


def lanes_inside(block, shift, col_count):
    cols = block * 128 - shift + lax.broadcasted_iota(jnp.int32, (1, 128), 1)
    return ((cols >= 0) & (cols < col_count)).astype(jnp.float32)


def rows_of(ref, lead, start, count, lanes):
    if lead is None:
        found = ref[pl.ds(start, count), lanes]
    else:
        found = ref[lead, pl.ds(start, count), lanes]
    return found.astype(jnp.float32)


def chunks(pieces, size):
    row = 0
    for ref, lead, first, rows in pieces:
        for start in range(0, rows, size):
            yield ref, lead, first + start, row
            row += size


def columns_tasks(ring, band, store):
    waves, blocks = ring.shape[0], ring.shape[2] // 256 - 1

    def task(w, blk):
        store(w, blk, dot(ring[w, :, 256 * blk : 256 * blk + 512], band[...]))
        if blk == blocks - 1:
            ring[w, :, :256] = ring[w, :, 256 * blocks :]

    return [functools.partial(task, w, blk) for w in range(waves) for blk in range(blocks)]


def spread_store(spread):
    rows = spread.shape[1] // 2

    def store(w, blk, value):
        lanes = pl.ds(128 * blk, 128)
        spread[w, :rows, lanes] = value[:, :128].astype(jnp.bfloat16)
        spread[w, rows:, lanes] = value[:, 128:].astype(jnp.bfloat16)

    return store


def rows_tasks(product, rows_band, spread):
    def task(w):
        product[w] = dot(rows_band[...], spread[w])

    return [functools.partial(task, w) for w in range(spread.shape[0])]


def run(*lists):
    for tasks in lists:
        for task in tasks:
            task()


def start_tasks(pieces, ex, ey, first_lane, ring):
    waves, blocks = ring.shape[0], ring.shape[2] // 256 - 1

    def task(ref, lead, start, row):
        for blk in range(blocks):
            lanes = pl.ds(128 * blk, 128)
            cosine, sine = cos_sin(rows_of(ref, lead, start, 32, lanes))
            to = 256 * (blk + 1)
            for w in range(waves):
                at = pl.ds(first_lane + 128 * blk, 128)
                yr, yi = ey[2 * w : 2 * w + 1, at], ey[2 * w + 1 : 2 * w + 2, at]
                ur, ui = cosine * yr - sine * yi, cosine * yi + sine * yr
                xr, xi = ex[2 * w, pl.ds(row, 32)], ex[2 * w + 1, pl.ds(row, 32)]
                ring[w, pl.ds(row, 32), to : to + 128] = (ur * xr - ui * xi).astype(jnp.bfloat16)
                ring[w, pl.ds(row, 32), to + 128 : to + 256] = (ur * xi + ui * xr).astype(
                    jnp.bfloat16
                )

    return [functools.partial(task, *chunk) for chunk in chunks(pieces, 32)]


def transmit_tasks(pieces, product, ring, last, masks, turn):
    waves, rows = ring.shape[:2]

    def task(ref, lead, start, row):
        here = pl.ds(row, 32)
        before = last[here]
        low = lax.broadcasted_iota(jnp.int32, (32, 128), 1) < 64
        for blk, mask in enumerate(masks):
            found = rows_of(ref, lead, start, 32, pl.ds(128 * blk, 128))
            if turn:
                found = pltpu.roll(found, 64, 1)
            phase = jnp.where(low, before, found) if turn else before
            before = found
            cosine, sine = cos_sin(phase)
            cosine, sine = cosine * mask, sine * mask
            to = 256 * (blk + 1)
            for w in range(waves):
                real = product[w, here, 128 * blk : 128 * blk + 128]
                imag = product[w, pl.ds(rows + row, 32), 128 * blk : 128 * blk + 128]
                ring[w, here, to : to + 128] = (real * cosine - imag * sine).astype(jnp.bfloat16)
                ring[w, here, to + 128 : to + 256] = (real * sine + imag * cosine).astype(
                    jnp.bfloat16
                )
        last[here] = before

    return [functools.partial(task, *chunk) for chunk in chunks(pieces, 32)]


def steps_kernel(waves, rows, col_count, begin, count, resumed, handed, order, owner, *refs):
    up2, up, own1, own2, own3, down, down2, ex, ey, mats = refs[:10]
    refs = refs[10:]
    given, refs = (refs[:7], refs[9:]) if resumed else (None, refs)
    exit_wave, focused = refs[:2]
    given_on, refs = (refs[2:9], refs[9:]) if handed else (None, refs[2:])
    ring1, ring2, ring3, waved, last2, last3, turned = carried = refs[:7]
    spread1, spread2, spread3, product2, product3, exit_held, focused_held, sems = refs[7:]
    local_step = pl.program_id(0)
    g = local_step + begin
    rings = carried[:4]
    blocks = STEP // 128
    tiles = STEP // TILE
    slot = local_step % 2

    @pl.when(local_step == 0)
    def _():
        for i, ref in enumerate(carried):
            if given is None:
                if i < 4:
                    ref[:, :, :256] = jnp.zeros((waves, ref.shape[1], 256), jnp.bfloat16)
                else:
                    ref[...] = jnp.zeros_like(ref)
            elif i < 4:
                ref[:, :, :256] = given[i][...]
            else:
                ref[...] = given[i][...]

    def for_copies(step, slot, act):
        for k in range(tiles):
            tile = tiles * (step + begin) - 1 + k

            @pl.when((tile >= 0) & (tile < col_count // TILE))
            def _(tile=tile, k=k):
                lanes = pl.ds(TILE * k, TILE)
                there = pl.ds(pl.multiple_of(tile * TILE, TILE), TILE)
                act(
                    pltpu.make_async_copy(
                        exit_held.at[slot, :, :, :, lanes],
                        exit_wave.at[:, :, :, there],
                        sems.at[0, slot, k],
                    )
                )
                if len(focused.shape) == 5:
                    target = focused.at[owner[tile]]
                else:
                    target = focused.at[:, :, :, there]
                act(
                    pltpu.make_async_copy(
                        focused_held.at[slot, :, :, :, lanes], target, sems.at[1, slot, k]
                    )
                )

    @pl.when(local_step >= 2)
    def _():
        for_copies(local_step - 2, slot, lambda copy: copy.wait())

    sizes = [ring.shape[1] for ring in rings]
    band2 = mats.at[pl.ds(0, 2 * sizes[1]), pl.ds(0, 2 * sizes[0])]
    at = 2 * sizes[1]
    band3 = mats.at[pl.ds(at, 2 * sizes[2]), pl.ds(0, 2 * sizes[1])]
    at += 2 * sizes[2]
    band4 = mats.at[pl.ds(at, 2 * sizes[3]), pl.ds(0, 2 * sizes[2])]
    at += 2 * sizes[3]
    band = mats.at[pl.ds(at, 512), pl.ds(0, 256)]
    wide_band = mats.at[pl.ds(at, 512), pl.ds(256, 256)]
    first = (
        (up2, None, 0, HALO), (up, None, 0, rows), (own1, 0, 0, rows),
        (down, None, 0, rows), (down2, None, 0, HALO),
    )
    second = ((up, None, rows, rows), (own2, 0, 0, rows), (down, None, rows, rows))
    third = ((up, None, 2 * rows, HALO), (own3, 0, 0, rows), (down, None, 2 * rows, HALO))
    masks2 = [lanes_inside(blocks * g + blk, 64, col_count) for blk in range(blocks)]
    masks3 = [lanes_inside(blocks * g - 1 + blk, 0, col_count) for blk in range(blocks)]
    masks4 = [lanes_inside(blocks * g - 1 + blk, 64, col_count) for blk in range(blocks)]
    kept = waved.shape[1]
    low = lax.broadcasted_iota(jnp.int32, (kept, 128), 1) < 64

    def exit_task(w):
        product = dot(band4[...], spread3[w])
        for part in range(2):
            before = turned[w, part]
            for blk in range(blocks):
                value = product[kept * part : kept * part + kept, 128 * blk : 128 * blk + 128]
                lane = 256 * (blk + 1) + 128 * part
                waved[w, :, lane : lane + 128] = (value * masks4[blk]).astype(jnp.bfloat16)
                rolled = pltpu.roll(value, 64, 1)
                exit_held[slot, w, part, :, 128 * blk : 128 * blk + 128] = jnp.where(
                    low, before, rolled
                )
                before = rolled
            turned[w, part] = before

    def focused_store(w, blk, value):
        for part in range(2):
            block = value[:, 128 * part : 128 * part + 128].astype(jnp.bfloat16)
            focused_held[slot, w, part, :, 128 * blk : 128 * blk + 128] = block

    first_lane = pl.multiple_of(g * STEP, STEP)
    run(start_tasks(first, ex, ey, first_lane, ring1))
    run(columns_tasks(ring1, band, spread_store(spread1)))
    run(rows_tasks(product2, band2, spread1))
    run(transmit_tasks(second, product2, ring2, last2, masks2, True))
    run(columns_tasks(ring2, band, spread_store(spread2)))
    run(rows_tasks(product3, band3, spread2))
    run(transmit_tasks(third, product3, ring3, last3, masks3, False))
    run(columns_tasks(ring3, band, spread_store(spread3)))
    run([functools.partial(exit_task, w) for w in range(waves)])
    run(columns_tasks(waved, wide_band, focused_store))
    for_copies(local_step, slot, lambda copy: copy.start())

    @pl.when(local_step == count - 1)
    def _():
        if count > 1:
            for_copies(local_step - 1, 1 - slot, lambda copy: copy.wait())
        for_copies(local_step, slot, lambda copy: copy.wait())
        if handed:
            for i, ref in enumerate(carried):
                given_on[i][...] = ref[:, :, :256] if i < 4 else ref[...]


def pick_kernel(halo, edges, order, potential, *refs):
    outs, held, load_sems, sems = refs[:-3], refs[-3], refs[-2], refs[-1]
    rows = potential.shape[1]
    loads = []
    for step in range(3):
        load = pltpu.make_async_copy(potential.at[order[step]], held.at[step], load_sems.at[step])
        load.start()
        loads.append(load)
    for load in loads:
        load.wait()
    copies = []
    for i, (left, right) in enumerate(zip(edges[:-1], edges[1:])):
        lanes = pl.ds(left, right - left)
        up, down, up2, down2 = outs[4 * i : 4 * i + 4]
        high, low = pl.ds(rows - halo, halo), pl.ds(0, halo)
        after = pl.ds(2 * rows, halo)
        pairs = []
        for target, part in ((up, high), (down, low)):
            for step in range(2):
                pairs.append((held.at[step, :, lanes], target.at[pl.ds(rows * step, rows)]))
            pairs.append((held.at[2, part, lanes], target.at[after]))
        pairs += [(held.at[0, high, lanes], up2), (held.at[0, low, lanes], down2)]
        for source, target in pairs:
            copy = pltpu.make_async_copy(source, target, sems.at[len(copies)])
            copy.start()
            copies.append(copy)
    for copy in copies:
        copy.wait()


def toeplitz(row, count, shift):
    wide = jnp.broadcast_to(row, (count, 256))
    return pltpu.roll(wide, shift % 256, 1, stride=1, stride_axis=0)


def inside_rows(first, count, total):
    at = first + lax.broadcasted_iota(jnp.int32, (count, 1), 0)
    return ((at >= 0) & (at < total)).astype(jnp.float32)


def prepare_kernel(
    waves, rows, total_rows, col_count, tilt_index, first_row, tilt_table, fresnel, ctf, mtf,
    mats, wide_rows, row_taps, col_taps, ex, ey, line,
):
    rows3, rows2, rows1 = (rows + 2 * HALO * k for k in (1, 2, 3))
    mats[...] = jnp.zeros_like(mats)
    at = 2 * rows2 + 2 * rows3 + 2 * rows
    band, wide_band = (mats.at[pl.ds(at, 512), pl.ds(256 * i, 256)] for i in range(2))
    band2 = mats.at[pl.ds(0, 2 * rows2), pl.ds(0, 2 * rows1)]
    band3 = mats.at[pl.ds(2 * rows2, 2 * rows3), pl.ds(0, 2 * rows2)]
    band4 = mats.at[pl.ds(2 * rows2 + 2 * rows3, 2 * rows), pl.ds(0, 2 * rows3)]
    line[...] = jnp.zeros_like(line)
    line[0:2, : fresnel.shape[1]] = fresnel[...].astype(jnp.bfloat16).astype(jnp.float32)
    line[2:4, : ctf.shape[1]] = ctf[...].astype(jnp.bfloat16).astype(jnp.float32)
    line[4:5, : mtf.shape[1]] = mtf[...]
    first = first_row[0]

    def columns(target, at, shift):
        for part in range(2):
            made = toeplitz(line[at + part : at + part + 1], 128, shift)
            for k in range(2):
                turned = jnp.transpose(made[:, 128 * k : 128 * k + 128])
                up, down = 256 * k, 256 * k + 128
                if part == 0:
                    target[up:down, :128] = turned.astype(jnp.bfloat16)
                    target[down : down + 128, 128:] = turned.astype(jnp.bfloat16)
                else:
                    target[up:down, 128:] = turned.astype(jnp.bfloat16)
                    target[down : down + 128, :128] = (-turned).astype(jnp.bfloat16)

    columns(band, 0, 65 - (fresnel.shape[1] + 1) // 2)
    columns(wide_band, 2, 65 - (ctf.shape[1] + 1) // 2)
    for target, halo in ((band2, 2 * HALO), (band3, HALO), (band4, 0)):
        count, count_in = target.shape[0] // 2, target.shape[1] // 2
        keep = inside_rows(first - halo, count, total_rows)
        for part in range(2):
            made = toeplitz(line[part : part + 1], count, HALO - (fresnel.shape[1] - 1) // 2) * keep
            made = made[:, :count_in].astype(jnp.bfloat16)
            if part == 0:
                target[:count, :count_in] = made
                target[count:, count_in:] = made
            else:
                target[:count, count_in:] = -made
                target[count:, :count_in] = made
    for part in range(2):
        made = toeplitz(line[2 + part : 3 + part], 128, 65 - (ctf.shape[1] + 1) // 2)
        wide_rows[128 * part : 128 * part + 128] = made.astype(jnp.bfloat16)
    reach = (mtf.shape[1] - 1) // 2
    row_taps[...] = toeplitz(line[4:5], 128, 64 - reach)
    width = col_taps.shape[0]
    off = lax.broadcasted_iota(jnp.int32, (width, 256), 1) - lax.broadcasted_iota(
        jnp.int32, (width, 256), 0
    )
    made = jnp.where(jnp.abs(off) <= reach, toeplitz(line[4:5], width, -reach), 0.0)
    col_taps[...] = made[:, :width]
    count = ex.shape[1]
    at = first - 3 * HALO + lax.broadcasted_iota(jnp.int32, (count, 128), 0)
    keep = ((at >= 0) & (at < total_rows)).astype(jnp.float32)
    at = at.astype(jnp.float32) * (1.0 / total_rows)
    across = lax.broadcasted_iota(jnp.int32, (1, ey.shape[1]), 1)
    keep_cols = (across < col_count).astype(jnp.float32)
    across = across.astype(jnp.float32) * (1.0 / col_count)
    for w in range(waves):
        cosine, sine = cos_sin_turns(at * tilt_table[tilt_index[w], 0])
        ex[2 * w] = cosine * keep
        ex[2 * w + 1] = sine * keep
        cosine, sine = cos_sin_turns(across * tilt_table[tilt_index[w], 1])
        ey[2 * w : 2 * w + 1] = cosine * keep_cols
        ey[2 * w + 1 : 2 * w + 2] = sine * keep_cols


def detector_kernel(waves, tile_wave, taps_band, row_taps, col_taps, out, padded):
    sources, rows, width = tile_wave.shape[0], tile_wave.shape[3], tile_wave.shape[4]
    total = sources * rows
    edge = jnp.zeros((64, width), jnp.float32)
    padded[:64] = edge
    padded[64 + total :] = edge
    for b in range(total // 128):
        image = None
        for w in range(waves):
            parts = []
            for part in range(2):
                window = []
                for k in range(2 * b - 1, 2 * b + 3):
                    if 0 <= k < total // 64:
                        window.append(tile_wave[k, w, part])
                    else:
                        window.append(jnp.zeros((64, width), jnp.bfloat16))
                parts.append(jnp.concatenate(window, axis=0))
            real, imag = dot(taps_band[...], parts[0]), dot(taps_band[...], parts[1])
            re = real[:128] - imag[128:]
            im = imag[:128] + real[128:]
            term = re * re + im * im
            image = term if image is None else image + term
        padded[64 + 128 * b : 192 + 128 * b] = image / waves
    for b in range(total // 128):
        rows_done = jnp.dot(
            row_taps[...],
            padded[128 * b : 128 * b + 256],
            precision=highest,
            preferred_element_type=jnp.float32,
        )
        out[:, 128 * b : 128 * b + 128] = lax.dot_general(
            col_taps[...],
            rows_done,
            (((1,), (1,)), ((), ())),
            precision=highest,
            preferred_element_type=jnp.float32,
        )


def block_windows(values):
    length = values.shape[-1]
    padded = jnp.pad(values, [(0, 0)] * (values.ndim - 1) + [(64, 64)])
    blocks = padded.reshape(values.shape[:-1] + (length // 128 + 1, 128))
    return jnp.concatenate([blocks[..., :-1, :], blocks[..., 1:, :]], axis=-1)


def narrow_tiles(focused, owner, wide_rows, row_taps, col_taps, lane_count):
    waves, _, rows, col_count = focused.shape
    width = col_count // lane_count
    slots = jnp.arange(lane_count, dtype=jnp.int32)
    placing = (owner[None, :] == slots[:, None]).astype(jnp.bfloat16)
    focused = focused.reshape(waves, 2, rows, lane_count, width)
    focused = jnp.einsum("jl,acrlk->jackr", placing, focused, preferred_element_type=jnp.float32)
    sent = focused.astype(jnp.bfloat16)
    tile_wave = lax.all_to_all(sent, "lat", split_axis=0, concat_axis=4, tiled=True)[0]
    windows = block_windows(tile_wave)
    taps_band = wide_rows.reshape(2, 128, 256)
    made = jnp.einsum("acwbi,doi->acdwbo", windows, taps_band, preferred_element_type=jnp.float32)
    real = made[:, 0, 0] - made[:, 1, 1]
    imag = made[:, 1, 0] + made[:, 0, 1]
    image = jnp.sum(real * real + imag * imag, axis=0) / waves
    image = image.reshape(width, lane_count * rows)
    blurred = jnp.einsum("wbi,oi->wbo", block_windows(image), row_taps, precision=highest)
    return jnp.dot(col_taps, blurred.reshape(width, lane_count * rows), precision=highest)


def local(potential, tilt_index, slice_order, tilt_table, fresnel_taps, ctf_taps, mtf_taps, owner):
    row_count, col_count = potential.shape[1:]
    lane_count = lax.axis_size("lat")
    total_rows = row_count * lane_count
    tile_cols = col_count // lane_count
    waves = tilt_index.shape[0]
    first_row = lax.axis_index("lat") * row_count
    steps = col_count // STEP

    def neighbour(value, offset):
        pairs = [(i, i + offset) for i in range(lane_count) if 0 <= i + offset < lane_count]
        return lax.ppermute(value, "lat", pairs)

    rows1, rows2, rows3 = (row_count + 2 * HALO * k for k in (3, 2, 1))
    anywhere = pl.BlockSpec(memory_space=pl.ANY)
    in_vmem = pl.BlockSpec(memory_space=pltpu.VMEM)
    in_smem = pl.BlockSpec(memory_space=pltpu.SMEM)
    widths = [steps // 2, steps - steps // 2]
    edges = [STEP * sum(widths[:i]) for i in range(len(widths) + 1)]
    sent_rows = (2 * row_count + HALO, 2 * row_count + HALO, HALO, HALO)
    picked = pl.pallas_call(
        functools.partial(pick_kernel, HALO, edges),
        name="pick_rows",
        out_shape=[
            jax.ShapeDtypeStruct((rows, STEP * width), potential.dtype)
            for width in widths
            for rows in sent_rows
        ],
        in_specs=[in_smem, anywhere],
        out_specs=[anywhere] * (4 * len(widths)),
        scratch_shapes=[
            pltpu.VMEM((3, row_count, col_count), potential.dtype),
            pltpu.SemaphoreType.DMA((3,)),
            pltpu.SemaphoreType.DMA((8 * len(widths),)),
        ],
        cost_estimate=pl.CostEstimate(flops=0, bytes_accessed=4 << 20, transcendentals=0),
    )(slice_order, potential)
    halos = [
        [neighbour(value, offset) for value, offset in zip(picked[4 * i : 4 * i + 4], (1, -1, 2, -2))]
        for i in range(len(widths))
    ]

    mats_shape = (2 * rows2 + 2 * rows3 + 2 * row_count + 512, 2 * rows1)

    def made(shape, dtype):
        return jax.ShapeDtypeStruct(shape, dtype)

    mats, wide_rows, row_taps, col_taps, ex, ey = pl.pallas_call(
        functools.partial(prepare_kernel, waves, row_count, total_rows, col_count),
        name="prepare",
        out_shape=[
            made(mats_shape, jnp.bfloat16),
            made((256, 256), jnp.bfloat16),
            made((128, 256), jnp.float32),
            made((tile_cols, tile_cols), jnp.float32),
            made((2 * waves, rows1, 128), jnp.float32),
            made((2 * waves, col_count + STEP), jnp.float32),
        ],
        in_specs=[in_smem] * 3 + [in_vmem] * 3,
        out_specs=[in_vmem] * 6,
        scratch_shapes=[pltpu.VMEM((8, 256), jnp.float32)],
        cost_estimate=pl.CostEstimate(flops=1 << 31, bytes_accessed=2 << 20, transcendentals=0),
    )(tilt_index, first_row[None], tilt_table, fresnel_taps, ctf_taps, mtf_taps[None])

    def clamp(g):
        return jnp.clip(g, 0, steps - 1)

    def fixed(*shape):
        return pl.BlockSpec(shape, lambda g, *_: (0,) * len(shape))

    placed = tile_cols == TILE
    if placed:
        focused_shape = (lane_count, waves, 2, row_count, tile_cols)
    else:
        focused_shape = (waves, 2, row_count, col_count)
    carried = [((waves, rows, 256), jnp.bfloat16) for rows in (rows1, rows2, rows3, row_count)]
    carried += [
        ((rows2, 128), jnp.float32),
        ((rows3, 128), jnp.float32),
        ((waves, 2, row_count, 128), jnp.float32),
    ]

    def ring(rows, lanes, dtype=jnp.bfloat16):
        return pltpu.VMEM((waves, rows, lanes), dtype)

    outputs = [
        made((waves, 2, row_count, col_count), jnp.float32),
        made(focused_shape, jnp.bfloat16),
    ]
    given = None
    for i, width in enumerate(widths):
        begin, last_call = edges[i] // STEP, i + 1 == len(widths)
        count = width + 1 if last_call else width

        def piece(rows, width=width):
            return pl.BlockSpec((rows, STEP), lambda g, *_: (0, jnp.minimum(g, width - 1)))

        def mine(step, begin=begin):
            return pl.BlockSpec(
                (1, row_count, STEP), lambda g, order, *_: (order[step], 0, clamp(g + begin))
            )

        up, down, up2, down2 = halos[i]
        args = [slice_order, owner, up2, up, potential, potential, potential, down, down2, ex, ey, mats]
        in_specs = [
            piece(HALO),
            piece(2 * row_count + HALO),
            mine(0),
            mine(1),
            mine(2),
            piece(2 * row_count + HALO),
            piece(HALO),
            fixed(*ex.shape),
            fixed(*ey.shape),
            fixed(*mats.shape),
        ]
        aliases = {}
        if given is not None:
            args += given
            in_specs += [fixed(*shape) for shape, _ in carried] + [anywhere, anywhere]
            aliases = {len(args) - 2: 0, len(args) - 1: 1}
        out_shape = list(outputs)
        out_specs = [anywhere, anywhere]
        if not last_call:
            out_shape += [made(shape, dtype) for shape, dtype in carried]
            out_specs += [fixed(*shape) for shape, _ in carried]
        results = pl.pallas_call(
            functools.partial(
                steps_kernel, waves, row_count, col_count, begin, count, given is not None, not last_call
            ),
            name="steps",
            out_shape=out_shape,
            grid_spec=pltpu.PrefetchScalarGridSpec(
                num_scalar_prefetch=2,
                grid=(count,),
                in_specs=in_specs,
                out_specs=out_specs,
                scratch_shapes=[
                    ring(rows, 256 + 2 * STEP) for rows in (rows1, rows2, rows3, row_count)
                ]
                + [pltpu.VMEM(shape, dtype) for shape, dtype in carried[4:]]
                + [ring(2 * rows, STEP) for rows in (rows1, rows2, rows3)]
                + [ring(2 * rows, STEP, jnp.float32) for rows in (rows2, rows3)]
                + [
                    pltpu.VMEM((2, waves, 2, row_count, STEP), jnp.float32),
                    pltpu.VMEM((2, waves, 2, row_count, STEP), jnp.bfloat16),
                    pltpu.SemaphoreType.DMA((2, 2, STEP // TILE)),
                ],
            ),
            input_output_aliases=aliases,
            compiler_params=pltpu.CompilerParams(
                dimension_semantics=("arbitrary",), vmem_limit_bytes=32 * 1024 * 1024
            ),
            cost_estimate=pl.CostEstimate(
                flops=count * (1 << 31), bytes_accessed=count << 20, transcendentals=0
            ),
        )(*args)
        given = list(results[2:]) + list(results[:2])
    exit_wave, focused = results[:2]

    if not placed:
        detector = narrow_tiles(focused, owner, wide_rows, row_taps, col_taps, lane_count)
        return exit_wave, detector[None]

    tile_wave = lax.all_to_all(focused, "lat", split_axis=0, concat_axis=0, tiled=True)
    detector = pl.pallas_call(
        functools.partial(detector_kernel, waves),
        name="detector",
        out_shape=jax.ShapeDtypeStruct((tile_cols, total_rows), jnp.float32),
        in_specs=[pl.BlockSpec(memory_space=pltpu.VMEM)] * 4,
        out_specs=pl.BlockSpec(memory_space=pltpu.VMEM),
        scratch_shapes=[pltpu.VMEM((total_rows + 128, tile_cols), jnp.float32)],
        compiler_params=pltpu.CompilerParams(vmem_limit_bytes=48 * 1024 * 1024),
        cost_estimate=pl.CostEstimate(
            flops=1 << 33, bytes_accessed=4 << 20, transcendentals=0
        ),
    )(tile_wave, wide_rows, row_taps, col_taps)
    return exit_wave, detector[None]


def solution(mesh):
    placed = (
        P(None, ("lamella", "lat"), None),
        P("lamella"),
        P("lamella"),
        P(),
        P(),
        P(),
        P(),
        P("lamella"),
    )
    return jax.shard_map(
        local,
        mesh=mesh,
        in_specs=placed,
        out_specs=(P(None, None, ("lamella", "lat"), None), P(("lamella", "lat"), None, None)),
        check_vma=False,
    )
```

```python
import functools
import math

import jax
import jax.numpy as jnp
from jax import lax
from jax.experimental import pallas as pl
from jax.experimental.pallas import tpu as pltpu
from jax.sharding import PartitionSpec as P

highest = lax.Precision.HIGHEST
SIN_TURN = (
    6.2831854820251465,
    -41.34170150756836,
    81.60513305664062,
    -76.70301818847656,
    42.02592849731445,
    -14.899847030639648,
    3.2381374835968018,
)
COS_TURN = (
    1.0,
    -19.73920440673828,
    64.93911743164062,
    -85.45014190673828,
    60.16762924194336,
    -25.967599868774414,
    6.528658390045166,
)
SIN_QUARTER = (
    0.4204482138156891,
    -0.004379667341709137,
    1.3686111742572393e-05,
    -2.0339173900651986e-08,
    1.679661791598175e-11,
)
COS_QUARTER = (
    1.6817927360534668,
    -0.052555955946445465,
    0.00027371387113817036,
    -5.690624220733298e-07,
    5.977824346636851e-10,
)
HALO = 32
STEP = 512
TILE = 256


def horner(coefs, z):
    total = coefs[-1] * z + coefs[-2]
    for coef in coefs[-3::-1]:
        total = total * z + coef
    return total


def cos_sin_turns(turns):
    rest = turns - jnp.round(turns)
    z = rest * rest
    return horner(COS_TURN, z), horner(SIN_TURN, z) * rest


def cos_sin(phase):
    z = phase * phase
    quarter_sin = horner(SIN_QUARTER, z) * phase
    half_sin = quarter_sin * horner(COS_QUARTER, z)
    half_cos = math.sqrt(2.0) - quarter_sin * quarter_sin
    return 1.0 - half_sin * half_sin, half_sin * half_cos


def dot(a, b):
    return jnp.dot(a, b, preferred_element_type=jnp.float32)


def lanes_inside(block, shift, col_count):
    cols = block * 128 - shift + lax.broadcasted_iota(jnp.int32, (1, 128), 1)
    return ((cols >= 0) & (cols < col_count)).astype(jnp.float32)


def rows_of(ref, lead, start, count, lanes):
    if lead is None:
        found = ref[pl.ds(start, count), lanes]
    else:
        found = ref[lead, pl.ds(start, count), lanes]
    return found.astype(jnp.float32)


def chunks(pieces, size):
    row = 0
    for ref, lead, first, rows in pieces:
        for start in range(0, rows, size):
            yield ref, lead, first + start, row
            row += size


def columns_tasks(ring, band, store):
    waves, blocks = ring.shape[0], ring.shape[2] // 256 - 1

    def task(w, blk):
        store(w, blk, dot(ring[w, :, 256 * blk : 256 * blk + 512], band[...]))
        if blk == blocks - 1:
            ring[w, :, :256] = ring[w, :, 256 * blocks :]

    return [functools.partial(task, w, blk) for w in range(waves) for blk in range(blocks)]


def spread_store(spread):
    rows = spread.shape[1] // 2

    def store(w, blk, value):
        lanes = pl.ds(128 * blk, 128)
        spread[w, :rows, lanes] = value[:, :128].astype(jnp.bfloat16)
        spread[w, rows:, lanes] = value[:, 128:].astype(jnp.bfloat16)

    return store


def rows_product(rows_band, spread, w, block):
    half = spread.shape[1] // 2
    window = [spread[w, half * part + 64 * block : half * part + 64 * block + 128] for part in range(2)]
    return dot(rows_band[...], jnp.concatenate(window, axis=0))


def rows_tasks(product, rows_band, spread):
    waves, rows = product.shape[0], product.shape[1] // 2

    def task(w, block):
        result = rows_product(rows_band, spread, w, block)
        at = 64 * block
        product[w, at : at + 64] = result[:64]
        product[w, rows + at : rows + at + 64] = result[64:]

    return [functools.partial(task, w, block) for w in range(waves) for block in range(rows // 64)]


def run(*lists):
    for tasks in lists:
        for task in tasks:
            task()


def start_tasks(pieces, table, first_block, ring):
    waves, blocks = ring.shape[0], ring.shape[2] // 256 - 1

    def task(ref, lead, start, row):
        for blk in range(blocks):
            lanes = pl.ds(128 * blk, 128)
            cosine, sine = cos_sin(rows_of(ref, lead, start, 32, lanes))
            to = 256 * (blk + 1)
            at = pl.ds(ring.shape[1] + first_block + blk, 1)
            for w in range(waves):
                yr, yi = table[2 * w, at], table[2 * w + 1, at]
                ur, ui = cosine * yr - sine * yi, cosine * yi + sine * yr
                xr, xi = table[2 * w, pl.ds(row, 32)], table[2 * w + 1, pl.ds(row, 32)]
                ring[w, pl.ds(row, 32), to : to + 128] = (ur * xr - ui * xi).astype(jnp.bfloat16)
                ring[w, pl.ds(row, 32), to + 128 : to + 256] = (ur * xi + ui * xr).astype(
                    jnp.bfloat16
                )

    return [functools.partial(task, *chunk) for chunk in chunks(pieces, 32)]


def transmit_tasks(pieces, product, ring, last, masks, turn, first_row, total_rows):
    waves, rows = ring.shape[:2]

    def task(ref, lead, start, row):
        here = pl.ds(row, 32)
        at = first_row + row
        inside = ((at >= 0) & (at < total_rows)).astype(jnp.float32)
        before = last[here]
        low = lax.broadcasted_iota(jnp.int32, (32, 128), 1) < 64
        for blk, mask in enumerate(masks):
            found = rows_of(ref, lead, start, 32, pl.ds(128 * blk, 128))
            if turn:
                found = pltpu.roll(found, 64, 1)
            phase = jnp.where(low, before, found) if turn else before
            before = found
            cosine, sine = cos_sin(phase)
            cosine, sine = cosine * (mask * inside), sine * (mask * inside)
            to = 256 * (blk + 1)
            for w in range(waves):
                real = product[w, here, 128 * blk : 128 * blk + 128]
                imag = product[w, pl.ds(rows + row, 32), 128 * blk : 128 * blk + 128]
                ring[w, here, to : to + 128] = (real * cosine - imag * sine).astype(jnp.bfloat16)
                ring[w, here, to + 128 : to + 256] = (real * sine + imag * cosine).astype(
                    jnp.bfloat16
                )
        last[here] = before

    return [functools.partial(task, *chunk) for chunk in chunks(pieces, 32)]


def steps_kernel(
    waves, rows, total_rows, col_count, begin, count, resumed, handed, order, owner, first_row, *refs
):
    up2, up, own1, own2, own3, down, down2, table, mats = refs[:9]
    refs = refs[9:]
    given, refs = (refs[:7], refs[9:]) if resumed else (None, refs)
    exit_wave, focused = refs[:2]
    given_on, refs = (refs[2:9], refs[9:]) if handed else (None, refs[2:])
    ring1, ring2, ring3, waved, last2, last3, turned = carried = refs[:7]
    spread1, spread2, spread3, product2, product3, exit_held, focused_held, sems = refs[7:]
    local_step = pl.program_id(0)
    g = local_step + begin
    blocks = STEP // 128
    tiles = STEP // TILE
    slot = local_step % 2

    @pl.when(local_step == 0)
    def _():
        for i, ref in enumerate(carried):
            if given is None:
                if i < 4:
                    ref[:, :, :256] = jnp.zeros((waves, ref.shape[1], 256), jnp.bfloat16)
                else:
                    ref[...] = jnp.zeros_like(ref)
            elif i < 4:
                ref[:, :, :256] = given[i][...]
            else:
                ref[...] = given[i][...]

    def for_copies(step, slot, act):
        for k in range(tiles):
            tile = tiles * (step + begin) - 1 + k

            @pl.when((tile >= 0) & (tile < col_count // TILE))
            def _(tile=tile, k=k):
                lanes = pl.ds(TILE * k, TILE)
                there = pl.ds(pl.multiple_of(tile * TILE, TILE), TILE)
                act(
                    pltpu.make_async_copy(
                        exit_held.at[slot, :, :, :, lanes],
                        exit_wave.at[:, :, :, there],
                        sems.at[0, slot, k],
                    )
                )
                if len(focused.shape) == 5:
                    target = focused.at[owner[tile]]
                else:
                    target = focused.at[:, :, :, there]
                act(
                    pltpu.make_async_copy(
                        focused_held.at[slot, :, :, :, lanes], target, sems.at[1, slot, k]
                    )
                )

    @pl.when(local_step >= 2)
    def _():
        for_copies(local_step - 2, slot, lambda copy: copy.wait())

    rows_band = mats.at[pl.ds(0, 128), pl.ds(0, 256)]
    band = mats.at[pl.ds(128, 512), pl.ds(0, 256)]
    wide_band = mats.at[pl.ds(128, 512), pl.ds(256, 256)]
    first = (
        (up2, None, 0, HALO), (up, None, 0, rows), (own1, 0, 0, rows),
        (down, None, 0, rows), (down2, None, 0, HALO),
    )
    second = ((up, None, rows, rows), (own2, 0, 0, rows), (down, None, rows, rows))
    third = ((up, None, 2 * rows, HALO), (own3, 0, 0, rows), (down, None, 2 * rows, HALO))
    masks2 = [lanes_inside(blocks * g + blk, 64, col_count) for blk in range(blocks)]
    masks3 = [lanes_inside(blocks * g - 1 + blk, 0, col_count) for blk in range(blocks)]
    masks4 = [lanes_inside(blocks * g - 1 + blk, 64, col_count) for blk in range(blocks)]
    kept = waved.shape[1]
    low = lax.broadcasted_iota(jnp.int32, (kept, 128), 1) < 64

    def exit_task(w):
        product = rows_product(rows_band, spread3, w, 0)
        for part in range(2):
            before = turned[w, part]
            for blk in range(blocks):
                value = product[kept * part : kept * part + kept, 128 * blk : 128 * blk + 128]
                lane = 256 * (blk + 1) + 128 * part
                waved[w, :, lane : lane + 128] = (value * masks4[blk]).astype(jnp.bfloat16)
                rolled = pltpu.roll(value, 64, 1)
                exit_held[slot, w, part, :, 128 * blk : 128 * blk + 128] = jnp.where(
                    low, before, rolled
                )
                before = rolled
            turned[w, part] = before

    def focused_store(w, blk, value):
        for part in range(2):
            block = value[:, 128 * part : 128 * part + 128].astype(jnp.bfloat16)
            focused_held[slot, w, part, :, 128 * blk : 128 * blk + 128] = block

    run(start_tasks(first, table, blocks * g, ring1))
    run(columns_tasks(ring1, band, spread_store(spread1)))
    run(rows_tasks(product2, rows_band, spread1))
    at = first_row[0] - 2 * HALO
    run(transmit_tasks(second, product2, ring2, last2, masks2, True, at, total_rows))
    run(columns_tasks(ring2, band, spread_store(spread2)))
    run(rows_tasks(product3, rows_band, spread2))
    at = first_row[0] - HALO
    run(transmit_tasks(third, product3, ring3, last3, masks3, False, at, total_rows))
    run(columns_tasks(ring3, band, spread_store(spread3)))
    run([functools.partial(exit_task, w) for w in range(waves)])
    run(columns_tasks(waved, wide_band, focused_store))
    for_copies(local_step, slot, lambda copy: copy.start())

    @pl.when(local_step == count - 1)
    def _():
        if count > 1:
            for_copies(local_step - 1, 1 - slot, lambda copy: copy.wait())
        for_copies(local_step, slot, lambda copy: copy.wait())
        if handed:
            for i, ref in enumerate(carried):
                given_on[i][...] = ref[:, :, :256] if i < 4 else ref[...]


def pick_kernel(halo, edges, order, potential, *refs):
    outs, held, load_sems, sems = refs[:-3], refs[-3], refs[-2], refs[-1]
    rows = potential.shape[1]
    loads = []
    for step in range(3):
        load = pltpu.make_async_copy(potential.at[order[step]], held.at[step], load_sems.at[step])
        load.start()
        loads.append(load)
    high, low = pl.ds(rows - halo, halo), pl.ds(0, halo)
    copies = []
    for step, load in enumerate(loads):
        load.wait()
        pairs = []
        for i, (left, right) in enumerate(zip(edges[:-1], edges[1:])):
            lanes = pl.ds(left, right - left)
            up, down, up2, down2 = outs[4 * i : 4 * i + 4]
            for target, far, part in ((up, up2, high), (down, down2, low)):
                if step == 2:
                    pairs.append((held.at[2, part, lanes], target.at[pl.ds(2 * rows, halo)]))
                else:
                    pairs.append((held.at[step, :, lanes], target.at[pl.ds(rows * step, rows)]))
                if step == 0:
                    pairs.append((held.at[0, part, lanes], far))
        for source, target in pairs:
            copy = pltpu.make_async_copy(source, target, sems.at[len(copies)])
            copy.start()
            copies.append(copy)
    for copy in copies:
        copy.wait()


def toeplitz(row, count, shift):
    wide = jnp.broadcast_to(row, (count, 256))
    return pltpu.roll(wide, shift % 256, 1, stride=1, stride_axis=0)


def inside_rows(first, count, total):
    at = first + lax.broadcasted_iota(jnp.int32, (count, 1), 0)
    return ((at >= 0) & (at < total)).astype(jnp.float32)


def prepare_kernel(
    waves, rows, total_rows, col_count, tilt_index, first_row, tilt_table, fresnel, ctf, mtf,
    mats, wide_rows, row_taps, col_taps, table, line,
):
    mats[:128, 256:] = jnp.zeros((128, mats.shape[1] - 256), jnp.bfloat16)
    band, wide_band = (mats.at[pl.ds(128, 512), pl.ds(256 * i, 256)] for i in range(2))
    line[...] = jnp.zeros_like(line)
    line[0:2, : fresnel.shape[1]] = fresnel[...].astype(jnp.bfloat16).astype(jnp.float32)
    line[2:4, : ctf.shape[1]] = ctf[...].astype(jnp.bfloat16).astype(jnp.float32)
    line[4:5, : mtf.shape[1]] = mtf[...]
    first = first_row[0]

    def columns(target, at, shift):
        for part in range(2):
            made = toeplitz(line[at + part : at + part + 1], 128, shift)
            for k in range(2):
                turned = jnp.transpose(made[:, 128 * k : 128 * k + 128])
                up, down = 256 * k, 256 * k + 128
                if part == 0:
                    target[up:down, :128] = turned.astype(jnp.bfloat16)
                    target[down : down + 128, 128:] = turned.astype(jnp.bfloat16)
                else:
                    target[up:down, 128:] = turned.astype(jnp.bfloat16)
                    target[down : down + 128, :128] = (-turned).astype(jnp.bfloat16)

    columns(band, 0, 65 - (fresnel.shape[1] + 1) // 2)
    columns(wide_band, 2, 65 - (ctf.shape[1] + 1) // 2)
    for part in range(2):
        made = toeplitz(line[part : part + 1], 64, HALO - (fresnel.shape[1] - 1) // 2)
        made = made[:, :128].astype(jnp.bfloat16)
        if part == 0:
            mats[:64, :128] = made
            mats[64:128, 128:256] = made
        else:
            mats[:64, 128:256] = -made
            mats[64:128, :128] = made
    for part in range(2):
        made = toeplitz(line[2 + part : 3 + part], 128, 65 - (ctf.shape[1] + 1) // 2)
        wide_rows[128 * part : 128 * part + 128] = made.astype(jnp.bfloat16)
    reach = (mtf.shape[1] - 1) // 2
    row_taps[...] = toeplitz(line[4:5], 128, 64 - reach)
    width = col_taps.shape[0]
    off = lax.broadcasted_iota(jnp.int32, (width, 256), 1) - lax.broadcasted_iota(
        jnp.int32, (width, 256), 0
    )
    made = jnp.where(jnp.abs(off) <= reach, toeplitz(line[4:5], width, -reach), 0.0)
    col_taps[...] = made[:, :width]
    count = rows + 6 * HALO
    wide = table.shape[1] - count
    at = first - 3 * HALO + lax.broadcasted_iota(jnp.int32, (count, 128), 0)
    keep = ((at >= 0) & (at < total_rows)).astype(jnp.float32)
    at = at.astype(jnp.float32) * (1.0 / total_rows)
    across = 128 * lax.broadcasted_iota(jnp.int32, (wide, 128), 0)
    across = across + lax.broadcasted_iota(jnp.int32, (wide, 128), 1)
    keep_cols = (across < col_count).astype(jnp.float32)
    across = across.astype(jnp.float32) * (1.0 / col_count)
    for w in range(waves):
        cosine, sine = cos_sin_turns(at * tilt_table[tilt_index[w], 0])
        table[2 * w, :count] = cosine * keep
        table[2 * w + 1, :count] = sine * keep
        cosine, sine = cos_sin_turns(across * tilt_table[tilt_index[w], 1])
        table[2 * w, count:] = cosine * keep_cols
        table[2 * w + 1, count:] = sine * keep_cols


def halves(value):
    high = value.astype(jnp.bfloat16)
    return high, (value - high.astype(jnp.float32)).astype(jnp.bfloat16)


def three_products(a, b, contracted):
    def product(left, right):
        return lax.dot_general(
            left, right, (((1,), (contracted,)), ((), ())), preferred_element_type=jnp.float32
        )

    return product(a[0], b[0]) + (product(a[0], b[1]) + product(a[1], b[0]))


def detector_kernel(waves, tile_wave, taps_band, row_taps, col_taps, out, padded):
    sources, rows, width = tile_wave.shape[0], tile_wave.shape[3], tile_wave.shape[4]
    total = sources * rows
    edge = jnp.zeros((64, width), jnp.float32)
    padded[:64] = edge
    padded[64 + total :] = edge
    for b in range(total // 128):
        image = None
        for w in range(waves):
            parts = []
            for part in range(2):
                window = []
                for k in range(2 * b - 1, 2 * b + 3):
                    if 0 <= k < total // 64:
                        window.append(tile_wave[k, w, part])
                    else:
                        window.append(jnp.zeros((64, width), jnp.bfloat16))
                parts.append(jnp.concatenate(window, axis=0))
            real, imag = dot(taps_band[...], parts[0]), dot(taps_band[...], parts[1])
            re = real[:128] - imag[128:]
            im = imag[:128] + real[128:]
            term = re * re + im * im
            image = term if image is None else image + term
        padded[64 + 128 * b : 192 + 128 * b] = image / waves
    taps_rows, taps_cols = halves(row_taps[...]), halves(col_taps[...])
    image_high, image_low = halves(padded[...])
    for b in range(total // 128):
        window = tuple(part[128 * b : 128 * b + 256] for part in (image_high, image_low))
        rows_done = halves(three_products(taps_rows, window, 0))
        out[:, 128 * b : 128 * b + 128] = three_products(taps_cols, rows_done, 1)


def block_windows(values):
    length = values.shape[-1]
    padded = jnp.pad(values, [(0, 0)] * (values.ndim - 1) + [(64, 64)])
    blocks = padded.reshape(values.shape[:-1] + (length // 128 + 1, 128))
    return jnp.concatenate([blocks[..., :-1, :], blocks[..., 1:, :]], axis=-1)


def narrow_tiles(focused, owner, wide_rows, row_taps, col_taps, lane_count):
    waves, _, rows, col_count = focused.shape
    width = col_count // lane_count
    slots = jnp.arange(lane_count, dtype=jnp.int32)
    placing = (owner[None, :] == slots[:, None]).astype(jnp.bfloat16)
    focused = focused.reshape(waves, 2, rows, lane_count, width)
    focused = jnp.einsum("jl,acrlk->jackr", placing, focused, preferred_element_type=jnp.float32)
    sent = focused.astype(jnp.bfloat16)
    tile_wave = lax.all_to_all(sent, "lat", split_axis=0, concat_axis=4, tiled=True)[0]
    windows = block_windows(tile_wave)
    taps_band = wide_rows.reshape(2, 128, 256)
    made = jnp.einsum("acwbi,doi->acdwbo", windows, taps_band, preferred_element_type=jnp.float32)
    real = made[:, 0, 0] - made[:, 1, 1]
    imag = made[:, 1, 0] + made[:, 0, 1]
    image = jnp.sum(real * real + imag * imag, axis=0) / waves
    image = image.reshape(width, lane_count * rows)
    blurred = jnp.einsum("wbi,oi->wbo", block_windows(image), row_taps, precision=highest)
    return jnp.dot(col_taps, blurred.reshape(width, lane_count * rows), precision=highest)


def local(potential, tilt_index, slice_order, tilt_table, fresnel_taps, ctf_taps, mtf_taps, owner):
    row_count, col_count = potential.shape[1:]
    lane_count = lax.axis_size("lat")
    total_rows = row_count * lane_count
    tile_cols = col_count // lane_count
    waves = tilt_index.shape[0]
    first_row = lax.axis_index("lat") * row_count
    steps = col_count // STEP

    def neighbour(value, offset):
        pairs = [(i, i + offset) for i in range(lane_count) if 0 <= i + offset < lane_count]
        return lax.ppermute(value, "lat", pairs)

    rows1, rows2, rows3 = (row_count + 2 * HALO * k for k in (3, 2, 1))
    anywhere = pl.BlockSpec(memory_space=pl.ANY)
    in_vmem = pl.BlockSpec(memory_space=pltpu.VMEM)
    in_smem = pl.BlockSpec(memory_space=pltpu.SMEM)
    widths = [steps // 2, steps - steps // 2]
    edges = [STEP * sum(widths[:i]) for i in range(len(widths) + 1)]
    sent_rows = (2 * row_count + HALO, 2 * row_count + HALO, HALO, HALO)
    picked = pl.pallas_call(
        functools.partial(pick_kernel, HALO, edges),
        name="pick_rows",
        out_shape=[
            jax.ShapeDtypeStruct((rows, STEP * width), potential.dtype)
            for width in widths
            for rows in sent_rows
        ],
        in_specs=[in_smem, anywhere],
        out_specs=[anywhere] * (4 * len(widths)),
        scratch_shapes=[
            pltpu.VMEM((3, row_count, col_count), potential.dtype),
            pltpu.SemaphoreType.DMA((3,)),
            pltpu.SemaphoreType.DMA((8 * len(widths),)),
        ],
        cost_estimate=pl.CostEstimate(flops=0, bytes_accessed=4 << 20, transcendentals=0),
    )(slice_order, potential)
    halos = [
        [neighbour(value, offset) for value, offset in zip(picked[4 * i : 4 * i + 4], (1, -1, 2, -2))]
        for i in range(len(widths))
    ]

    mats_shape = (128 + 512, 512)

    def made(shape, dtype):
        return jax.ShapeDtypeStruct(shape, dtype)

    mats, wide_rows, row_taps, col_taps, table = pl.pallas_call(
        functools.partial(prepare_kernel, waves, row_count, total_rows, col_count),
        name="prepare",
        out_shape=[
            made(mats_shape, jnp.bfloat16),
            made((256, 256), jnp.bfloat16),
            made((128, 256), jnp.float32),
            made((tile_cols, tile_cols), jnp.float32),
            made((2 * waves, rows1 + -(-(col_count + STEP) // 1024) * 8, 128), jnp.float32),
        ],
        in_specs=[in_smem] * 3 + [in_vmem] * 3,
        out_specs=[in_vmem] * 5,
        scratch_shapes=[pltpu.VMEM((8, 256), jnp.float32)],
        cost_estimate=pl.CostEstimate(flops=1 << 31, bytes_accessed=2 << 20, transcendentals=0),
    )(tilt_index, first_row[None], tilt_table, fresnel_taps, ctf_taps, mtf_taps[None])

    def clamp(g):
        return jnp.clip(g, 0, steps - 1)

    def fixed(*shape):
        return pl.BlockSpec(shape, lambda g, *_: (0,) * len(shape))

    placed = tile_cols == TILE
    if placed:
        focused_shape = (lane_count, waves, 2, row_count, tile_cols)
    else:
        focused_shape = (waves, 2, row_count, col_count)
    carried = [((waves, rows, 256), jnp.bfloat16) for rows in (rows1, rows2, rows3, row_count)]
    carried += [
        ((rows2, 128), jnp.float32),
        ((rows3, 128), jnp.float32),
        ((waves, 2, row_count, 128), jnp.float32),
    ]

    def ring(rows, lanes, dtype=jnp.bfloat16):
        return pltpu.VMEM((waves, rows, lanes), dtype)

    outputs = [
        made((waves, 2, row_count, col_count), jnp.float32),
        made(focused_shape, jnp.bfloat16),
    ]
    given = None
    for i, width in enumerate(widths):
        begin, last_call = edges[i] // STEP, i + 1 == len(widths)
        count = width + 1 if last_call else width

        def piece(rows, width=width):
            return pl.BlockSpec((rows, STEP), lambda g, *_: (0, jnp.minimum(g, width - 1)))

        def mine(step, begin=begin):
            return pl.BlockSpec(
                (1, row_count, STEP), lambda g, order, *_: (order[step], 0, clamp(g + begin))
            )

        up, down, up2, down2 = halos[i]
        args = [slice_order, owner, first_row[None]]
        args += [up2, up, potential, potential, potential, down, down2, table, mats]
        in_specs = [
            piece(HALO),
            piece(2 * row_count + HALO),
            mine(0),
            mine(1),
            mine(2),
            piece(2 * row_count + HALO),
            piece(HALO),
            fixed(*table.shape),
            fixed(*mats.shape),
        ]
        aliases = {}
        if given is not None:
            args += given
            in_specs += [fixed(*shape) for shape, _ in carried] + [anywhere, anywhere]
            aliases = {len(args) - 2: 0, len(args) - 1: 1}
        out_shape = list(outputs)
        out_specs = [anywhere, anywhere]
        if not last_call:
            out_shape += [made(shape, dtype) for shape, dtype in carried]
            out_specs += [fixed(*shape) for shape, _ in carried]
        results = pl.pallas_call(
            functools.partial(
                steps_kernel, waves, row_count, total_rows, col_count, begin, count, given is not None, not last_call
            ),
            name="steps",
            out_shape=out_shape,
            grid_spec=pltpu.PrefetchScalarGridSpec(
                num_scalar_prefetch=3,
                grid=(count,),
                in_specs=in_specs,
                out_specs=out_specs,
                scratch_shapes=[
                    ring(rows, 256 + 2 * STEP) for rows in (rows1, rows2, rows3, row_count)
                ]
                + [pltpu.VMEM(shape, dtype) for shape, dtype in carried[4:]]
                + [ring(2 * rows, STEP) for rows in (rows1, rows2, rows3)]
                + [ring(2 * rows, STEP, jnp.float32) for rows in (rows2, rows3)]
                + [
                    pltpu.VMEM((2, waves, 2, row_count, STEP), jnp.float32),
                    pltpu.VMEM((2, waves, 2, row_count, STEP), jnp.bfloat16),
                    pltpu.SemaphoreType.DMA((2, 2, STEP // TILE)),
                ],
            ),
            input_output_aliases=aliases,
            compiler_params=pltpu.CompilerParams(
                dimension_semantics=("arbitrary",), vmem_limit_bytes=32 * 1024 * 1024
            ),
            cost_estimate=pl.CostEstimate(
                flops=count * (1 << 31), bytes_accessed=count << 20, transcendentals=0
            ),
        )(*args)
        given = list(results[2:]) + list(results[:2])
    exit_wave, focused = results[:2]

    if not placed:
        detector = narrow_tiles(focused, owner, wide_rows, row_taps, col_taps, lane_count)
        return exit_wave, detector[None]

    tile_wave = lax.all_to_all(focused, "lat", split_axis=0, concat_axis=0, tiled=True)
    detector = pl.pallas_call(
        functools.partial(detector_kernel, waves),
        name="detector",
        out_shape=jax.ShapeDtypeStruct((tile_cols, total_rows), jnp.float32),
        in_specs=[pl.BlockSpec(memory_space=pltpu.VMEM)] * 4,
        out_specs=pl.BlockSpec(memory_space=pltpu.VMEM),
        scratch_shapes=[pltpu.VMEM((total_rows + 128, tile_cols), jnp.float32)],
        compiler_params=pltpu.CompilerParams(vmem_limit_bytes=48 * 1024 * 1024),
        cost_estimate=pl.CostEstimate(
            flops=1 << 33, bytes_accessed=4 << 20, transcendentals=0
        ),
    )(tile_wave, wide_rows, row_taps, col_taps)
    return exit_wave, detector[None]


def solution(mesh):
    placed = (
        P(None, ("lamella", "lat"), None),
        P("lamella"),
        P("lamella"),
        P(),
        P(),
        P(),
        P(),
        P("lamella"),
    )
    return jax.shard_map(
        local,
        mesh=mesh,
        in_specs=placed,
        out_specs=(P(None, None, ("lamella", "lat"), None), P(("lamella", "lat"), None, None)),
        check_vma=False,
    )
```

```python
import functools
import math

import jax
import jax.numpy as jnp
from jax import lax
from jax.experimental import pallas as pl
from jax.experimental.pallas import tpu as pltpu
from jax.sharding import PartitionSpec as P

highest = lax.Precision.HIGHEST
SIN_TURN = (
    6.2831854820251465,
    -41.34170150756836,
    81.60513305664062,
    -76.70301818847656,
    42.02592849731445,
    -14.899847030639648,
    3.2381374835968018,
)
COS_TURN = (
    1.0,
    -19.73920440673828,
    64.93911743164062,
    -85.45014190673828,
    60.16762924194336,
    -25.967599868774414,
    6.528658390045166,
)
SIN_QUARTER = (
    0.4204482138156891,
    -0.004379667341709137,
    1.3686111742572393e-05,
    -2.0339173900651986e-08,
    1.679661791598175e-11,
)
COS_QUARTER = (
    1.6817927360534668,
    -0.052555955946445465,
    0.00027371387113817036,
    -5.690624220733298e-07,
    5.977824346636851e-10,
)
HALO = 32
STEP = 512
TILE = 256


def horner(coefs, z):
    total = coefs[-1] * z + coefs[-2]
    for coef in coefs[-3::-1]:
        total = total * z + coef
    return total


def cos_sin_turns(turns):
    rest = turns - jnp.round(turns)
    z = rest * rest
    return horner(COS_TURN, z), horner(SIN_TURN, z) * rest


def cos_sin(phase):
    z = phase * phase
    quarter_sin = horner(SIN_QUARTER, z) * phase
    half_sin = quarter_sin * horner(COS_QUARTER, z)
    half_cos = math.sqrt(2.0) - quarter_sin * quarter_sin
    return 1.0 - half_sin * half_sin, half_sin * half_cos


def dot(a, b):
    return jnp.dot(a, b, preferred_element_type=jnp.float32)


def lanes_inside(block, shift, col_count):
    cols = block * 128 - shift + lax.broadcasted_iota(jnp.int32, (1, 128), 1)
    return ((cols >= 0) & (cols < col_count)).astype(jnp.float32)


def rows_of(ref, lead, start, count, lanes):
    if lead is None:
        found = ref[pl.ds(start, count), lanes]
    else:
        found = ref[lead, pl.ds(start, count), lanes]
    return found.astype(jnp.float32)


def chunks(pieces, size):
    row = 0
    for ref, lead, first, rows in pieces:
        for start in range(0, rows, size):
            yield ref, lead, first + start, row
            row += size


def columns_tasks(ring, band, store):
    waves, blocks = ring.shape[0], ring.shape[2] // 256 - 1

    def task(w, blk):
        store(w, blk, dot(ring[w, :, 256 * blk : 256 * blk + 512], band[...]))
        if blk == blocks - 1:
            ring[w, :, :256] = ring[w, :, 256 * blocks :]

    return [functools.partial(task, w, blk) for w in range(waves) for blk in range(blocks)]


def spread_store(spread):
    rows = spread.shape[1] // 2

    def store(w, blk, value):
        lanes = pl.ds(128 * blk, 128)
        spread[w, :rows, lanes] = value[:, :128].astype(jnp.bfloat16)
        spread[w, rows:, lanes] = value[:, 128:].astype(jnp.bfloat16)

    return store


def rows_product(rows_band, spread, w, block):
    half = spread.shape[1] // 2
    window = [spread[w, half * part + 64 * block : half * part + 64 * block + 128] for part in range(2)]
    return dot(rows_band[...], jnp.concatenate(window, axis=0))


def rows_tasks(product, rows_band, spread):
    waves, rows = product.shape[0], product.shape[1] // 2

    def task(w, block):
        result = rows_product(rows_band, spread, w, block)
        at = 64 * block
        product[w, at : at + 64] = result[:64]
        product[w, rows + at : rows + at + 64] = result[64:]

    return [functools.partial(task, w, block) for w in range(waves) for block in range(rows // 64)]


def run(*lists):
    for tasks in lists:
        for task in tasks:
            task()


def start_tasks(pieces, table, first_block, ring):
    waves, blocks = ring.shape[0], ring.shape[2] // 256 - 1

    def task(ref, lead, start, row):
        for blk in range(blocks):
            lanes = pl.ds(128 * blk, 128)
            cosine, sine = cos_sin(rows_of(ref, lead, start, 32, lanes))
            to = 256 * (blk + 1)
            at = pl.ds(ring.shape[1] + first_block + blk, 1)
            for w in range(waves):
                yr, yi = table[2 * w, at], table[2 * w + 1, at]
                ur, ui = cosine * yr - sine * yi, cosine * yi + sine * yr
                xr, xi = table[2 * w, pl.ds(row, 32)], table[2 * w + 1, pl.ds(row, 32)]
                ring[w, pl.ds(row, 32), to : to + 128] = (ur * xr - ui * xi).astype(jnp.bfloat16)
                ring[w, pl.ds(row, 32), to + 128 : to + 256] = (ur * xi + ui * xr).astype(
                    jnp.bfloat16
                )

    return [functools.partial(task, *chunk) for chunk in chunks(pieces, 32)]


def transmit_tasks(pieces, product, ring, last, masks, turn, first_row, total_rows):
    waves, rows = ring.shape[:2]

    def task(ref, lead, start, row):
        here = pl.ds(row, 32)
        at = first_row + row
        inside = ((at >= 0) & (at < total_rows)).astype(jnp.float32)
        before = last[here]
        low = lax.broadcasted_iota(jnp.int32, (32, 128), 1) < 64
        for blk, mask in enumerate(masks):
            found = rows_of(ref, lead, start, 32, pl.ds(128 * blk, 128))
            if turn:
                found = pltpu.roll(found, 64, 1)
            phase = jnp.where(low, before, found) if turn else before
            before = found
            cosine, sine = cos_sin(phase)
            cosine, sine = cosine * (mask * inside), sine * (mask * inside)
            to = 256 * (blk + 1)
            for w in range(waves):
                real = product[w, here, 128 * blk : 128 * blk + 128]
                imag = product[w, pl.ds(rows + row, 32), 128 * blk : 128 * blk + 128]
                ring[w, here, to : to + 128] = (real * cosine - imag * sine).astype(jnp.bfloat16)
                ring[w, here, to + 128 : to + 256] = (real * sine + imag * cosine).astype(
                    jnp.bfloat16
                )
        last[here] = before

    return [functools.partial(task, *chunk) for chunk in chunks(pieces, 32)]


def steps_kernel(
    waves, rows, total_rows, col_count, begin, count, resumed, handed, order, owner, first_row, *refs
):
    up2, up, own1, own2, own3, down, down2, table, mats = refs[:9]
    refs = refs[9:]
    given, refs = (refs[:7], refs[9:]) if resumed else (None, refs)
    exit_wave, focused = refs[:2]
    given_on, refs = (refs[2:9], refs[9:]) if handed else (None, refs[2:])
    ring1, ring2, ring3, waved, last2, last3, turned = carried = refs[:7]
    spread1, spread2, spread3, product2, product3, exit_held, focused_held, sems = refs[7:]
    local_step = pl.program_id(0)
    g = local_step + begin
    blocks = STEP // 128
    tiles = STEP // TILE
    slot = local_step % 2

    @pl.when(local_step == 0)
    def _():
        for i, ref in enumerate(carried):
            if given is None:
                if i < 4:
                    ref[:, :, :256] = jnp.zeros((waves, ref.shape[1], 256), jnp.bfloat16)
                else:
                    ref[...] = jnp.zeros_like(ref)
            elif i < 4:
                ref[:, :, :256] = given[i][...]
            else:
                ref[...] = given[i][...]

    def for_copies(step, slot, act):
        for k in range(tiles):
            tile = tiles * (step + begin) - 1 + k

            @pl.when((tile >= 0) & (tile < col_count // TILE))
            def _(tile=tile, k=k):
                lanes = pl.ds(TILE * k, TILE)
                there = pl.ds(pl.multiple_of(tile * TILE, TILE), TILE)
                act(
                    pltpu.make_async_copy(
                        exit_held.at[slot, :, :, :, lanes],
                        exit_wave.at[:, :, :, there],
                        sems.at[0, slot, k],
                    )
                )
                if len(focused.shape) == 5:
                    target = focused.at[owner[tile]]
                else:
                    target = focused.at[:, :, :, there]
                act(
                    pltpu.make_async_copy(
                        focused_held.at[slot, :, :, :, lanes], target, sems.at[1, slot, k]
                    )
                )

    @pl.when(local_step >= 2)
    def _():
        for_copies(local_step - 2, slot, lambda copy: copy.wait())

    rows_band = mats.at[pl.ds(0, 128), pl.ds(0, 256)]
    band = mats.at[pl.ds(128, 512), pl.ds(0, 256)]
    wide_band = mats.at[pl.ds(128, 512), pl.ds(256, 256)]
    first = (
        (up2, None, 0, HALO), (up, None, 0, rows), (own1, 0, 0, rows),
        (down, None, 0, rows), (down2, None, 0, HALO),
    )
    second = ((up, None, rows, rows), (own2, 0, 0, rows), (down, None, rows, rows))
    third = ((up, None, 2 * rows, HALO), (own3, 0, 0, rows), (down, None, 2 * rows, HALO))
    low = lax.broadcasted_iota(jnp.int32, (waved.shape[1], 128), 1) < 64

    def advance(now):
        def masks(shift, offset):
            return [lanes_inside(blocks * g + shift + blk, offset, col_count) for blk in range(now)]

        def part_of(ref, lanes):
            return ref.at[:, :, pl.ds(0, lanes)]

        part1, part2, part3, part4 = (
            part_of(ref, 256 * (now + 1)) for ref in (ring1, ring2, ring3, waved)
        )
        made1, made2, made3, rows2, rows3 = (
            part_of(ref, 128 * now) for ref in (spread1, spread2, spread3, product2, product3)
        )
        masks4 = masks(-1, 64)
        kept = waved.shape[1]

        def exit_task(w):
            product = rows_product(rows_band, made3, w, 0)
            for part in range(2):
                before = turned[w, part]
                for blk in range(now):
                    value = product[kept * part : kept * part + kept, 128 * blk : 128 * blk + 128]
                    lane = 256 * (blk + 1) + 128 * part
                    waved[w, :, lane : lane + 128] = (value * masks4[blk]).astype(jnp.bfloat16)
                    rolled = pltpu.roll(value, 64, 1)
                    exit_held[slot, w, part, :, 128 * blk : 128 * blk + 128] = jnp.where(
                        low, before, rolled
                    )
                    before = rolled
                turned[w, part] = before

        def focused_store(w, blk, value):
            for part in range(2):
                block = value[:, 128 * part : 128 * part + 128].astype(jnp.bfloat16)
                focused_held[slot, w, part, :, 128 * blk : 128 * blk + 128] = block

        at = first_row[0]
        run(start_tasks(first, table, blocks * g, part1))
        run(columns_tasks(part1, band, spread_store(made1)))
        run(rows_tasks(rows2, rows_band, made1))
        run(
            transmit_tasks(
                second, rows2, part2, last2, masks(0, 64), True, at - 2 * HALO, total_rows
            )
        )
        run(columns_tasks(part2, band, spread_store(made2)))
        run(rows_tasks(rows3, rows_band, made2))
        run(
            transmit_tasks(third, rows3, part3, last3, masks(-1, 0), False, at - HALO, total_rows)
        )
        run(columns_tasks(part3, band, spread_store(made3)))
        run([functools.partial(exit_task, w) for w in range(waves)])
        run(columns_tasks(part4, wide_band, focused_store))

    if handed:
        advance(blocks)
    else:
        pl.when(local_step < count - 1)(functools.partial(advance, blocks))
        pl.when(local_step == count - 1)(functools.partial(advance, TILE // 128))
    for_copies(local_step, slot, lambda copy: copy.start())

    @pl.when(local_step == count - 1)
    def _():
        if count > 1:
            for_copies(local_step - 1, 1 - slot, lambda copy: copy.wait())
        for_copies(local_step, slot, lambda copy: copy.wait())
        if handed:
            for i, ref in enumerate(carried):
                given_on[i][...] = ref[:, :, :256] if i < 4 else ref[...]


def pick_kernel(halo, edges, order, potential, *refs):
    outs, held, load_sems, sems = refs[:-3], refs[-3], refs[-2], refs[-1]
    rows = potential.shape[1]
    loads = []
    for step in range(3):
        load = pltpu.make_async_copy(potential.at[order[step]], held.at[step], load_sems.at[step])
        load.start()
        loads.append(load)
    high, low = pl.ds(rows - halo, halo), pl.ds(0, halo)
    copies = []
    for step, load in enumerate(loads):
        load.wait()
        pairs = []
        for i, (left, right) in enumerate(zip(edges[:-1], edges[1:])):
            lanes = pl.ds(left, right - left)
            up, down, up2, down2 = outs[4 * i : 4 * i + 4]
            for target, far, part in ((up, up2, high), (down, down2, low)):
                if step == 2:
                    pairs.append((held.at[2, part, lanes], target.at[pl.ds(2 * rows, halo)]))
                else:
                    pairs.append((held.at[step, :, lanes], target.at[pl.ds(rows * step, rows)]))
                if step == 0:
                    pairs.append((held.at[0, part, lanes], far))
        for source, target in pairs:
            copy = pltpu.make_async_copy(source, target, sems.at[len(copies)])
            copy.start()
            copies.append(copy)
    for copy in copies:
        copy.wait()


def toeplitz(row, count, shift):
    wide = jnp.broadcast_to(row, (count, 256))
    return pltpu.roll(wide, shift % 256, 1, stride=1, stride_axis=0)


def inside_rows(first, count, total):
    at = first + lax.broadcasted_iota(jnp.int32, (count, 1), 0)
    return ((at >= 0) & (at < total)).astype(jnp.float32)


def prepare_kernel(
    waves, rows, total_rows, col_count, tilt_index, first_row, tilt_table, fresnel, ctf, mtf,
    mats, wide_rows, row_taps, col_taps, table, line,
):
    mats[:128, 256:] = jnp.zeros((128, mats.shape[1] - 256), jnp.bfloat16)
    band, wide_band = (mats.at[pl.ds(128, 512), pl.ds(256 * i, 256)] for i in range(2))
    line[...] = jnp.zeros_like(line)
    line[0:2, : fresnel.shape[1]] = fresnel[...].astype(jnp.bfloat16).astype(jnp.float32)
    line[2:4, : ctf.shape[1]] = ctf[...].astype(jnp.bfloat16).astype(jnp.float32)
    line[4:5, : mtf.shape[1]] = mtf[...]
    first = first_row[0]

    def columns(target, at, shift):
        for part in range(2):
            made = toeplitz(line[at + part : at + part + 1], 128, shift)
            for k in range(2):
                turned = jnp.transpose(made[:, 128 * k : 128 * k + 128])
                up, down = 256 * k, 256 * k + 128
                if part == 0:
                    target[up:down, :128] = turned.astype(jnp.bfloat16)
                    target[down : down + 128, 128:] = turned.astype(jnp.bfloat16)
                else:
                    target[up:down, 128:] = turned.astype(jnp.bfloat16)
                    target[down : down + 128, :128] = (-turned).astype(jnp.bfloat16)

    columns(band, 0, 65 - (fresnel.shape[1] + 1) // 2)
    columns(wide_band, 2, 65 - (ctf.shape[1] + 1) // 2)
    for part in range(2):
        made = toeplitz(line[part : part + 1], 64, HALO - (fresnel.shape[1] - 1) // 2)
        made = made[:, :128].astype(jnp.bfloat16)
        if part == 0:
            mats[:64, :128] = made
            mats[64:128, 128:256] = made
        else:
            mats[:64, 128:256] = -made
            mats[64:128, :128] = made
    for part in range(2):
        made = toeplitz(line[2 + part : 3 + part], 128, 65 - (ctf.shape[1] + 1) // 2)
        wide_rows[128 * part : 128 * part + 128] = made.astype(jnp.bfloat16)
    reach = (mtf.shape[1] - 1) // 2
    row_taps[...] = toeplitz(line[4:5], 128, 64 - reach)
    width = col_taps.shape[0]
    off = lax.broadcasted_iota(jnp.int32, (width, 256), 1) - lax.broadcasted_iota(
        jnp.int32, (width, 256), 0
    )
    made = jnp.where(jnp.abs(off) <= reach, toeplitz(line[4:5], width, -reach), 0.0)
    col_taps[...] = made[:, :width]
    count = rows + 6 * HALO
    wide = table.shape[1] - count
    at = first - 3 * HALO + lax.broadcasted_iota(jnp.int32, (count, 128), 0)
    keep = ((at >= 0) & (at < total_rows)).astype(jnp.float32)
    at = at.astype(jnp.float32) * (1.0 / total_rows)
    across = 128 * lax.broadcasted_iota(jnp.int32, (wide, 128), 0)
    across = across + lax.broadcasted_iota(jnp.int32, (wide, 128), 1)
    keep_cols = (across < col_count).astype(jnp.float32)
    across = across.astype(jnp.float32) * (1.0 / col_count)
    for w in range(waves):
        cosine, sine = cos_sin_turns(at * tilt_table[tilt_index[w], 0])
        table[2 * w, :count] = cosine * keep
        table[2 * w + 1, :count] = sine * keep
        cosine, sine = cos_sin_turns(across * tilt_table[tilt_index[w], 1])
        table[2 * w, count:] = cosine * keep_cols
        table[2 * w + 1, count:] = sine * keep_cols


def halves(value):
    high = value.astype(jnp.bfloat16)
    return high, (value - high.astype(jnp.float32)).astype(jnp.bfloat16)


def three_products(a, b, contracted):
    def product(left, right):
        return lax.dot_general(
            left, right, (((1,), (contracted,)), ((), ())), preferred_element_type=jnp.float32
        )

    return product(a[0], b[0]) + (product(a[0], b[1]) + product(a[1], b[0]))


def detector_kernel(waves, tile_wave, taps_band, row_taps, col_taps, out, padded):
    sources, rows, width = tile_wave.shape[0], tile_wave.shape[3], tile_wave.shape[4]
    total = sources * rows
    edge = jnp.zeros((64, width), jnp.float32)
    padded[:64] = edge
    padded[64 + total :] = edge
    for b in range(total // 128):
        image = None
        for w in range(waves):
            parts = []
            for part in range(2):
                window = []
                for k in range(2 * b - 1, 2 * b + 3):
                    if 0 <= k < total // 64:
                        window.append(tile_wave[k, w, part])
                    else:
                        window.append(jnp.zeros((64, width), jnp.bfloat16))
                parts.append(jnp.concatenate(window, axis=0))
            real, imag = dot(taps_band[...], parts[0]), dot(taps_band[...], parts[1])
            re = real[:128] - imag[128:]
            im = imag[:128] + real[128:]
            term = re * re + im * im
            image = term if image is None else image + term
        padded[64 + 128 * b : 192 + 128 * b] = image / waves
    taps_rows, taps_cols = halves(row_taps[...]), halves(col_taps[...])
    image_high, image_low = halves(padded[...])
    for b in range(total // 128):
        window = tuple(part[128 * b : 128 * b + 256] for part in (image_high, image_low))
        rows_done = halves(three_products(taps_rows, window, 0))
        out[:, 128 * b : 128 * b + 128] = three_products(taps_cols, rows_done, 1)


def block_windows(values):
    length = values.shape[-1]
    padded = jnp.pad(values, [(0, 0)] * (values.ndim - 1) + [(64, 64)])
    blocks = padded.reshape(values.shape[:-1] + (length // 128 + 1, 128))
    return jnp.concatenate([blocks[..., :-1, :], blocks[..., 1:, :]], axis=-1)


def narrow_tiles(focused, owner, wide_rows, row_taps, col_taps, lane_count):
    waves, _, rows, col_count = focused.shape
    width = col_count // lane_count
    slots = jnp.arange(lane_count, dtype=jnp.int32)
    placing = (owner[None, :] == slots[:, None]).astype(jnp.bfloat16)
    focused = focused.reshape(waves, 2, rows, lane_count, width)
    focused = jnp.einsum("jl,acrlk->jackr", placing, focused, preferred_element_type=jnp.float32)
    sent = focused.astype(jnp.bfloat16)
    tile_wave = lax.all_to_all(sent, "lat", split_axis=0, concat_axis=4, tiled=True)[0]
    windows = block_windows(tile_wave)
    taps_band = wide_rows.reshape(2, 128, 256)
    made = jnp.einsum("acwbi,doi->acdwbo", windows, taps_band, preferred_element_type=jnp.float32)
    real = made[:, 0, 0] - made[:, 1, 1]
    imag = made[:, 1, 0] + made[:, 0, 1]
    image = jnp.sum(real * real + imag * imag, axis=0) / waves
    image = image.reshape(width, lane_count * rows)
    blurred = jnp.einsum("wbi,oi->wbo", block_windows(image), row_taps, precision=highest)
    return jnp.dot(col_taps, blurred.reshape(width, lane_count * rows), precision=highest)


def local(potential, tilt_index, slice_order, tilt_table, fresnel_taps, ctf_taps, mtf_taps, owner):
    row_count, col_count = potential.shape[1:]
    lane_count = lax.axis_size("lat")
    total_rows = row_count * lane_count
    tile_cols = col_count // lane_count
    waves = tilt_index.shape[0]
    first_row = lax.axis_index("lat") * row_count
    steps = col_count // STEP

    def neighbour(value, offset):
        pairs = [(i, i + offset) for i in range(lane_count) if 0 <= i + offset < lane_count]
        return lax.ppermute(value, "lat", pairs)

    rows1, rows2, rows3 = (row_count + 2 * HALO * k for k in (3, 2, 1))
    anywhere = pl.BlockSpec(memory_space=pl.ANY)
    in_vmem = pl.BlockSpec(memory_space=pltpu.VMEM)
    in_smem = pl.BlockSpec(memory_space=pltpu.SMEM)
    widths = [steps // 2, steps - steps // 2]
    edges = [STEP * sum(widths[:i]) for i in range(len(widths) + 1)]
    sent_rows = (2 * row_count + HALO, 2 * row_count + HALO, HALO, HALO)
    picked = pl.pallas_call(
        functools.partial(pick_kernel, HALO, edges),
        name="pick_rows",
        out_shape=[
            jax.ShapeDtypeStruct((rows, STEP * width), potential.dtype)
            for width in widths
            for rows in sent_rows
        ],
        in_specs=[in_smem, anywhere],
        out_specs=[anywhere] * (4 * len(widths)),
        scratch_shapes=[
            pltpu.VMEM((3, row_count, col_count), potential.dtype),
            pltpu.SemaphoreType.DMA((3,)),
            pltpu.SemaphoreType.DMA((8 * len(widths),)),
        ],
        cost_estimate=pl.CostEstimate(flops=0, bytes_accessed=4 << 20, transcendentals=0),
    )(slice_order, potential)
    halos = [
        [neighbour(value, offset) for value, offset in zip(picked[4 * i : 4 * i + 4], (1, -1, 2, -2))]
        for i in range(len(widths))
    ]

    mats_shape = (128 + 512, 512)

    def made(shape, dtype):
        return jax.ShapeDtypeStruct(shape, dtype)

    mats, wide_rows, row_taps, col_taps, table = pl.pallas_call(
        functools.partial(prepare_kernel, waves, row_count, total_rows, col_count),
        name="prepare",
        out_shape=[
            made(mats_shape, jnp.bfloat16),
            made((256, 256), jnp.bfloat16),
            made((128, 256), jnp.float32),
            made((tile_cols, tile_cols), jnp.float32),
            made((2 * waves, rows1 + -(-(col_count + STEP) // 1024) * 8, 128), jnp.float32),
        ],
        in_specs=[in_smem] * 3 + [in_vmem] * 3,
        out_specs=[in_vmem] * 5,
        scratch_shapes=[pltpu.VMEM((8, 256), jnp.float32)],
        cost_estimate=pl.CostEstimate(flops=1 << 31, bytes_accessed=2 << 20, transcendentals=0),
    )(tilt_index, first_row[None], tilt_table, fresnel_taps, ctf_taps, mtf_taps[None])

    def clamp(g):
        return jnp.clip(g, 0, steps - 1)

    def fixed(*shape):
        return pl.BlockSpec(shape, lambda g, *_: (0,) * len(shape))

    placed = tile_cols == TILE
    if placed:
        focused_shape = (lane_count, waves, 2, row_count, tile_cols)
    else:
        focused_shape = (waves, 2, row_count, col_count)
    carried = [((waves, rows, 256), jnp.bfloat16) for rows in (rows1, rows2, rows3, row_count)]
    carried += [
        ((rows2, 128), jnp.float32),
        ((rows3, 128), jnp.float32),
        ((waves, 2, row_count, 128), jnp.float32),
    ]

    def ring(rows, lanes, dtype=jnp.bfloat16):
        return pltpu.VMEM((waves, rows, lanes), dtype)

    outputs = [
        made((waves, 2, row_count, col_count), jnp.float32),
        made(focused_shape, jnp.bfloat16),
    ]
    given = None
    for i, width in enumerate(widths):
        begin, last_call = edges[i] // STEP, i + 1 == len(widths)
        count = width + 1 if last_call else width

        def piece(rows, width=width):
            return pl.BlockSpec((rows, STEP), lambda g, *_: (0, jnp.minimum(g, width - 1)))

        def mine(step, begin=begin):
            return pl.BlockSpec(
                (1, row_count, STEP), lambda g, order, *_: (order[step], 0, clamp(g + begin))
            )

        up, down, up2, down2 = halos[i]
        args = [slice_order, owner, first_row[None]]
        args += [up2, up, potential, potential, potential, down, down2, table, mats]
        in_specs = [
            piece(HALO),
            piece(2 * row_count + HALO),
            mine(0),
            mine(1),
            mine(2),
            piece(2 * row_count + HALO),
            piece(HALO),
            fixed(*table.shape),
            fixed(*mats.shape),
        ]
        aliases = {}
        if given is not None:
            args += given
            in_specs += [fixed(*shape) for shape, _ in carried] + [anywhere, anywhere]
            aliases = {len(args) - 2: 0, len(args) - 1: 1}
        out_shape = list(outputs)
        out_specs = [anywhere, anywhere]
        if not last_call:
            out_shape += [made(shape, dtype) for shape, dtype in carried]
            out_specs += [fixed(*shape) for shape, _ in carried]
        results = pl.pallas_call(
            functools.partial(
                steps_kernel, waves, row_count, total_rows, col_count, begin, count, given is not None, not last_call
            ),
            name="steps",
            out_shape=out_shape,
            grid_spec=pltpu.PrefetchScalarGridSpec(
                num_scalar_prefetch=3,
                grid=(count,),
                in_specs=in_specs,
                out_specs=out_specs,
                scratch_shapes=[
                    ring(rows, 256 + 2 * STEP) for rows in (rows1, rows2, rows3, row_count)
                ]
                + [pltpu.VMEM(shape, dtype) for shape, dtype in carried[4:]]
                + [ring(2 * rows, STEP) for rows in (rows1, rows2, rows3)]
                + [ring(2 * rows, STEP, jnp.float32) for rows in (rows2, rows3)]
                + [
                    pltpu.VMEM((2, waves, 2, row_count, STEP), jnp.float32),
                    pltpu.VMEM((2, waves, 2, row_count, STEP), jnp.bfloat16),
                    pltpu.SemaphoreType.DMA((2, 2, STEP // TILE)),
                ],
            ),
            input_output_aliases=aliases,
            compiler_params=pltpu.CompilerParams(
                dimension_semantics=("arbitrary",), vmem_limit_bytes=32 * 1024 * 1024
            ),
            cost_estimate=pl.CostEstimate(
                flops=count * (1 << 31), bytes_accessed=count << 20, transcendentals=0
            ),
        )(*args)
        given = list(results[2:]) + list(results[:2])
    exit_wave, focused = results[:2]

    if not placed:
        detector = narrow_tiles(focused, owner, wide_rows, row_taps, col_taps, lane_count)
        return exit_wave, detector[None]

    tile_wave = lax.all_to_all(focused, "lat", split_axis=0, concat_axis=0, tiled=True)
    detector = pl.pallas_call(
        functools.partial(detector_kernel, waves),
        name="detector",
        out_shape=jax.ShapeDtypeStruct((tile_cols, total_rows), jnp.float32),
        in_specs=[pl.BlockSpec(memory_space=pltpu.VMEM)] * 4,
        out_specs=pl.BlockSpec(memory_space=pltpu.VMEM),
        scratch_shapes=[pltpu.VMEM((total_rows + 128, tile_cols), jnp.float32)],
        compiler_params=pltpu.CompilerParams(vmem_limit_bytes=48 * 1024 * 1024),
        cost_estimate=pl.CostEstimate(
            flops=1 << 33, bytes_accessed=4 << 20, transcendentals=0
        ),
    )(tile_wave, wide_rows, row_taps, col_taps)
    return exit_wave, detector[None]


def solution(mesh):
    placed = (
        P(None, ("lamella", "lat"), None),
        P("lamella"),
        P("lamella"),
        P(),
        P(),
        P(),
        P(),
        P("lamella"),
    )
    return jax.shard_map(
        local,
        mesh=mesh,
        in_specs=placed,
        out_specs=(P(None, None, ("lamella", "lat"), None), P(("lamella", "lat"), None, None)),
        check_vma=False,
    )
```
